128 devices in a mesh: gx: 8 (over x, z_hi), gy: 16 (over y, z_lo, core).
Axes of the slice: x: 4, y: 4, z: 4 (z_hi: 2, z_lo: 2; z = z_hi * 2 + z_lo), core: 2. Of those that a mesh axis runs over, the one named last changes fastest.
Arguments:
- adjoint_vel: float32 [512, 2, 62, 32, 128], P(('gx', 'gy')), may hold values from -6 to 6
- velocity: bfloat16 [512, 2, 62, 32, 128], P(('gx', 'gy')), may hold values from -6 to 6
- drag_coef: float32 [512, 32, 128], P(('gx', 'gy')), may hold values from 0.3 to 3
- level_count: int32 [512, 32, 128], P(('gx', 'gy')), may hold values from 1 to 62
- block_ids: int32 [512], P(('gx', 'gy')), may hold values from 0 to 256, as said below
- bathymetry: float32 [512, 2048], P('gy', 'gx'), may hold values from 0.25 to 1
- land_mask: int32 [512, 2048], P('gy', 'gx'), may hold values 0 or 1
Outputs:
- corrected_adjoint: float32 [512, 2, 62, 32, 128], P(('gx', 'gy'))
- drag_gradient: float32 [512, 32, 128], P(('gx', 'gy'))
- surface_height: float32 [512, 2048], P('gy', 'gx')
- bathy_sensitivity: float32 [512, 2048], P('gy', 'gx')
The draws below stay inside these ranges and needn't reach their ends.
Inputs may be any that keep to these rules, and one draw needn't show every extreme that they name: `block_ids`: each device's 4 entries name the blocks it holds, then 256 in unused slots; each block number below 256 appears exactly once over all devices; each device holds 1 to 4 blocks, and some device holds 4.
All inputs are finite; a program needn't handle non-finite values. No bound on the sum of `land_mask` on one device may be relied on, other than what follows from the above.
Results may differ from the reference program's by a relative error of at most 0.0003.
Values sent between devices are 32-bit elements; how exact they have to be, the bound alone decides.
A program may use at most 128 MiB of HBM per device.

```python
import math
import jax
import jax.numpy as jnp
from jax import lax

LEV = 62
BY = 32
BX = 128
SLOTS = 4
STEPS = 32
NBLK = 256
NY = 512
NX = 2048
N_GX = 8
N_GY = 16
DEVICES = 128


def draw_block_ids(key, part):
    device_total = NBLK // 2
    first_key, second_key = jax.random.split(jax.random.fold_in(key, 7))
    pattern = jnp.array([4, 1, 1, 2], jnp.int32)
    ranking = jax.random.permutation(first_key, device_total).astype(jnp.int32)
    counts = pattern[ranking % 4]
    starts = jnp.cumsum(counts) - counts
    ordering = jax.random.permutation(second_key, NBLK).astype(jnp.int32)
    slot_index = jnp.arange(SLOTS, dtype=jnp.int32)
    position = jnp.minimum(starts[:, None] + slot_index[None, :], NBLK - 1)
    listed = jnp.where(slot_index[None, :] < counts[:, None], ordering[position], NBLK)
    return listed.reshape(-1).astype(jnp.int32)


def draw_adjoint_vel(key, part):
    noise_key, offset_key = jax.random.split(jax.random.fold_in(key, 11))
    slot_total = NBLK // 2 * SLOTS
    full_shape = (slot_total, 2, LEV, BY, BX)
    noise = jax.random.normal(noise_key, full_shape, jnp.float32)
    offset = jax.random.uniform(offset_key, (slot_total, 1, 1, 1, 1), jnp.float32, 0.003, 0.012)
    return jnp.clip(noise + offset, -6.0, 6.0).astype(jnp.float32)


def plant(values, stream_key, low, top_value):
    dims = values.shape
    place = [jax.random.randint(jax.random.fold_in(stream_key, axis), (), 0, dims[axis]) for axis in range(len(dims))]
    values = values.at[tuple(place)].set(low)
    longest = dims.index(max(dims))
    place[longest] = (place[longest] + 1) % dims[longest]
    return values.at[tuple(place)].set(top_value)


def shard_levels(own_key, shape, cuts, smallest, largest):
    def one(axis_at, shards_of):
        heights = jax.random.uniform(jax.random.fold_in(jax.random.fold_in(own_key, 6), axis_at), (shards_of,), jnp.float32, smallest / len(cuts), largest / len(cuts))
        return jnp.repeat(jnp.exp(heights), shape[axis_at] // shards_of).reshape((-1,) + (1,) * (len(shape) - axis_at - 1))

    factor_of = one(*cuts[0])
    for cut in cuts[1:]:
        factor_of = factor_of * one(*cut)
    return factor_of


def centred(own_key, extent, width, limit, pieces=(), held_as=jnp.bfloat16):
    values = jax.random.normal(own_key, extent, jnp.float32) * width
    if len(pieces) > 0:
        values = shard_levels(own_key, extent, pieces, -0.22, 0.18) * values
    return jnp.clip(values, min=-limit, max=limit).astype(held_as)


def setup_inputs(seed: int = 0) -> dict:
    seeds = jax.random.split(jax.random.key(seed), 8)
    adjoint_vel = draw_adjoint_vel(jax.random.fold_in(seeds[7], 71), 0)
    velocity = centred(seeds[1], (DEVICES * SLOTS, 2, LEV, BY, BX), 1.0, 6.0, ((0, 128),))
    drag_coef = jnp.clip(jnp.exp(math.log(3.0) - 2.3025851 * jax.random.uniform(seeds[2], (DEVICES * SLOTS, BY, BX), jnp.float32) ** shard_levels(seeds[2], (DEVICES * SLOTS, BY, BX), ((0, 128),), -0.2, 0.2)), 0.3, 3.0)
    level_count = plant(jax.random.randint(seeds[3], (DEVICES * SLOTS, BY, BX), 1, LEV + 1), jax.random.fold_in(seeds[3], 1), 1, LEV).astype(jnp.int32)
    block_ids = draw_block_ids(jax.random.fold_in(seeds[7], 71), 0)
    bathymetry = jnp.clip(jnp.exp(math.log(1.0) - 1.3862944 * jax.random.uniform(seeds[5], (NY, NX), jnp.float32) ** shard_levels(seeds[5], (NY, NX), ((0, 16), (1, 8)), -0.2, 0.2)), 0.25, 1.0)
    land_mask = plant((jax.random.randint(seeds[6], (NY, NX), 0, 8) < 7).astype(jnp.int32), jax.random.fold_in(seeds[6], 1), 0, 1)
    return {"adjoint_vel": adjoint_vel, "velocity": velocity, "drag_coef": drag_coef, "level_count": level_count, "block_ids": block_ids, "bathymetry": bathymetry, "land_mask": land_mask}


mix_rate = 0.25
mix_sweeps = 2
drag_step = 0.5
force_scale = 0.25
pressure_gain = 0.5
surface_shift = 1.0 / 64.0
speed_floor = 0.01

def chebyshev_table(total_steps):
    lowest = surface_shift
    highest = surface_shift + 8.0
    centre = 0.5 * (highest + lowest)
    radius = 0.5 * (highest - lowest)
    sigma_ratio = centre / radius
    ratio_prev = 1.0 / sigma_ratio
    table = []
    for _ in range(total_steps):
        ratio_next = 1.0 / (2.0 * sigma_ratio - ratio_prev)
        table.append((ratio_next * ratio_prev, 2.0 * ratio_next / radius))
        ratio_prev = ratio_next
    return (centre, table)

def column_block(adjoint, velocity, drag, levels):
    depth_index = lax.broadcasted_iota(jnp.int32, adjoint.shape[1:], 0)
    wetness = (depth_index < levels[None]).astype(jnp.float32)
    forcing = force_scale * lax.optimization_barrier(jnp.sum(wetness[None] * adjoint, axis=(0, 1)))
    column_field = adjoint * wetness[None]
    wet_below = wetness[None, 1:]
    for _ in range(mix_sweeps):
        level_flux = mix_rate * (column_field[:, 1:] - column_field[:, :-1]) * wet_below
        zeros_row = jnp.zeros_like(column_field[:, :1])
        column_field = column_field + jnp.concatenate([level_flux, zeros_row], axis=1) - jnp.concatenate([zeros_row, level_flux], axis=1)
    bottom = (depth_index == levels[None] - 1).astype(jnp.float32)
    flow_all = velocity.astype(jnp.float32)
    flow_bottom = lax.optimization_barrier(jnp.sum(bottom[None] * flow_all, axis=1))
    field_bottom = lax.optimization_barrier(jnp.sum(bottom[None] * column_field, axis=1))
    bottom_speed = jnp.sqrt(flow_bottom[0] * flow_bottom[0] + flow_bottom[1] * flow_bottom[1] + speed_floor)
    along_flow = flow_bottom[0] * field_bottom[0] + flow_bottom[1] * field_bottom[1]
    drag_pull = drag[None] * (bottom_speed[None] * field_bottom + flow_bottom * (along_flow / bottom_speed)[None])
    mixed_field = column_field - drag_step * bottom[None] * drag_pull[:, None]
    drag_grad = -drag_step * bottom_speed * along_flow
    return (mixed_field, drag_grad, forcing, wetness)

def face_weights(scaled):
    east = jnp.sqrt(scaled[:, :-1] * scaled[:, 1:])
    north = jnp.sqrt(scaled[:-1, :] * scaled[1:, :])
    return (east, north)

def operate(values, east, north):
    east_flux = east * (values[:, :-1] - values[:, 1:])
    north_flux = north * (values[:-1, :] - values[1:, :])
    result = surface_shift * values
    result = result + jnp.pad(east_flux, ((0, 0), (0, 1))) - jnp.pad(east_flux, ((0, 0), (1, 0)))
    result = result + jnp.pad(north_flux, ((0, 1), (0, 0))) - jnp.pad(north_flux, ((1, 0), (0, 0)))
    return result

def surface_terms(height, scaled):
    east, north = face_weights(scaled)
    east_step = height[:, 1:] - height[:, :-1]
    north_step = height[1:, :] - height[:-1, :]
    east_energy = east * east_step * east_step
    north_energy = north * north_step * north_step
    total = east_energy[1:-1, 1:] + east_energy[1:-1, :-1] + north_energy[1:, 1:-1] + north_energy[:-1, 1:-1]
    sensitivity = 0.25 * total / jnp.maximum(scaled[1:-1, 1:-1], 0.25)
    return (height[1:-1, 1:-1], east_step[1:-1, 1:], north_step[1:, 1:-1], sensitivity)

def to_grid(blocks):
    shaped = blocks.reshape(N_GX, N_GY, 2, BY, BX)
    return shaped.transpose(1, 3, 0, 2, 4).reshape(NY, NX)

def from_grid(planes):
    shaped = planes.reshape(2, N_GY, BY, N_GX, 2, BX)
    return shaped.transpose(3, 1, 4, 0, 2, 5).reshape(NBLK, 2, BY, BX)

def reference(adjoint_vel, velocity, drag_coef, level_count, block_ids, bathymetry, land_mask):

    def first_pass(inputs):
        mixed_field, drag_grad, forcing, wetness = column_block(inputs[0], inputs[1], inputs[2], inputs[3])
        return (mixed_field, drag_grad, forcing)
    mixed_all, drag_all, forcing_all = lax.map(first_pass, (adjoint_vel, velocity, drag_coef, level_count))
    valid = (block_ids < NBLK).astype(jnp.float32)
    even_blocks = jnp.zeros((NBLK + 1, BY, BX), jnp.float32).at[block_ids].add(forcing_all)[:NBLK]
    wet_mask = land_mask.astype(jnp.float32)
    scaled = bathymetry * wet_mask
    source = to_grid(even_blocks) * wet_mask
    east, north = face_weights(scaled)
    centre, table = chebyshev_table(STEPS)
    height = jnp.zeros_like(source)
    residual = source
    direction = source / centre
    for carry_coef, push_coef in table:
        height = height + direction
        residual = residual - operate(direction, east, north)
        direction = carry_coef * direction + push_coef * residual
    surface, east_step, north_step, sensitivity = surface_terms(jnp.pad(height, 1), jnp.pad(scaled, 1))
    grad_blocks = from_grid(jnp.stack([east_step, north_step]))
    grad_blocks = jnp.concatenate([grad_blocks, jnp.zeros((1, 2, BY, BX), jnp.float32)], axis=0)
    slot_grads = grad_blocks[block_ids]

    def second_pass(inputs):
        mixed_field, slot_grad, levels, flag = inputs
        depth_index = lax.broadcasted_iota(jnp.int32, mixed_field.shape[1:], 0)
        wetness = (depth_index < levels[None]).astype(jnp.float32)
        return flag * (mixed_field - pressure_gain * wetness[None] * slot_grad[:, None])
    corrected = lax.map(second_pass, (mixed_all, slot_grads, level_count, valid))
    return (corrected, drag_all * valid[:, None, None], surface, sensitivity)
```

```python
import jax
import jax.numpy as jnp
from jax import lax
from jax.experimental import pallas as pl
from jax.experimental.pallas import tpu as pltpu
from jax.sharding import PartitionSpec as P

MESH = pl.DeviceIdType.MESH
STEPS = 32
LEV = 62
BY = 32
BX = 128
SLOTS = 4
HEIGHT_ROWS = 40
NX_CHIPS, NY_CHIPS, NZ_CHIPS, CORES = 4, 4, 4, 2
A_SIZE = NX_CHIPS * CORES
B_SIZE = NY_CHIPS * NZ_CHIPS
AROUND = ((-1, -1), (-1, 0), (-1, 1), (0, -1), (0, 1), (1, -1), (1, 0), (1, 1))

mix_rate = 0.25
drag_step = 0.5
force_scale = 0.25
pressure_gain = 0.5
surface_shift = 1.0 / 64.0
speed_floor = 0.01


def chebyshev_table(total_steps):
    highest = surface_shift + 8.0
    centre = 0.5 * (highest + surface_shift)
    radius = 0.5 * (highest - surface_shift)
    sigma_ratio = centre / radius
    ratio_prev = 1.0 / sigma_ratio
    table = []
    for _ in range(total_steps):
        ratio_next = 1.0 / (2.0 * sigma_ratio - ratio_prev)
        table.append((ratio_next * ratio_prev, 2.0 * ratio_next / radius))
        ratio_prev = ratio_next
    return (centre, table)


def forcing_kernel(levels_ref, adjoint_ref, forcing_ref):
    for row in range(0, BY, 8):
        levels = levels_ref[0, row : row + 8, :]
        total = jnp.zeros((8, BX), jnp.float32)
        for k in range(LEV):
            pair = adjoint_ref[0, 0, k, row : row + 8, :] + adjoint_ref[0, 1, k, row : row + 8, :]
            total = total + jnp.where(levels > k, pair, 0.0)
        forcing_ref[0, row : row + 8, :] = force_scale * total


def column_forcing(level_count, adjoint_vel):
    return pl.pallas_call(
        forcing_kernel,
        grid=(SLOTS,),
        in_specs=[
            pl.BlockSpec((1, BY, BX), lambda s: (s, 0, 0)),
            pl.BlockSpec((1, 2, LEV, BY, BX), lambda s: (s, 0, 0, 0, 0)),
        ],
        out_specs=pl.BlockSpec((1, BY, BX), lambda s: (s, 0, 0)),
        out_shape=jax.ShapeDtypeStruct((SLOTS, BY, BX), jnp.float32),
        name="column_forcing",
    )(level_count, adjoint_vel)


def lane_roll(values, shift):
    return pltpu.roll(values, shift % values.shape[-1], values.ndim - 1)


def surface_kernel(
    ids_ref,
    table_ref,
    forcing_ref,
    bathymetry_ref,
    mask_ref,
    grads_ref,
    surface_ref,
    sens_ref,
    idbuf,
    forward_vec,
    back_vec,
    forward_idx,
    back_idx,
    cand,
    spread,
    gathered,
    source_own,
    scaled_own,
    packed_scaled,
    packed_source,
    vert_scaled,
    vert_source,
    side_scaled,
    side_source,
    east_w,
    north_w,
    scaled_ext,
    direction,
    residual,
    height,
    blocks,
    returned,
    slot_out,
    slot_in,
    slot_sum,
    id_send,
    id_recv,
    a_send,
    a_recv,
    b_send,
    b_recv,
    h_send,
    h_recv,
    g_send,
    g_recv,
    rb_send,
    rb_recv,
    ra_send,
    ra_recv,
    local_sem,
):
    gx = lax.axis_index("gx")
    gy = lax.axis_index("gy")
    my_x, my_zh = lax.div(gx, 2), lax.rem(gx, 2)
    my_y, my_zl, my_c = lax.div(gy, 4), lax.rem(lax.div(gy, 2), 2), lax.rem(gy, 2)
    my_z = my_zh * 2 + my_zl

    def a_peer(o, sign):
        step_x, step_c = o // 2, o % 2
        if sign < 0:
            step_x = (NX_CHIPS - step_x) % NX_CHIPS
        x = lax.rem(my_x + step_x, NX_CHIPS)
        c = lax.rem(my_c + step_c, CORES)
        return (x * 2 + my_zh, my_y * 4 + my_zl * 2 + c)

    def b_peer(p, sign):
        step_y, step_z = p // NZ_CHIPS, p % NZ_CHIPS
        if sign < 0:
            step_y = (NY_CHIPS - step_y) % NY_CHIPS
            step_z = (NZ_CHIPS - step_z) % NZ_CHIPS
        y = lax.rem(my_y + step_y, NY_CHIPS)
        z = lax.rem(my_z + step_z, NZ_CHIPS)
        return (my_x * 2 + lax.div(z, 2), y * 4 + lax.rem(z, 2) * 2 + my_c)

    def near(n):
        dx, dy = AROUND[n]
        return (lax.rem(gx + dx + 8, 8), lax.rem(gy + dy + 16, 16))

    def copy(src, dst, send, recv, to):
        return pltpu.make_async_remote_copy(
            src_ref=src, dst_ref=dst, send_sem=send, recv_sem=recv, device_id=to, device_id_type=MESH
        )

    barrier = pltpu.get_barrier_semaphore()
    for o in range(1, A_SIZE):
        pl.semaphore_signal(barrier, inc=1, device_id=a_peer(o, 1), device_id_type=MESH)
    for p in range(1, B_SIZE):
        pl.semaphore_signal(barrier, inc=1, device_id=b_peer(p, 1), device_id_type=MESH)
    for n in range(8):
        pl.semaphore_signal(barrier, inc=1, device_id=near(n), device_id_type=MESH)

    lane8 = lax.broadcasted_iota(jnp.int32, (8, BX), 1)
    lane32 = lax.broadcasted_iota(jnp.int32, (BY, BX), 1)
    row32 = lax.broadcasted_iota(jnp.int32, (BY, BX), 0)

    id_row = jnp.full((8, BX), -1, jnp.int32)
    for s in range(SLOTS):
        id_row = jnp.where(lane8 == s, ids_ref[s], id_row)
    idbuf[0] = id_row
    cand[0] = jnp.zeros((BY, BX), jnp.float32)
    cand[1 : 1 + SLOTS] = forcing_ref[...]
    blank = jnp.zeros((HEIGHT_ROWS, BX), jnp.float32)
    returned[0] = blank

    def pack(block, base):
        out = jnp.zeros((8, BX), jnp.float32)
        for q in range(4):
            part = lane_roll(block[8 * q : 8 * q + 8, :], 32 * q - base)
            out = jnp.where(lane8 // 32 == q, part, out)
        return out

    def unpack(packed, base):
        return jnp.concatenate([lane_roll(packed, base - 32 * q) for q in range(4)], axis=0)

    wet = mask_ref[...].astype(jnp.float32)
    scaled = bathymetry_ref[...] * wet
    scaled_own[0] = scaled[:, :BX]
    scaled_own[1] = scaled[:, BX:]

    pl.semaphore_wait(barrier, A_SIZE - 1 + B_SIZE - 1 + 8)

    id_copies = [None] * A_SIZE
    a_copies = [None] * A_SIZE
    for o in range(1, A_SIZE):
        id_copies[o] = copy(idbuf.at[0], idbuf.at[o], id_send.at[o], id_recv.at[o], a_peer(o, 1))
        id_copies[o].start()
    for o in range(1, A_SIZE):
        a_copies[o] = copy(
            forcing_ref, cand.at[pl.ds(1 + SLOTS * o, SLOTS)], a_send.at[o], a_recv.at[o], a_peer(o, 1)
        )
        a_copies[o].start()

    def halo_copies(own, packed, vert, side, send, recv):
        copies = []
        for n, (dx, dy) in enumerate(AROUND):
            if dx == 0:
                src, dst = own, vert.at[0 if dy < 0 else 1]
            else:
                src, dst = packed.at[0 if dx < 0 else 1], side.at[n]
            copies.append(copy(src, dst, send.at[n], recv.at[n], near(n)))
        return copies

    def extended(own, vert, side):
        bands = []
        for dy in (-1, 0, 1):
            if dy == 0:
                left, right = own[0], own[1]
                inside = jnp.float32(1.0)
            else:
                k = 0 if dy > 0 else 1
                left, right = vert[k, 0], vert[k, 1]
                inside = jnp.where(gy + dy >= 0, 1.0, 0.0) * jnp.where(gy + dy < 16, 1.0, 0.0)
            west = unpack(side[AROUND.index((1, -dy))], 32) * jnp.where(gx > 0, 1.0, 0.0)
            east = unpack(side[AROUND.index((-1, -dy))], 64) * jnp.where(gx < 7, 1.0, 0.0)
            left, right = lane_roll(left, 64), lane_roll(right, 64)
            first = jnp.where(lane32 < 32, 0.0, jnp.where(lane32 < 64, west, left))
            middle = jnp.where(lane32 < 64, left, right)
            last = jnp.where(lane32 < 64, right, jnp.where(lane32 < 96, east, 0.0))
            bands.append(jnp.concatenate([first, middle, last], axis=1) * inside)
        return jnp.concatenate(bands, axis=0)

    packed_scaled[0] = pack(scaled_own[0], 0)
    packed_scaled[1] = pack(scaled_own[1], 96)
    scaled_copies = halo_copies(scaled_own, packed_scaled, vert_scaled, side_scaled, h_send, h_recv)
    for c in scaled_copies:
        c.start()

    for o in range(1, A_SIZE):
        id_copies[o].wait()
    spot = lax.broadcasted_iota(jnp.int32, (2 * B_SIZE, BX), 0)
    spot_lane = lax.broadcasted_iota(jnp.int32, (2 * B_SIZE, BX), 1)
    spot_p = spot // 2
    spot_y = (my_y + spot_p // NZ_CHIPS) % NY_CHIPS
    spot_z = (my_z + spot_p % NZ_CHIPS) % NZ_CHIPS
    owner = (my_x * 2 + spot_z // 2) * 16 + spot_y * 4 + (spot_z % 2) * 2 + my_c
    target = owner * 2 + spot % 2
    forward = jnp.zeros((2 * B_SIZE, BX), jnp.int32)
    for o in range(A_SIZE):
        ids = jnp.broadcast_to(idbuf[o, 0:1, :], (2 * B_SIZE, BX))
        hit = ids == target
        forward = forward + jnp.where(hit, spot_lane + (1 + SLOTS * o), 0)
        back = jnp.sum(jnp.where(hit, spot + 1, 0), axis=0, keepdims=True)
        back_vec[o : o + 1, :] = back
    forward_vec[...] = jnp.broadcast_to(jnp.sum(forward, axis=1, keepdims=True), forward.shape)
    to_scalar = [
        pltpu.make_async_copy(forward_vec, forward_idx, local_sem.at[0]),
        pltpu.make_async_copy(back_vec, back_idx, local_sem.at[1]),
    ]
    for c in to_scalar:
        c.start()
    for c in to_scalar:
        c.wait()

    for c in scaled_copies:
        c.wait()
    scaled_ext[...] = extended(scaled_own, vert_scaled, side_scaled)
    all_scaled = scaled_ext[...]
    east_w[...] = jnp.sqrt(all_scaled * lane_roll(all_scaled, -1))
    north_w[...] = jnp.sqrt(all_scaled * pltpu.roll(all_scaled, all_scaled.shape[0] - 1, 0))

    for o in range(1, A_SIZE):
        a_copies[o].wait()
    b_copies = [None] * B_SIZE
    for p in range(B_SIZE):
        for h in range(2):
            spread[p, h] = cand[jnp.clip(forward_idx[2 * p + h, 0], 0, SLOTS * A_SIZE)]
        if p > 0:
            b_copies[p] = copy(spread.at[p], gathered.at[p], b_send.at[p], b_recv.at[p], b_peer(p, 1))
            b_copies[p].start()
    for p in range(1, B_SIZE):
        b_copies[p].wait()
    for h in range(2):
        total = spread[0, h]
        for p in range(1, B_SIZE):
            total = total + gathered[p, h]
        source_own[h] = total * wet[:, h * BX : (h + 1) * BX]

    packed_source[0] = pack(source_own[0], 0)
    packed_source[1] = pack(source_own[1], 96)
    source_copies = halo_copies(source_own, packed_source, vert_source, side_source, g_send, g_recv)
    for c in source_copies:
        c.start()
    for c in source_copies:
        c.wait()
    start = extended(source_own, vert_source, side_source)
    centre, _ = chebyshev_table(STEPS)
    residual[...] = start
    direction[...] = start / centre
    height[...] = jnp.zeros_like(start)
    tall = start.shape[0]

    def advance(step, carry):
        now = direction[...]
        east_flux = east_w[...] * (now - lane_roll(now, -1))
        north_flux = north_w[...] * (now - pltpu.roll(now, tall - 1, 0))
        image = surface_shift * now + east_flux - lane_roll(east_flux, 1)
        image = image + north_flux - pltpu.roll(north_flux, 1, 0)
        height[...] = height[...] + now
        left = residual[...] - image
        residual[...] = left
        direction[...] = table_ref[2 * step] * now + table_ref[2 * step + 1] * left
        return carry

    lax.fori_loop(0, STEPS, advance, 0)

    def own_blocks(values):
        a, b, c = (lane_roll(values[:, k * BX : (k + 1) * BX], 64) for k in range(3))
        low = lax.broadcasted_iota(jnp.int32, a.shape, 1) < 64
        return jnp.where(low, a, b), jnp.where(low, b, c)

    mid = height[BY : 2 * BY, :]
    east_step = lane_roll(mid, -1) - mid
    north_step = height[BY + 1 : 2 * BY + 1, :] - mid
    south_step = mid - height[BY - 1 : 2 * BY - 1, :]
    east_energy = east_w[BY : 2 * BY, :] * east_step * east_step
    total = (
        east_energy
        + lane_roll(east_energy, 1)
        + north_w[BY : 2 * BY, :] * north_step * north_step
        + north_w[BY - 1 : 2 * BY - 1, :] * south_step * south_step
    )
    sens = 0.25 * total / jnp.maximum(scaled_ext[BY : 2 * BY, :], 0.25)
    sens_ref[:, :BX], sens_ref[:, BX:] = own_blocks(sens)
    own_heights = own_blocks(mid)
    surface_ref[:, :BX], surface_ref[:, BX:] = own_heights
    next_rows = own_blocks(height[2 * BY : 2 * BY + 8, :])
    row8 = lax.broadcasted_iota(jnp.int32, (8, BX), 0)
    for h in range(2):
        tile = mid[:, (h + 1) * BX : (h + 2) * BX]
        column = jnp.sum(jnp.where(lane32 == 64, tile, 0.0), axis=1, keepdims=True)
        flat = jnp.sum(jnp.where(row32 == lane32, column, 0.0), axis=0, keepdims=True)
        edge = jnp.where(row8 == 0, next_rows[h], jnp.where(row8 == 1, flat, 0.0))
        returned[1 + h, 0:BY, :] = own_heights[h]
        returned[1 + h, BY : BY + 8, :] = edge

    rb_copies = [None] * B_SIZE
    for p in range(1, B_SIZE):
        rb_copies[p] = copy(
            returned.at[pl.ds(1, 2)],
            returned.at[pl.ds(1 + 2 * p, 2)],
            rb_send.at[p],
            rb_recv.at[p],
            b_peer(p, -1),
        )
        rb_copies[p].start()
    for p in range(1, B_SIZE):
        rb_copies[p].wait()
    ra_copies = [None] * A_SIZE
    for o in range(A_SIZE):
        for s in range(SLOTS):
            slot_out[o, s] = returned[jnp.clip(back_idx[o, s], 0, 2 * B_SIZE)]
        if o > 0:
            ra_copies[o] = copy(slot_out.at[o], slot_in.at[o], ra_send.at[o], ra_recv.at[o], a_peer(o, -1))
            ra_copies[o].start()
    for o in range(1, A_SIZE):
        ra_copies[o].wait()
    for s in range(SLOTS):
        total = slot_out[0, s]
        for o in range(1, A_SIZE):
            total = total + slot_in[o, s]
        slot_sum[s] = total
        here = slot_sum[s, 0:BY, :]
        flat = jnp.broadcast_to(slot_sum[s, BY + 1 : BY + 2, :], (BY, BX))
        column = jnp.sum(jnp.where(row32 == lane32, flat, 0.0), axis=1, keepdims=True)
        beside = jnp.where(lane32 == BX - 1, column, lane_roll(here, -1))
        grads_ref[s, 0] = beside - here
        grads_ref[s, 1] = slot_sum[s, 1 : BY + 1, :] - here


def surface_solve(block_ids, forcing, bathymetry, land_mask):
    _, table = chebyshev_table(STEPS)
    flat_table = jnp.array([v for pair in table for v in pair], jnp.float32)
    f32, i32 = jnp.float32, jnp.int32
    wide = (3 * BY, 3 * BX)
    dma = pltpu.SemaphoreType.DMA
    vmem = pl.BlockSpec(memory_space=pltpu.VMEM)
    smem = pl.BlockSpec(memory_space=pltpu.SMEM)
    return pl.pallas_call(
        surface_kernel,
        out_shape=(
            jax.ShapeDtypeStruct((SLOTS, 2, BY, BX), f32),
            jax.ShapeDtypeStruct((BY, 2 * BX), f32),
            jax.ShapeDtypeStruct((BY, 2 * BX), f32),
        ),
        in_specs=[smem, smem, vmem, vmem, vmem],
        out_specs=(vmem, vmem, vmem),
        scratch_shapes=[
            pltpu.VMEM((A_SIZE, 8, BX), i32),
            pltpu.VMEM((2 * B_SIZE, BX), i32),
            pltpu.VMEM((A_SIZE, BX), i32),
            pltpu.SMEM((2 * B_SIZE, BX), i32),
            pltpu.SMEM((A_SIZE, BX), i32),
            pltpu.VMEM((1 + SLOTS * A_SIZE, BY, BX), f32),
            pltpu.VMEM((B_SIZE, 2, BY, BX), f32),
            pltpu.VMEM((B_SIZE, 2, BY, BX), f32),
            pltpu.VMEM((2, BY, BX), f32),
            pltpu.VMEM((2, BY, BX), f32),
            pltpu.VMEM((2, 8, BX), f32),
            pltpu.VMEM((2, 8, BX), f32),
            pltpu.VMEM((2, 2, BY, BX), f32),
            pltpu.VMEM((2, 2, BY, BX), f32),
            pltpu.VMEM((8, 8, BX), f32),
            pltpu.VMEM((8, 8, BX), f32),
            pltpu.VMEM(wide, f32),
            pltpu.VMEM(wide, f32),
            pltpu.VMEM(wide, f32),
            pltpu.VMEM(wide, f32),
            pltpu.VMEM(wide, f32),
            pltpu.VMEM(wide, f32),
            pltpu.VMEM((2, BY, BX), f32),
            pltpu.VMEM((1 + 2 * B_SIZE, HEIGHT_ROWS, BX), f32),
            pltpu.VMEM((A_SIZE, SLOTS, HEIGHT_ROWS, BX), f32),
            pltpu.VMEM((A_SIZE, SLOTS, HEIGHT_ROWS, BX), f32),
            pltpu.VMEM((SLOTS, HEIGHT_ROWS, BX), f32),
        ]
        + [dma((A_SIZE,))] * 4
        + [dma((B_SIZE,))] * 2
        + [dma((8,))] * 4
        + [dma((B_SIZE,))] * 2
        + [dma((A_SIZE,))] * 2
        + [dma((2,))],
        compiler_params=pltpu.CompilerParams(collective_id=0, has_side_effects=True),
        name="surface_solve",
    )(block_ids, flat_table, forcing, bathymetry, land_mask)


COL_ROWS = 16


def column_kernel(ids_ref, levels_ref, drag_ref, grads_ref, adjoint_ref, velocity_ref, out_ref, drag_out_ref):
    slot = pl.program_id(0)
    used = jnp.where(ids_ref[slot] < 256, 1.0, 0.0)
    tile = (COL_ROWS, BX)
    levels = levels_ref[0]
    zero = jnp.zeros(tile, jnp.float32)

    def masked(c, k):
        return jnp.where(levels > k, adjoint_ref[0, c, k], 0.0)

    flow_b = [zero, zero]
    column_b = [zero, zero]
    above0 = [masked(c, 0) for c in range(2)]
    flux0 = [zero, zero]
    above1 = [None, None]
    flux1 = [zero, zero]
    rate_prev = None
    for k in range(LEV + 1):
        if k < LEV - 1:
            rate_next = jnp.where(levels > k + 1, mix_rate, 0.0)
        bottom = levels == k
        for c in range(2):
            if k < LEV:
                if k < LEV - 1:
                    below = masked(c, k + 1)
                    flux = (below - above0[c]) * rate_next
                else:
                    below, flux = None, zero
                first = above0[c] + flux - flux0[c]
                flux0[c], above0[c] = flux, below
            if k > 0:
                if k < LEV:
                    flux = (first - above1[c]) * rate_prev
                else:
                    flux = zero
                second = above1[c] + flux - flux1[c]
                flux1[c] = flux
                out_ref[0, c, k - 1] = second
                column_b[c] = jnp.where(bottom, second, column_b[c])
                flow_b[c] = jnp.where(bottom, velocity_ref[0, c, k - 1].astype(jnp.float32), flow_b[c])
            above1[c] = first
        rate_prev = rate_next
    speed = jnp.sqrt(flow_b[0] * flow_b[0] + flow_b[1] * flow_b[1] + speed_floor)
    along = flow_b[0] * column_b[0] + flow_b[1] * column_b[1]
    ratio = along / speed
    drag = drag_ref[0]
    drag_out_ref[0] = -drag_step * speed * along * used
    for c in range(2):
        pull = drag_step * (drag * (speed * column_b[c] + flow_b[c] * ratio)) * used
        press = pressure_gain * grads_ref[0, c] * used
        for k in range(LEV):
            value = out_ref[0, c, k] * used
            value = value - jnp.where(levels == k + 1, pull, 0.0)
            out_ref[0, c, k] = value - jnp.where(levels > k, press, 0.0)


def columns(block_ids, level_count, drag_coef, grads, adjoint_vel, velocity):
    flat = pl.BlockSpec((1, COL_ROWS, BX), lambda s, r: (s, r, 0))
    deep = pl.BlockSpec((1, 2, LEV, COL_ROWS, BX), lambda s, r: (s, 0, 0, r, 0))
    return pl.pallas_call(
        column_kernel,
        grid=(SLOTS, BY // COL_ROWS),
        in_specs=[
            pl.BlockSpec(memory_space=pltpu.SMEM),
            flat,
            flat,
            pl.BlockSpec((1, 2, COL_ROWS, BX), lambda s, r: (s, 0, r, 0)),
            deep,
            deep,
        ],
        out_specs=(deep, flat),
        out_shape=(
            jax.ShapeDtypeStruct((SLOTS, 2, LEV, BY, BX), jnp.float32),
            jax.ShapeDtypeStruct((SLOTS, BY, BX), jnp.float32),
        ),
        name="columns",
    )(block_ids, level_count, drag_coef, grads, adjoint_vel, velocity)


def per_device(adjoint_vel, velocity, drag_coef, level_count, block_ids, bathymetry, land_mask):
    forcing = column_forcing(level_count, adjoint_vel)
    grads, surface, sens = surface_solve(block_ids, forcing, bathymetry, land_mask)
    corrected, drag_grad = columns(block_ids, level_count, drag_coef, grads, adjoint_vel, velocity)
    return (corrected, drag_grad, surface, sens)


def solution(mesh):
    slots = P(("gx", "gy"), None, None, None, None)
    flat = P(("gx", "gy"), None, None)
    return jax.shard_map(
        per_device,
        mesh=mesh,
        in_specs=(slots, slots, flat, flat, P(("gx", "gy")), P("gy", "gx"), P("gy", "gx")),
        out_specs=(slots, flat, P("gy", "gx"), P("gy", "gx")),
        check_vma=False,
    )
```

```python
import jax
import jax.numpy as jnp
from jax import lax
from jax.experimental import pallas as pl
from jax.experimental.pallas import tpu as pltpu
from jax.sharding import PartitionSpec as P

MESH = pl.DeviceIdType.MESH
STEPS = 32
LEV = 62
BY = 32
BX = 128
SLOTS = 4
CHUNKS = 4
CH = BY // CHUNKS
NX_CHIPS, NY_CHIPS, NZ_CHIPS, CORES = 4, 4, 4, 2
A_SIZE = NX_CHIPS * CORES
B_SIZE = NY_CHIPS * NZ_CHIPS
AROUND = ((-1, -1), (-1, 0), (-1, 1), (0, -1), (0, 1), (1, -1), (1, 0), (1, 1))
UNIT = 16
UNITS = SLOTS * BY // UNIT

mix_rate = 0.25
drag_step = 0.5
force_scale = 0.25
pressure_gain = 0.5
surface_shift = 1.0 / 64.0
speed_floor = 0.01


def chebyshev_table(total_steps):
    highest = surface_shift + 8.0
    centre = 0.5 * (highest + surface_shift)
    radius = 0.5 * (highest - surface_shift)
    sigma_ratio = centre / radius
    ratio_prev = 1.0 / sigma_ratio
    table = []
    for _ in range(total_steps):
        ratio_next = 1.0 / (2.0 * sigma_ratio - ratio_prev)
        table.append((ratio_next * ratio_prev, 2.0 * ratio_next / radius))
        ratio_prev = ratio_next
    return (centre, table)


def lane_roll(values, shift):
    return pltpu.roll(values, shift % values.shape[-1], values.ndim - 1)


def mix_unit(unit, levels_ref, drag_ref, mixed_ref, velocity_ref, pull_ref, drag_out_ref):
    slot = lax.div(unit, BY // UNIT)
    rows = pl.ds(pl.multiple_of(lax.rem(unit, BY // UNIT) * UNIT, UNIT), UNIT)
    levels = levels_ref[slot, rows, :]
    zero = jnp.zeros((UNIT, BX), jnp.float32)

    def level(k, state, first_level=False):
        above0, flux0, above1, flux1, flow_b, column_b, rate = state
        if isinstance(k, int):
            under = min(k + 1, LEV - 1)
        else:
            under = jnp.minimum(k + 1, LEV - 1)
        wet_next = levels > k + 1
        rate_next = jnp.where(wet_next, mix_rate, 0.0)
        bottom = levels == k
        out = [[], [], [], [], [], []]
        for c in range(2):
            below = jnp.where(wet_next, mixed_ref[slot, c, under, rows, :], 0.0)
            down = (below - above0[c]) * rate_next
            first = above0[c] + down - flux0[c]
            if first_level:
                down1, flow, col = zero, flow_b[c], column_b[c]
            else:
                down1 = (first - above1[c]) * rate
                second = above1[c] + down1 - flux1[c]
                mixed_ref[slot, c, k - 1, rows, :] = second
                col = jnp.where(bottom, second, column_b[c])
                flow = jnp.where(bottom, velocity_ref[slot, c, k - 1, rows, :].astype(jnp.float32), flow_b[c])
            for pile, value in zip(out, (below, down, first, down1, flow, col)):
                pile.append(value)
        return (*(tuple(pile) for pile in out), rate_next)

    wet_top = levels > 0
    top = tuple(jnp.where(wet_top, mixed_ref[slot, c, 0, rows, :], 0.0) for c in range(2))
    both = (zero, zero)
    state = (top, both, both, both, both, both, zero)
    state = level(0, state, first_level=True)
    state = level(1, state)
    state = level(2, state)

    def ten(j, state):
        for i in range(10):
            state = level(j * 10 + (3 + i), state)
        return state

    state = lax.fori_loop(0, (LEV - 2) // 10, ten, state)
    flow_b, column_b = state[4], state[5]
    speed = jnp.sqrt(flow_b[0] * flow_b[0] + flow_b[1] * flow_b[1] + speed_floor)
    along = flow_b[0] * column_b[0] + flow_b[1] * column_b[1]
    ratio = along / speed
    drag = drag_ref[slot, rows, :]
    drag_out_ref[slot, rows, :] = -drag_step * speed * along
    for c in range(2):
        pull_ref[slot, c, rows, :] = drag_step * (drag * (speed * column_b[c] + flow_b[c] * ratio))


def main_kernel(
    ids_ref,
    table_ref,
    count_ref,
    drag_ref,
    bathymetry_ref,
    mask_ref,
    adjoint_hbm,
    velocity_hbm,
    mixed_ref,
    press_ref,
    pull_ref,
    drag_out_ref,
    surface_ref,
    sens_ref,
    levels_ref,
    velocity_ref,
    idbuf,
    forward_vec,
    back_vec,
    forward_idx,
    back_idx,
    cand,
    spread,
    gathered,
    source_own,
    scaled_own,
    packed_scaled,
    packed_source,
    vert_scaled,
    vert_source,
    side_scaled,
    side_source,
    east_w,
    north_w,
    scaled_ext,
    direction,
    residual,
    height,
    returned,
    edge_pairs,
    edges,
    slot_out,
    slot_in,
    edge_out,
    edge_in,
    slot_sum,
    load_sem,
    id_send,
    id_recv,
    a_send,
    a_recv,
    b_send,
    b_recv,
    h_send,
    h_recv,
    g_send,
    g_recv,
    rb_send,
    rb_recv,
    ra_send,
    ra_recv,
    local_sem,
):
    gx = lax.axis_index("gx")
    gy = lax.axis_index("gy")
    my_x, my_zh = lax.div(gx, 2), lax.rem(gx, 2)
    my_y, my_zl, my_c = lax.div(gy, 4), lax.rem(lax.div(gy, 2), 2), lax.rem(gy, 2)
    my_z = my_zh * 2 + my_zl

    def a_peer(o, sign):
        step_x, step_c = o // 2, o % 2
        if sign < 0:
            step_x = (NX_CHIPS - step_x) % NX_CHIPS
        x = lax.rem(my_x + step_x, NX_CHIPS)
        c = lax.rem(my_c + step_c, CORES)
        return (x * 2 + my_zh, my_y * 4 + my_zl * 2 + c)

    def b_peer(p, sign):
        step_y, step_z = p // NZ_CHIPS, p % NZ_CHIPS
        if sign < 0:
            step_y = (NY_CHIPS - step_y) % NY_CHIPS
            step_z = (NZ_CHIPS - step_z) % NZ_CHIPS
        y = lax.rem(my_y + step_y, NY_CHIPS)
        z = lax.rem(my_z + step_z, NZ_CHIPS)
        return (my_x * 2 + lax.div(z, 2), y * 4 + lax.rem(z, 2) * 2 + my_c)

    def near(n):
        dx, dy = AROUND[n]
        return (lax.rem(gx + dx + 8, 8), lax.rem(gy + dy + 16, 16))

    def copy(src, dst, send, recv, to):
        return pltpu.make_async_remote_copy(
            src_ref=src, dst_ref=dst, send_sem=send, recv_sem=recv, device_id=to, device_id_type=MESH
        )

    a_order = sorted(range(1, A_SIZE), key=lambda o: -min(o // 2, NX_CHIPS - o // 2))
    b_order = sorted(
        range(1, B_SIZE),
        key=lambda p: -min(p // NZ_CHIPS, NY_CHIPS - p // NZ_CHIPS) - min(p % NZ_CHIPS, NZ_CHIPS - p % NZ_CHIPS),
    )

    loads = []
    for q in range(CHUNKS):
        part = (slice(None), slice(None), slice(None), pl.ds(q * CH, CH))
        loads.append(pltpu.make_async_copy(adjoint_hbm.at[part], mixed_ref.at[part], load_sem.at[q]))
    loads.append(pltpu.make_async_copy(velocity_hbm, velocity_ref, load_sem.at[CHUNKS]))
    for c in loads:
        c.start()

    barrier = pltpu.get_barrier_semaphore()
    for o in range(1, A_SIZE):
        pl.semaphore_signal(barrier, inc=1, device_id=a_peer(o, 1), device_id_type=MESH)
    for p in range(1, B_SIZE):
        pl.semaphore_signal(barrier, inc=1, device_id=b_peer(p, 1), device_id_type=MESH)
    for n in range(8):
        pl.semaphore_signal(barrier, inc=1, device_id=near(n), device_id_type=MESH)

    lane8 = lax.broadcasted_iota(jnp.int32, (8, BX), 1)
    lane32 = lax.broadcasted_iota(jnp.int32, (BY, BX), 1)
    row8 = lax.broadcasted_iota(jnp.int32, (8, BX), 0)
    row32 = lax.broadcasted_iota(jnp.int32, (BY, BX), 0)

    id_row = jnp.full((8, BX), -1, jnp.int32)
    for s in range(SLOTS):
        id_row = jnp.where(lane8 == s, ids_ref[s], id_row)
        levels_ref[s] = count_ref[s] * jnp.where(ids_ref[s] < 256, 1, 0)
    idbuf[0] = id_row
    for q in range(CHUNKS):
        cand[q][0] = jnp.zeros((CH, BX), jnp.float32)
        returned[q][0] = jnp.zeros((CH, BX), jnp.float32)
    edges[0] = jnp.zeros((8, BX), jnp.float32)

    def pack(block, base):
        out = jnp.zeros((8, BX), jnp.float32)
        for q in range(4):
            part = lane_roll(block[8 * q : 8 * q + 8, :], 32 * q - base)
            out = jnp.where(lane8 // 32 == q, part, out)
        return out

    def unpack(packed, base):
        return jnp.concatenate([lane_roll(packed, base - 32 * q) for q in range(4)], axis=0)

    wet = mask_ref[...].astype(jnp.float32)
    scaled = bathymetry_ref[...] * wet
    scaled_own[0] = scaled[:, :BX]
    scaled_own[1] = scaled[:, BX:]
    packed_scaled[0] = pack(scaled_own[0], 0)
    packed_scaled[1] = pack(scaled_own[1], 96)

    def force(q):
        rows = slice(q * CH, (q + 1) * CH)

        def one(s, carry):
            levels = levels_ref[s, rows, :]
            totals = [jnp.zeros((CH, BX), jnp.float32)] * 4
            for k in range(LEV):
                pair = mixed_ref[s, 0, k, rows, :] + mixed_ref[s, 1, k, rows, :]
                totals[k % 4] = totals[k % 4] + jnp.where(levels > k, pair, 0.0)
            cand[q][1 + s] = force_scale * ((totals[0] + totals[1]) + (totals[2] + totals[3]))
            return carry

        lax.fori_loop(0, SLOTS, one, 0)

    loads[0].wait()
    force(0)
    pl.semaphore_wait(barrier, A_SIZE - 1 + B_SIZE - 1 + 8)

    id_copies = {}
    for o in a_order:
        id_copies[o] = copy(idbuf.at[0], idbuf.at[o], id_send.at[o], id_recv.at[o], a_peer(o, 1))
        id_copies[o].start()

    a_copies = [{} for _ in range(CHUNKS)]

    def send_a(q):
        for o in a_order:
            a_copies[q][o] = copy(
                cand[q].at[pl.ds(1, SLOTS)],
                cand[q].at[pl.ds(1 + SLOTS * o, SLOTS)],
                a_send.at[q, o],
                a_recv.at[q, o],
                a_peer(o, 1),
            )
            a_copies[q][o].start()

    send_a(0)

    def halo_copies(own, packed, vert, side, send, recv):
        copies = []
        for n, (dx, dy) in enumerate(AROUND):
            if dx == 0:
                src, dst = own, vert.at[0 if dy < 0 else 1]
            else:
                src, dst = packed.at[0 if dx < 0 else 1], side.at[n]
            copies.append(copy(src, dst, send.at[n], recv.at[n], near(n)))
        return copies

    def extended(own, vert, side):
        bands = []
        for dy in (-1, 0, 1):
            if dy == 0:
                left, right = own[0], own[1]
                inside = jnp.float32(1.0)
            else:
                k = 0 if dy > 0 else 1
                left, right = vert[k, 0], vert[k, 1]
                inside = jnp.where(gy + dy >= 0, 1.0, 0.0) * jnp.where(gy + dy < 16, 1.0, 0.0)
            west = unpack(side[AROUND.index((1, -dy))], 32) * jnp.where(gx > 0, 1.0, 0.0)
            east = unpack(side[AROUND.index((-1, -dy))], 64) * jnp.where(gx < 7, 1.0, 0.0)
            left, right = lane_roll(left, 64), lane_roll(right, 64)
            first = jnp.where(lane32 < 32, 0.0, jnp.where(lane32 < 64, west, left))
            middle = jnp.where(lane32 < 64, left, right)
            last = jnp.where(lane32 < 64, right, jnp.where(lane32 < 96, east, 0.0))
            bands.append(jnp.concatenate([first, middle, last], axis=1) * inside)
        return jnp.concatenate(bands, axis=0)

    for q in range(1, CHUNKS):
        loads[q].wait()
        force(q)
        send_a(q)

    scaled_copies = halo_copies(scaled_own, packed_scaled, vert_scaled, side_scaled, h_send, h_recv)
    for c in scaled_copies:
        c.start()

    for o in a_order:
        id_copies[o].wait()
    spot = lax.broadcasted_iota(jnp.int32, (2 * B_SIZE, BX), 0)
    spot_lane = lax.broadcasted_iota(jnp.int32, (2 * B_SIZE, BX), 1)
    spot_p = spot // 2
    spot_y = (my_y + spot_p // NZ_CHIPS) % NY_CHIPS
    spot_z = (my_z + spot_p % NZ_CHIPS) % NZ_CHIPS
    owner = (my_x * 2 + spot_z // 2) * 16 + spot_y * 4 + (spot_z % 2) * 2 + my_c
    target = owner * 2 + spot % 2
    forward = jnp.zeros((2 * B_SIZE, BX), jnp.int32)
    for o in range(A_SIZE):
        ids = jnp.broadcast_to(idbuf[o, 0:1, :], (2 * B_SIZE, BX))
        hit = ids == target
        forward = forward + jnp.where(hit, spot_lane + (1 + SLOTS * o), 0)
        back = jnp.sum(jnp.where(hit, spot + 1, 0), axis=0, keepdims=True)
        back_vec[o : o + 1, :] = back
    forward_vec[...] = jnp.broadcast_to(jnp.sum(forward, axis=1, keepdims=True), forward.shape)
    to_scalar = [
        pltpu.make_async_copy(forward_vec, forward_idx, local_sem.at[0]),
        pltpu.make_async_copy(back_vec, back_idx, local_sem.at[1]),
    ]
    for c in to_scalar:
        c.start()
    for c in to_scalar:
        c.wait()

    def picked(r):
        return jnp.clip(forward_idx[r, 0], 0, SLOTS * A_SIZE)

    def back_of(o, s):
        return jnp.clip(back_idx[o, s], 0, 2 * B_SIZE)

    def units(first, last):
        def one(unit, carry):
            mix_unit(unit, levels_ref, drag_ref, mixed_ref, velocity_ref, pull_ref, drag_out_ref)
            return carry

        lax.fori_loop(first, last, one, 0)

    loads[CHUNKS].wait()
    b_copies = [{} for _ in range(CHUNKS)]
    for q in range(CHUNKS):
        for o in a_order:
            a_copies[q][o].wait()
        for p in b_order + [0]:
            for h in range(2):
                spread[q, p, h] = cand[q][picked(2 * p + h)]
            if p > 0:
                b_copies[q][p] = copy(
                    spread.at[q, p], gathered.at[q, p], b_send.at[q, p], b_recv.at[q, p], b_peer(p, 1)
                )
                b_copies[q][p].start()

    units(0, UNITS)
    for c in scaled_copies:
        c.wait()
    scaled_ext[...] = extended(scaled_own, vert_scaled, side_scaled)
    all_scaled = scaled_ext[...]
    tall = all_scaled.shape[0]
    east_w[...] = jnp.sqrt(all_scaled * lane_roll(all_scaled, -1))
    north_w[...] = jnp.sqrt(all_scaled * pltpu.roll(all_scaled, tall - 1, 0))

    for q in range(CHUNKS):
        for p in b_order:
            b_copies[q][p].wait()
        rows = slice(q * CH, (q + 1) * CH)
        for h in range(2):
            total = spread[q, 0, h]
            for p in range(1, B_SIZE):
                total = total + gathered[q, p, h]
            source_own[h, rows, :] = total * wet[rows, h * BX : (h + 1) * BX]

    packed_source[0] = pack(source_own[0], 0)
    packed_source[1] = pack(source_own[1], 96)
    source_copies = halo_copies(source_own, packed_source, vert_source, side_source, g_send, g_recv)
    for c in source_copies:
        c.start()
    for c in source_copies:
        c.wait()
    start = extended(source_own, vert_source, side_source)
    centre, _ = chebyshev_table(STEPS)
    residual[...] = start
    direction[...] = start / centre
    core = slice(BY - 8, 2 * BY + 8)
    height[...] = jnp.zeros(height.shape, jnp.float32)

    for phase in range(4):
        band = slice(8 * phase, tall - 8 * phase)
        wide = tall - 16 * phase

        def advance(step, carry, band=band, wide=wide, phase=phase):
            now = direction[band, :]
            inner = slice(BY - 8 - 8 * phase, BY - 8 - 8 * phase + BY + 16)
            height[...] = height[...] + now[inner, :]
            east_flux = east_w[band, :] * (now - lane_roll(now, -1))
            north_flux = north_w[band, :] * (now - pltpu.roll(now, wide - 1, 0))
            image = surface_shift * now + east_flux - lane_roll(east_flux, 1)
            image = image + north_flux - pltpu.roll(north_flux, 1, 0)
            left = residual[band, :] - image
            residual[band, :] = left
            direction[band, :] = table_ref[2 * step] * now + table_ref[2 * step + 1] * left
            return carry

        lax.fori_loop(8 * phase, min(8 * phase + 8, STEPS - 1), advance, 0)
    height[...] = height[...] + direction[core, :]

    def own_blocks(values):
        a, b, c = (lane_roll(values[:, k * BX : (k + 1) * BX], 64) for k in range(3))
        low = lax.broadcasted_iota(jnp.int32, a.shape, 1) < 64
        return jnp.where(low, a, b), jnp.where(low, b, c)

    mid = height[8 : BY + 8, :]
    own_heights = own_blocks(mid)
    next_rows = own_blocks(height[BY + 8 : BY + 16, :])
    pair = jnp.zeros((8, BX), jnp.float32)
    for h in range(2):
        tile = mid[:, (h + 1) * BX : (h + 2) * BX]
        column = jnp.sum(jnp.where(lane32 == 64, tile, 0.0), axis=1, keepdims=True)
        flat = jnp.sum(jnp.where(row32 == lane32, column, 0.0), axis=0, keepdims=True)
        next_row = next_rows[h] if h == 0 else pltpu.roll(next_rows[h], 2 * h, 0)
        pair = jnp.where(row8 == 2 * h, next_row, jnp.where(row8 == 2 * h + 1, flat, pair))
        for q in range(CHUNKS):
            returned[q][1 + h] = own_heights[h][q * CH : (q + 1) * CH, :]
    edge_pairs[0] = pair

    rb_copies = [{} for _ in range(CHUNKS + 1)]
    for p in b_order:
        rb_copies[CHUNKS][p] = copy(
            edge_pairs.at[0], edge_pairs.at[p], rb_send.at[CHUNKS, p], rb_recv.at[CHUNKS, p], b_peer(p, -1)
        )
        rb_copies[CHUNKS][p].start()
    for q in range(CHUNKS):
        for p in b_order:
            rb_copies[q][p] = copy(
                returned[q].at[pl.ds(1, 2)],
                returned[q].at[pl.ds(1 + 2 * p, 2)],
                rb_send.at[q, p],
                rb_recv.at[q, p],
                b_peer(p, -1),
            )
            rb_copies[q][p].start()

    east_step = lane_roll(mid, -1) - mid
    north_step = height[9 : BY + 9, :] - mid
    south_step = mid - height[7 : BY + 7, :]
    east_energy = east_w[BY : 2 * BY, :] * east_step * east_step
    total = (
        east_energy
        + lane_roll(east_energy, 1)
        + north_w[BY : 2 * BY, :] * north_step * north_step
        + north_w[BY - 1 : 2 * BY - 1, :] * south_step * south_step
    )
    sens = 0.25 * total / jnp.maximum(scaled_ext[BY : 2 * BY, :], 0.25)
    sens_ref[:, :BX], sens_ref[:, BX:] = own_blocks(sens)
    surface_ref[:, :BX], surface_ref[:, BX:] = own_heights

    ra_copies = [{} for _ in range(CHUNKS + 1)]
    for p in b_order:
        rb_copies[CHUNKS][p].wait()
    for p in range(B_SIZE):
        both = edge_pairs[p]
        edges[1 + 2 * p] = jnp.where(row8 < 2, both, 0.0)
        edges[2 + 2 * p] = jnp.where(row8 < 2, pltpu.roll(both, 6, 0), 0.0)
    for o in a_order + [0]:
        tile = edges[back_of(o, 0)]
        for s in range(1, SLOTS):
            tile = tile + pltpu.roll(edges[back_of(o, s)], 2 * s, 0)
        edge_out[o] = tile
        if o > 0:
            ra_copies[CHUNKS][o] = copy(
                edge_out.at[o], edge_in.at[o], ra_send.at[CHUNKS, o], ra_recv.at[CHUNKS, o], a_peer(o, -1)
            )
            ra_copies[CHUNKS][o].start()
    for q in range(CHUNKS):
        for p in b_order:
            rb_copies[q][p].wait()
        for o in a_order + [0]:
            for s in range(SLOTS):
                slot_out[q, o, s] = returned[q][back_of(o, s)]
            if o > 0:
                ra_copies[q][o] = copy(
                    slot_out.at[q, o], slot_in.at[q, o], ra_send.at[q, o], ra_recv.at[q, o], a_peer(o, -1)
                )
                ra_copies[q][o].start()
    for o in a_order:
        ra_copies[CHUNKS][o].wait()
    edge = edge_out[0]
    for o in range(1, A_SIZE):
        edge = edge + edge_in[o]
    for s in range(SLOTS):
        slot_sum[s, BY : BY + 8, :] = edge if s == 0 else pltpu.roll(edge, 8 - 2 * s, 0)
    for q in range(CHUNKS):
        for o in a_order:
            ra_copies[q][o].wait()
        for s in range(SLOTS):
            total = slot_out[q, 0, s]
            for o in range(1, A_SIZE):
                total = total + slot_in[q, o, s]
            slot_sum[s, q * CH : (q + 1) * CH, :] = total
    for s in range(SLOTS):
        here = slot_sum[s, 0:BY, :]
        flat = jnp.broadcast_to(slot_sum[s, BY + 1 : BY + 2, :], (BY, BX))
        column = jnp.sum(jnp.where(row32 == lane32, flat, 0.0), axis=1, keepdims=True)
        beside = jnp.where(lane32 == BX - 1, column, lane_roll(here, -1))
        press_ref[s, 0] = pressure_gain * (beside - here)
        press_ref[s, 1] = pressure_gain * (slot_sum[s, 1 : BY + 1, :] - here)


def main_call(block_ids, level_count, drag_coef, bathymetry, land_mask, adjoint_vel, velocity):
    _, table = chebyshev_table(STEPS)
    flat_table = jnp.array([v for pair in table for v in pair], jnp.float32)
    f32, i32 = jnp.float32, jnp.int32
    wide = (3 * BY, 3 * BX)
    dma = pltpu.SemaphoreType.DMA
    vmem = pl.BlockSpec(memory_space=pltpu.VMEM)
    smem = pl.BlockSpec(memory_space=pltpu.SMEM)
    hbm = pl.BlockSpec(memory_space=pltpu.HBM)
    return pl.pallas_call(
        main_kernel,
        out_shape=(
            pltpu.VMEM((SLOTS, 2, LEV, BY, BX), f32),
            pltpu.VMEM((SLOTS, 2, BY, BX), f32),
            pltpu.VMEM((SLOTS, 2, BY, BX), f32),
            pltpu.VMEM((SLOTS, BY, BX), f32),
            pltpu.VMEM((BY, 2 * BX), f32),
            pltpu.VMEM((BY, 2 * BX), f32),
        ),
        in_specs=[smem, smem, vmem, vmem, vmem, vmem, hbm, hbm],
        out_specs=(vmem,) * 6,
        scratch_shapes=[
            pltpu.VMEM((SLOTS, BY, BX), i32),
            pltpu.VMEM((SLOTS, 2, LEV, BY, BX), jnp.bfloat16),
            pltpu.VMEM((A_SIZE, 8, BX), i32),
            pltpu.VMEM((2 * B_SIZE, BX), i32),
            pltpu.VMEM((A_SIZE, BX), i32),
            pltpu.SMEM((2 * B_SIZE, BX), i32),
            pltpu.SMEM((A_SIZE, BX), i32),
            [pltpu.VMEM((1 + SLOTS * A_SIZE, CH, BX), f32) for _ in range(CHUNKS)],
            pltpu.VMEM((CHUNKS, B_SIZE, 2, CH, BX), f32),
            pltpu.VMEM((CHUNKS, B_SIZE, 2, CH, BX), f32),
            pltpu.VMEM((2, BY, BX), f32),
            pltpu.VMEM((2, BY, BX), f32),
            pltpu.VMEM((2, 8, BX), f32),
            pltpu.VMEM((2, 8, BX), f32),
            pltpu.VMEM((2, 2, BY, BX), f32),
            pltpu.VMEM((2, 2, BY, BX), f32),
            pltpu.VMEM((8, 8, BX), f32),
            pltpu.VMEM((8, 8, BX), f32),
            pltpu.VMEM(wide, f32),
            pltpu.VMEM(wide, f32),
            pltpu.VMEM(wide, f32),
            pltpu.VMEM(wide, f32),
            pltpu.VMEM(wide, f32),
            pltpu.VMEM((BY + 16, 3 * BX), f32),
            [pltpu.VMEM((1 + 2 * B_SIZE, CH, BX), f32) for _ in range(CHUNKS)],
            pltpu.VMEM((B_SIZE, 8, BX), f32),
            pltpu.VMEM((1 + 2 * B_SIZE, 8, BX), f32),
            pltpu.VMEM((CHUNKS, A_SIZE, SLOTS, CH, BX), f32),
            pltpu.VMEM((CHUNKS, A_SIZE, SLOTS, CH, BX), f32),
            pltpu.VMEM((A_SIZE, 8, BX), f32),
            pltpu.VMEM((A_SIZE, 8, BX), f32),
            pltpu.VMEM((SLOTS, BY + 8, BX), f32),
            dma((CHUNKS + 1,)),
            dma((A_SIZE,)),
            dma((A_SIZE,)),
            dma((CHUNKS, A_SIZE)),
            dma((CHUNKS, A_SIZE)),
            dma((CHUNKS, B_SIZE)),
            dma((CHUNKS, B_SIZE)),
            dma((8,)),
            dma((8,)),
            dma((8,)),
            dma((8,)),
            dma((CHUNKS + 1, B_SIZE)),
            dma((CHUNKS + 1, B_SIZE)),
            dma((CHUNKS + 1, A_SIZE)),
            dma((CHUNKS + 1, A_SIZE)),
            dma((2,)),
        ],
        compiler_params=pltpu.CompilerParams(
            collective_id=0, has_side_effects=True, vmem_limit_bytes=50 * 2**20
        ),
        name="columns_and_surface",
    )(block_ids, flat_table, level_count, drag_coef, bathymetry, land_mask, adjoint_vel, velocity)


def final_kernel(
    count_ref, mixed_ref, press_ref, pull_ref, drag_ref, surface_ref, sens_ref,
    out_hbm, drag_out_ref, surface_out_ref, sens_out_ref, stage, sems,
):
    drag_out_ref[...] = drag_ref[...]
    surface_out_ref[...] = surface_ref[...]
    sens_out_ref[...] = sens_ref[...]
    puts = []
    for unit in range(UNITS):
        slot, rows = unit // (BY // UNIT), slice(unit % (BY // UNIT) * UNIT, unit % (BY // UNIT) * UNIT + UNIT)
        levels = count_ref[slot, rows, :]
        press = [press_ref[slot, c, rows, :] for c in range(2)]
        bed = [press[c] + pull_ref[slot, c, rows, :] for c in range(2)]
        for k in range(LEV):
            wet, bottom = levels > k, levels == k + 1
            for c in range(2):
                less = jnp.where(bottom, bed[c], jnp.where(wet, press[c], 0.0))
                stage[slot, c, k, rows, :] = mixed_ref[slot, c, k, rows, :] - less
        part = (slot, slice(None), slice(None), pl.ds(unit % (BY // UNIT) * UNIT, UNIT))
        puts.append(pltpu.make_async_copy(stage.at[part], out_hbm.at[part], sems.at[unit]))
        puts[-1].start()
    for c in puts:
        c.wait()


def final_call(level_count, mixed, press, pull, drag_grad, surface, sens):
    f32 = jnp.float32
    vmem = pl.BlockSpec(memory_space=pltpu.VMEM)
    deep = (SLOTS, 2, LEV, BY, BX)
    return pl.pallas_call(
        final_kernel,
        out_shape=(
            jax.ShapeDtypeStruct(deep, f32),
            jax.ShapeDtypeStruct(drag_grad.shape, f32),
            jax.ShapeDtypeStruct(surface.shape, f32),
            jax.ShapeDtypeStruct(sens.shape, f32),
        ),
        in_specs=[vmem] * 7,
        out_specs=(pl.BlockSpec(memory_space=pltpu.HBM), vmem, vmem, vmem),
        scratch_shapes=[pltpu.VMEM(deep, f32), pltpu.SemaphoreType.DMA((UNITS,))],
        compiler_params=pltpu.CompilerParams(vmem_limit_bytes=24 * 2**20),
        name="pressure_correction",
    )(level_count, mixed, press, pull, drag_grad, surface, sens)


def per_device(adjoint_vel, velocity, drag_coef, level_count, block_ids, bathymetry, land_mask):
    mixed, press, pull, drag_grad, surface, sens = main_call(
        block_ids, level_count, drag_coef, bathymetry, land_mask, adjoint_vel, velocity
    )
    return final_call(level_count, mixed, press, pull, drag_grad, surface, sens)


def solution(mesh):
    slots = P(("gx", "gy"), None, None, None, None)
    flat = P(("gx", "gy"), None, None)
    return jax.shard_map(
        per_device,
        mesh=mesh,
        in_specs=(slots, slots, flat, flat, P(("gx", "gy")), P("gy", "gx"), P("gy", "gx")),
        out_specs=(slots, flat, P("gy", "gx"), P("gy", "gx")),
        check_vma=False,
    )
```

```python
import jax
import jax.numpy as jnp
from jax import lax
from jax.experimental import pallas as pl
from jax.experimental.pallas import tpu as pltpu
from jax.sharding import PartitionSpec as P

MESH = pl.DeviceIdType.MESH
STEPS = 32
LEV = 62
BY = 32
BX = 128
SLOTS = 4
CHUNKS = 4
CH = BY // CHUNKS
NX_CHIPS, NY_CHIPS, NZ_CHIPS, CORES = 4, 4, 4, 2
A_SIZE = NX_CHIPS * CORES
B_SIZE = NY_CHIPS * NZ_CHIPS
AROUND = ((-1, -1), (-1, 0), (-1, 1), (0, -1), (0, 1), (1, -1), (1, 0), (1, 1))
UNIT = 16
UNITS = SLOTS * BY // UNIT

mix_rate = 0.25
drag_step = 0.5
force_scale = 0.25
pressure_gain = 0.5
surface_shift = 1.0 / 64.0
speed_floor = 0.01


def chebyshev_table(total_steps):
    highest = surface_shift + 8.0
    centre = 0.5 * (highest + surface_shift)
    radius = 0.5 * (highest - surface_shift)
    sigma_ratio = centre / radius
    ratio_prev = 1.0 / sigma_ratio
    table = []
    for _ in range(total_steps):
        ratio_next = 1.0 / (2.0 * sigma_ratio - ratio_prev)
        table.append((ratio_next * ratio_prev, 2.0 * ratio_next / radius))
        ratio_prev = ratio_next
    return (centre, table)


def lane_roll(values, shift):
    return pltpu.roll(values, shift % values.shape[-1], values.ndim - 1)


def mix_unit(unit, levels_ref, drag_ref, mixed_ref, velocity_ref, pull_ref, drag_out_ref):
    slot = lax.div(unit, BY // UNIT)
    rows = pl.ds(pl.multiple_of(lax.rem(unit, BY // UNIT) * UNIT, UNIT), UNIT)
    levels = levels_ref[slot, rows, :]
    zero = jnp.zeros((UNIT, BX), jnp.float32)

    def level(k, state, first_level=False):
        above0, flux0, above1, flux1, flow_b, column_b, rate = state
        last = k >= LEV - 1
        wet_next = levels > k + 1
        rate_next = jnp.where(wet_next, mix_rate, 0.0)
        bottom = levels == k
        out = [[], [], [], [], [], []]
        for c in range(2):
            if last:
                below = down = zero
                first = above0[c] - flux0[c]
            else:
                below = jnp.where(wet_next, mixed_ref[slot, c, k + 1, rows, :], 0.0)
                down = (below - above0[c]) * rate_next
                first = above0[c] + down - flux0[c]
            if first_level:
                down1, flow, col = zero, flow_b[c], column_b[c]
            else:
                down1 = zero if k == LEV else (first - above1[c]) * rate
                second = above1[c] + down1 - flux1[c]
                mixed_ref[slot, c, k - 1, rows, :] = second
                col = jnp.where(bottom, second, column_b[c])
                flow = jnp.where(bottom, velocity_ref[slot, c, k - 1, rows, :].astype(jnp.float32), flow_b[c])
            for pile, value in zip(out, (below, down, first, down1, flow, col)):
                pile.append(value)
        return (*(tuple(pile) for pile in out), rate_next)

    wet_top = levels > 0
    top = tuple(jnp.where(wet_top, mixed_ref[slot, c, 0, rows, :], 0.0) for c in range(2))
    both = (zero, zero)
    state = level(0, (top, both, both, both, both, both, zero), first_level=True)
    for k in range(1, LEV + 1):
        state = level(k, state)
    flow_b, column_b = state[4], state[5]
    speed = jnp.sqrt(flow_b[0] * flow_b[0] + flow_b[1] * flow_b[1] + speed_floor)
    along = flow_b[0] * column_b[0] + flow_b[1] * column_b[1]
    ratio = along / speed
    drag = drag_ref[slot, rows, :]
    drag_out_ref[slot, rows, :] = -drag_step * speed * along
    for c in range(2):
        pull_ref[slot, c, rows, :] = drag_step * (drag * (speed * column_b[c] + flow_b[c] * ratio))


def main_kernel(
    ids_ref,
    table_ref,
    count_ref,
    drag_ref,
    bathymetry_ref,
    mask_ref,
    adjoint_hbm,
    velocity_hbm,
    mixed_ref,
    press_ref,
    pull_ref,
    drag_out_ref,
    surface_ref,
    sens_ref,
    levels_ref,
    velocity_ref,
    idbuf,
    forward_vec,
    back_vec,
    forward_idx,
    back_idx,
    cand,
    spread,
    gathered,
    source_own,
    scaled_own,
    packed_scaled,
    packed_source,
    vert_scaled,
    vert_source,
    side_scaled,
    side_source,
    east_w,
    north_w,
    scaled_ext,
    direction,
    residual,
    height,
    west_w,
    south_w,
    diagonal,
    returned,
    edge_pairs,
    edges,
    slot_out,
    slot_in,
    edge_out,
    edge_in,
    slot_sum,
    load_sem,
    id_send,
    id_recv,
    a_send,
    a_recv,
    b_send,
    b_recv,
    h_send,
    h_recv,
    g_send,
    g_recv,
    rb_send,
    rb_recv,
    ra_send,
    ra_recv,
    local_sem,
):
    gx = lax.axis_index("gx")
    gy = lax.axis_index("gy")
    my_x, my_zh = lax.div(gx, 2), lax.rem(gx, 2)
    my_y, my_zl, my_c = lax.div(gy, 4), lax.rem(lax.div(gy, 2), 2), lax.rem(gy, 2)
    my_z = my_zh * 2 + my_zl

    def a_peer(o, sign):
        step_x, step_c = o // 2, o % 2
        if sign < 0:
            step_x = (NX_CHIPS - step_x) % NX_CHIPS
        x = lax.rem(my_x + step_x, NX_CHIPS)
        c = lax.rem(my_c + step_c, CORES)
        return (x * 2 + my_zh, my_y * 4 + my_zl * 2 + c)

    def b_peer(p, sign):
        step_y, step_z = p // NZ_CHIPS, p % NZ_CHIPS
        if sign < 0:
            step_y = (NY_CHIPS - step_y) % NY_CHIPS
            step_z = (NZ_CHIPS - step_z) % NZ_CHIPS
        y = lax.rem(my_y + step_y, NY_CHIPS)
        z = lax.rem(my_z + step_z, NZ_CHIPS)
        return (my_x * 2 + lax.div(z, 2), y * 4 + lax.rem(z, 2) * 2 + my_c)

    def near(n):
        dx, dy = AROUND[n]
        return (lax.rem(gx + dx + 8, 8), lax.rem(gy + dy + 16, 16))

    def copy(src, dst, send, recv, to):
        return pltpu.make_async_remote_copy(
            src_ref=src, dst_ref=dst, send_sem=send, recv_sem=recv, device_id=to, device_id_type=MESH
        )

    a_order = sorted(range(1, A_SIZE), key=lambda o: -min(o // 2, NX_CHIPS - o // 2))
    b_order = sorted(
        range(1, B_SIZE),
        key=lambda p: -min(p // NZ_CHIPS, NY_CHIPS - p // NZ_CHIPS) - min(p % NZ_CHIPS, NZ_CHIPS - p % NZ_CHIPS),
    )

    loads = []
    for q in range(CHUNKS):
        part = (slice(None), slice(None), slice(None), pl.ds(q * CH, CH))
        loads.append(pltpu.make_async_copy(adjoint_hbm.at[part], mixed_ref.at[part], load_sem.at[q]))
    loads.append(pltpu.make_async_copy(velocity_hbm, velocity_ref, load_sem.at[CHUNKS]))
    for c in loads:
        c.start()

    barrier = pltpu.get_barrier_semaphore()
    for o in range(1, A_SIZE):
        pl.semaphore_signal(barrier, inc=1, device_id=a_peer(o, 1), device_id_type=MESH)
    for p in range(1, B_SIZE):
        pl.semaphore_signal(barrier, inc=1, device_id=b_peer(p, 1), device_id_type=MESH)
    for n in range(8):
        pl.semaphore_signal(barrier, inc=1, device_id=near(n), device_id_type=MESH)

    lane8 = lax.broadcasted_iota(jnp.int32, (8, BX), 1)
    lane32 = lax.broadcasted_iota(jnp.int32, (BY, BX), 1)
    row8 = lax.broadcasted_iota(jnp.int32, (8, BX), 0)
    row32 = lax.broadcasted_iota(jnp.int32, (BY, BX), 0)

    id_row = jnp.full((8, BX), -1, jnp.int32)
    for s in range(SLOTS):
        id_row = jnp.where(lane8 == s, ids_ref[s], id_row)
        levels_ref[s] = count_ref[s] * jnp.where(ids_ref[s] < 256, 1, 0)
    idbuf[0] = id_row
    for q in range(CHUNKS):
        cand[q][0] = jnp.zeros((CH, BX), jnp.float32)
        returned[q][0] = jnp.zeros((CH, BX), jnp.float32)
    edges[0] = jnp.zeros((8, BX), jnp.float32)

    def pack(block, base):
        out = jnp.zeros((8, BX), jnp.float32)
        for q in range(4):
            part = lane_roll(block[8 * q : 8 * q + 8, :], 32 * q - base)
            out = jnp.where(lane8 // 32 == q, part, out)
        return out

    def unpack(packed, base):
        return jnp.concatenate([lane_roll(packed, base - 32 * q) for q in range(4)], axis=0)

    wet = mask_ref[...].astype(jnp.float32)
    scaled = bathymetry_ref[...] * wet
    scaled_own[0] = scaled[:, :BX]
    scaled_own[1] = scaled[:, BX:]
    packed_scaled[0] = pack(scaled_own[0], 0)
    packed_scaled[1] = pack(scaled_own[1], 96)

    def force(q):
        rows = slice(q * CH, (q + 1) * CH)

        def one(s, carry):
            levels = levels_ref[s, rows, :]
            totals = [jnp.zeros((CH, BX), jnp.float32)] * 4
            for k in range(LEV):
                pair = mixed_ref[s, 0, k, rows, :] + mixed_ref[s, 1, k, rows, :]
                totals[k % 4] = totals[k % 4] + jnp.where(levels > k, pair, 0.0)
            cand[q][1 + s] = force_scale * ((totals[0] + totals[1]) + (totals[2] + totals[3]))
            return carry

        lax.fori_loop(0, SLOTS, one, 0)

    loads[0].wait()
    force(0)
    pl.semaphore_wait(barrier, A_SIZE - 1 + B_SIZE - 1 + 8)

    id_copies = {}
    for o in a_order:
        id_copies[o] = copy(idbuf.at[0], idbuf.at[o], id_send.at[o], id_recv.at[o], a_peer(o, 1))
        id_copies[o].start()

    a_copies = [{} for _ in range(CHUNKS)]

    def send_a(q):
        for o in a_order:
            a_copies[q][o] = copy(
                cand[q].at[pl.ds(1, SLOTS)],
                cand[q].at[pl.ds(1 + SLOTS * o, SLOTS)],
                a_send.at[q, o],
                a_recv.at[q, o],
                a_peer(o, 1),
            )
            a_copies[q][o].start()

    send_a(0)

    def halo_copies(own, packed, vert, side, send, recv):
        copies = []
        for n, (dx, dy) in enumerate(AROUND):
            if dx == 0:
                src, dst = own, vert.at[0 if dy < 0 else 1]
            else:
                src, dst = packed.at[0 if dx < 0 else 1], side.at[n]
            copies.append(copy(src, dst, send.at[n], recv.at[n], near(n)))
        return copies

    def extended(own, vert, side):
        bands = []
        for dy in (-1, 0, 1):
            if dy == 0:
                left, right = own[0], own[1]
                inside = jnp.float32(1.0)
            else:
                k = 0 if dy > 0 else 1
                left, right = vert[k, 0], vert[k, 1]
                inside = jnp.where(gy + dy >= 0, 1.0, 0.0) * jnp.where(gy + dy < 16, 1.0, 0.0)
            west = unpack(side[AROUND.index((1, -dy))], 32) * jnp.where(gx > 0, 1.0, 0.0)
            east = unpack(side[AROUND.index((-1, -dy))], 64) * jnp.where(gx < 7, 1.0, 0.0)
            left, right = lane_roll(left, 64), lane_roll(right, 64)
            first = jnp.where(lane32 < 32, 0.0, jnp.where(lane32 < 64, west, left))
            middle = jnp.where(lane32 < 64, left, right)
            last = jnp.where(lane32 < 64, right, jnp.where(lane32 < 96, east, 0.0))
            bands.append(jnp.concatenate([first, middle, last], axis=1) * inside)
        return jnp.concatenate(bands, axis=0)

    def units(first, last):
        def one(unit, carry):
            mix_unit(unit, levels_ref, drag_ref, mixed_ref, velocity_ref, pull_ref, drag_out_ref)
            return carry

        lax.fori_loop(first, last, one, 0)

    for q in range(1, CHUNKS):
        loads[q].wait()
        force(q)
        send_a(q)

    scaled_copies = halo_copies(scaled_own, packed_scaled, vert_scaled, side_scaled, h_send, h_recv)
    for c in scaled_copies:
        c.start()

    loads[CHUNKS].wait()
    units(0, 2)
    for o in a_order:
        id_copies[o].wait()
    spot = lax.broadcasted_iota(jnp.int32, (2 * B_SIZE, BX), 0)
    spot_lane = lax.broadcasted_iota(jnp.int32, (2 * B_SIZE, BX), 1)
    spot_p = spot // 2
    spot_y = (my_y + spot_p // NZ_CHIPS) % NY_CHIPS
    spot_z = (my_z + spot_p % NZ_CHIPS) % NZ_CHIPS
    owner = (my_x * 2 + spot_z // 2) * 16 + spot_y * 4 + (spot_z % 2) * 2 + my_c
    target = owner * 2 + spot % 2
    forward = jnp.zeros((2 * B_SIZE, BX), jnp.int32)
    for o in range(A_SIZE):
        ids = jnp.broadcast_to(idbuf[o, 0:1, :], (2 * B_SIZE, BX))
        hit = ids == target
        forward = forward + jnp.where(hit, spot_lane + (1 + SLOTS * o), 0)
        back = jnp.sum(jnp.where(hit, spot + 1, 0), axis=0, keepdims=True)
        back_vec[o : o + 1, :] = back
    forward_vec[...] = jnp.broadcast_to(jnp.sum(forward, axis=1, keepdims=True), forward.shape)
    to_scalar = [
        pltpu.make_async_copy(forward_vec, forward_idx, local_sem.at[0]),
        pltpu.make_async_copy(back_vec, back_idx, local_sem.at[1]),
    ]
    for c in to_scalar:
        c.start()
    for c in to_scalar:
        c.wait()

    def picked(r):
        return jnp.clip(forward_idx[r, 0], 0, SLOTS * A_SIZE)

    def back_of(o, s):
        return jnp.clip(back_idx[o, s], 0, 2 * B_SIZE)

    b_copies = [{} for _ in range(CHUNKS)]
    for q in range(CHUNKS):
        for o in a_order:
            a_copies[q][o].wait()
        for p in b_order + [0]:
            for h in range(2):
                spread[q, p, h] = cand[q][picked(2 * p + h)]
            if p > 0:
                b_copies[q][p] = copy(
                    spread.at[q, p], gathered.at[q, p], b_send.at[q, p], b_recv.at[q, p], b_peer(p, 1)
                )
                b_copies[q][p].start()

    units(2, 6)
    for c in scaled_copies:
        c.wait()
    scaled_ext[...] = extended(scaled_own, vert_scaled, side_scaled)
    all_scaled = scaled_ext[...]
    tall = all_scaled.shape[0]
    east_w[...] = jnp.sqrt(all_scaled * lane_roll(all_scaled, -1))
    north_w[...] = jnp.sqrt(all_scaled * pltpu.roll(all_scaled, tall - 1, 0))
    west_w[...] = lane_roll(east_w[...], 1)
    south_w[...] = pltpu.roll(north_w[...], 1, 0)
    diagonal[...] = surface_shift + ((east_w[...] + west_w[...]) + (north_w[...] + south_w[...]))

    for q in range(CHUNKS):
        for p in b_order:
            b_copies[q][p].wait()
        rows = slice(q * CH, (q + 1) * CH)
        for h in range(2):
            total = spread[q, 0, h]
            for p in range(1, B_SIZE):
                total = total + gathered[q, p, h]
            source_own[h, rows, :] = total * wet[rows, h * BX : (h + 1) * BX]

    packed_source[0] = pack(source_own[0], 0)
    packed_source[1] = pack(source_own[1], 96)
    source_copies = halo_copies(source_own, packed_source, vert_source, side_source, g_send, g_recv)
    for c in source_copies:
        c.start()
    for c in source_copies:
        c.wait()
    start = extended(source_own, vert_source, side_source)
    centre, _ = chebyshev_table(STEPS)
    residual[...] = start
    direction[...] = start / centre
    core = slice(BY - 8, 2 * BY + 8)
    height[...] = jnp.zeros(height.shape, jnp.float32)

    def group(step, count, phase):
        band = slice(8 * phase, tall - 8 * phase)
        rows = tall - 16 * phase
        inner = slice(BY - 8 - 8 * phase, BY - 8 - 8 * phase + BY + 16)
        now, left, total = direction[band, :], residual[band, :], height[...]
        for i in range(count):
            total = total + now[inner, :]
            image = diagonal[band, :] * now
            image = image - (east_w[band, :] * lane_roll(now, -1) + west_w[band, :] * lane_roll(now, 1))
            image = image - (north_w[band, :] * pltpu.roll(now, rows - 1, 0) + south_w[band, :] * pltpu.roll(now, 1, 0))
            left = left - image
            now = table_ref[2 * (step + i)] * now + table_ref[2 * (step + i) + 1] * left
        direction[band, :], residual[band, :], height[...] = now, left, total

    for phase in range(3):
        for half in range(2):
            group(8 * phase + 4 * half, 4, phase)
    group(24, 4, 3)
    group(28, 3, 3)
    height[...] = height[...] + direction[core, :]

    def own_blocks(values):
        a, b, c = (lane_roll(values[:, k * BX : (k + 1) * BX], 64) for k in range(3))
        low = lax.broadcasted_iota(jnp.int32, a.shape, 1) < 64
        return jnp.where(low, a, b), jnp.where(low, b, c)

    mid = height[8 : BY + 8, :]
    own_heights = own_blocks(mid)
    next_rows = own_blocks(height[BY + 8 : BY + 16, :])
    pair = jnp.zeros((8, BX), jnp.float32)
    for h in range(2):
        tile = mid[:, (h + 1) * BX : (h + 2) * BX]
        column = jnp.sum(jnp.where(lane32 == 64, tile, 0.0), axis=1, keepdims=True)
        flat = jnp.sum(jnp.where(row32 == lane32, column, 0.0), axis=0, keepdims=True)
        next_row = next_rows[h] if h == 0 else pltpu.roll(next_rows[h], 2 * h, 0)
        pair = jnp.where(row8 == 2 * h, next_row, jnp.where(row8 == 2 * h + 1, flat, pair))
        for q in range(CHUNKS):
            returned[q][1 + h] = own_heights[h][q * CH : (q + 1) * CH, :]
    edge_pairs[0] = pair

    rb_copies = [{} for _ in range(CHUNKS + 1)]
    for p in b_order:
        rb_copies[CHUNKS][p] = copy(
            edge_pairs.at[0], edge_pairs.at[p], rb_send.at[CHUNKS, p], rb_recv.at[CHUNKS, p], b_peer(p, -1)
        )
        rb_copies[CHUNKS][p].start()
    for q in range(CHUNKS):
        for p in b_order:
            rb_copies[q][p] = copy(
                returned[q].at[pl.ds(1, 2)],
                returned[q].at[pl.ds(1 + 2 * p, 2)],
                rb_send.at[q, p],
                rb_recv.at[q, p],
                b_peer(p, -1),
            )
            rb_copies[q][p].start()

    east_step = lane_roll(mid, -1) - mid
    north_step = height[9 : BY + 9, :] - mid
    south_step = mid - height[7 : BY + 7, :]
    east_energy = east_w[BY : 2 * BY, :] * east_step * east_step
    total = (
        east_energy
        + lane_roll(east_energy, 1)
        + north_w[BY : 2 * BY, :] * north_step * north_step
        + north_w[BY - 1 : 2 * BY - 1, :] * south_step * south_step
    )
    sens = 0.25 * total / jnp.maximum(scaled_ext[BY : 2 * BY, :], 0.25)
    sens_ref[:, :BX], sens_ref[:, BX:] = own_blocks(sens)
    surface_ref[:, :BX], surface_ref[:, BX:] = own_heights

    ra_copies = [{} for _ in range(CHUNKS + 1)]
    units(6, 8)
    for p in b_order:
        rb_copies[CHUNKS][p].wait()
    for p in range(B_SIZE):
        both = edge_pairs[p]
        edges[1 + 2 * p] = jnp.where(row8 < 2, both, 0.0)
        edges[2 + 2 * p] = jnp.where(row8 < 2, pltpu.roll(both, 6, 0), 0.0)
    for o in a_order + [0]:
        tile = edges[back_of(o, 0)]
        for s in range(1, SLOTS):
            tile = tile + pltpu.roll(edges[back_of(o, s)], 2 * s, 0)
        edge_out[o] = tile
        if o > 0:
            ra_copies[CHUNKS][o] = copy(
                edge_out.at[o], edge_in.at[o], ra_send.at[CHUNKS, o], ra_recv.at[CHUNKS, o], a_peer(o, -1)
            )
            ra_copies[CHUNKS][o].start()
    for q in range(CHUNKS):
        for p in b_order:
            rb_copies[q][p].wait()
        for o in a_order + [0]:
            for s in range(SLOTS):
                slot_out[q, o, s] = returned[q][back_of(o, s)]
            if o > 0:
                ra_copies[q][o] = copy(
                    slot_out.at[q, o], slot_in.at[q, o], ra_send.at[q, o], ra_recv.at[q, o], a_peer(o, -1)
                )
                ra_copies[q][o].start()
    for o in a_order:
        ra_copies[CHUNKS][o].wait()
    edge = edge_out[0]
    for o in range(1, A_SIZE):
        edge = edge + edge_in[o]
    for s in range(SLOTS):
        slot_sum[s, BY : BY + 8, :] = edge if s == 0 else pltpu.roll(edge, 8 - 2 * s, 0)
    for q in range(CHUNKS):
        for o in a_order:
            ra_copies[q][o].wait()
        for s in range(SLOTS):
            total = slot_out[q, 0, s]
            for o in range(1, A_SIZE):
                total = total + slot_in[q, o, s]
            slot_sum[s, q * CH : (q + 1) * CH, :] = total
    for s in range(SLOTS):
        here = slot_sum[s, 0:BY, :]
        flat = jnp.broadcast_to(slot_sum[s, BY + 1 : BY + 2, :], (BY, BX))
        column = jnp.sum(jnp.where(row32 == lane32, flat, 0.0), axis=1, keepdims=True)
        beside = jnp.where(lane32 == BX - 1, column, lane_roll(here, -1))
        press_ref[s, 0] = pressure_gain * (beside - here)
        press_ref[s, 1] = pressure_gain * (slot_sum[s, 1 : BY + 1, :] - here)


def main_call(block_ids, level_count, drag_coef, bathymetry, land_mask, adjoint_vel, velocity):
    _, table = chebyshev_table(STEPS)
    flat_table = jnp.array([v for pair in table for v in pair], jnp.float32)
    f32, i32 = jnp.float32, jnp.int32
    wide = (3 * BY, 3 * BX)
    dma = pltpu.SemaphoreType.DMA
    vmem = pl.BlockSpec(memory_space=pltpu.VMEM)
    smem = pl.BlockSpec(memory_space=pltpu.SMEM)
    hbm = pl.BlockSpec(memory_space=pltpu.HBM)
    return pl.pallas_call(
        main_kernel,
        out_shape=(
            pltpu.VMEM((SLOTS, 2, LEV, BY, BX), f32),
            pltpu.VMEM((SLOTS, 2, BY, BX), f32),
            pltpu.VMEM((SLOTS, 2, BY, BX), f32),
            pltpu.VMEM((SLOTS, BY, BX), f32),
            pltpu.VMEM((BY, 2 * BX), f32),
            pltpu.VMEM((BY, 2 * BX), f32),
        ),
        in_specs=[smem, smem, vmem, vmem, vmem, vmem, hbm, hbm],
        out_specs=(vmem,) * 6,
        scratch_shapes=[
            pltpu.VMEM((SLOTS, BY, BX), i32),
            pltpu.VMEM((SLOTS, 2, LEV, BY, BX), jnp.bfloat16),
            pltpu.VMEM((A_SIZE, 8, BX), i32),
            pltpu.VMEM((2 * B_SIZE, BX), i32),
            pltpu.VMEM((A_SIZE, BX), i32),
            pltpu.SMEM((2 * B_SIZE, BX), i32),
            pltpu.SMEM((A_SIZE, BX), i32),
            [pltpu.VMEM((1 + SLOTS * A_SIZE, CH, BX), f32) for _ in range(CHUNKS)],
            pltpu.VMEM((CHUNKS, B_SIZE, 2, CH, BX), f32),
            pltpu.VMEM((CHUNKS, B_SIZE, 2, CH, BX), f32),
            pltpu.VMEM((2, BY, BX), f32),
            pltpu.VMEM((2, BY, BX), f32),
            pltpu.VMEM((2, 8, BX), f32),
            pltpu.VMEM((2, 8, BX), f32),
            pltpu.VMEM((2, 2, BY, BX), f32),
            pltpu.VMEM((2, 2, BY, BX), f32),
            pltpu.VMEM((8, 8, BX), f32),
            pltpu.VMEM((8, 8, BX), f32),
            pltpu.VMEM(wide, f32),
            pltpu.VMEM(wide, f32),
            pltpu.VMEM(wide, f32),
            pltpu.VMEM(wide, f32),
            pltpu.VMEM(wide, f32),
            pltpu.VMEM((BY + 16, 3 * BX), f32),
            pltpu.VMEM(wide, f32),
            pltpu.VMEM(wide, f32),
            pltpu.VMEM(wide, f32),
            [pltpu.VMEM((1 + 2 * B_SIZE, CH, BX), f32) for _ in range(CHUNKS)],
            pltpu.VMEM((B_SIZE, 8, BX), f32),
            pltpu.VMEM((1 + 2 * B_SIZE, 8, BX), f32),
            pltpu.VMEM((CHUNKS, A_SIZE, SLOTS, CH, BX), f32),
            pltpu.VMEM((CHUNKS, A_SIZE, SLOTS, CH, BX), f32),
            pltpu.VMEM((A_SIZE, 8, BX), f32),
            pltpu.VMEM((A_SIZE, 8, BX), f32),
            pltpu.VMEM((SLOTS, BY + 8, BX), f32),
            dma((CHUNKS + 1,)),
            dma((A_SIZE,)),
            dma((A_SIZE,)),
            dma((CHUNKS, A_SIZE)),
            dma((CHUNKS, A_SIZE)),
            dma((CHUNKS, B_SIZE)),
            dma((CHUNKS, B_SIZE)),
            dma((8,)),
            dma((8,)),
            dma((8,)),
            dma((8,)),
            dma((CHUNKS + 1, B_SIZE)),
            dma((CHUNKS + 1, B_SIZE)),
            dma((CHUNKS + 1, A_SIZE)),
            dma((CHUNKS + 1, A_SIZE)),
            dma((2,)),
        ],
        compiler_params=pltpu.CompilerParams(
            collective_id=0, has_side_effects=True, vmem_limit_bytes=50 * 2**20
        ),
        name="columns_and_surface",
    )(block_ids, flat_table, level_count, drag_coef, bathymetry, land_mask, adjoint_vel, velocity)


def final_kernel(
    count_ref, mixed_ref, press_ref, pull_ref, drag_ref, surface_ref, sens_ref,
    out_hbm, drag_out_ref, surface_out_ref, sens_out_ref, stage, sems,
):
    drag_out_ref[...] = drag_ref[...]
    surface_out_ref[...] = surface_ref[...]
    sens_out_ref[...] = sens_ref[...]
    puts = []
    for unit in range(UNITS):
        slot, rows = unit // (BY // UNIT), slice(unit % (BY // UNIT) * UNIT, unit % (BY // UNIT) * UNIT + UNIT)
        levels = count_ref[slot, rows, :]
        press = [press_ref[slot, c, rows, :] for c in range(2)]
        bed = [press[c] + pull_ref[slot, c, rows, :] for c in range(2)]
        for k in range(LEV):
            wet, bottom = levels > k, levels == k + 1
            for c in range(2):
                less = jnp.where(bottom, bed[c], jnp.where(wet, press[c], 0.0))
                stage[slot, c, k, rows, :] = mixed_ref[slot, c, k, rows, :] - less
        part = (slot, slice(None), slice(None), pl.ds(unit % (BY // UNIT) * UNIT, UNIT))
        puts.append(pltpu.make_async_copy(stage.at[part], out_hbm.at[part], sems.at[unit]))
        puts[-1].start()
    for c in puts:
        c.wait()


def final_call(level_count, mixed, press, pull, drag_grad, surface, sens):
    f32 = jnp.float32
    vmem = pl.BlockSpec(memory_space=pltpu.VMEM)
    deep = (SLOTS, 2, LEV, BY, BX)
    return pl.pallas_call(
        final_kernel,
        out_shape=(
            jax.ShapeDtypeStruct(deep, f32),
            jax.ShapeDtypeStruct(drag_grad.shape, f32),
            jax.ShapeDtypeStruct(surface.shape, f32),
            jax.ShapeDtypeStruct(sens.shape, f32),
        ),
        in_specs=[vmem] * 7,
        out_specs=(pl.BlockSpec(memory_space=pltpu.HBM), vmem, vmem, vmem),
        scratch_shapes=[pltpu.VMEM(deep, f32), pltpu.SemaphoreType.DMA((UNITS,))],
        compiler_params=pltpu.CompilerParams(vmem_limit_bytes=24 * 2**20),
        name="pressure_correction",
    )(level_count, mixed, press, pull, drag_grad, surface, sens)


def per_device(adjoint_vel, velocity, drag_coef, level_count, block_ids, bathymetry, land_mask):
    mixed, press, pull, drag_grad, surface, sens = main_call(
        block_ids, level_count, drag_coef, bathymetry, land_mask, adjoint_vel, velocity
    )
    return final_call(level_count, mixed, press, pull, drag_grad, surface, sens)


def solution(mesh):
    slots = P(("gx", "gy"), None, None, None, None)
    flat = P(("gx", "gy"), None, None)
    return jax.shard_map(
        per_device,
        mesh=mesh,
        in_specs=(slots, slots, flat, flat, P(("gx", "gy")), P("gy", "gx"), P("gy", "gx")),
        out_specs=(slots, flat, P("gy", "gx"), P("gy", "gx")),
        check_vma=False,
    )
```

```python
import jax
import jax.numpy as jnp
from jax import lax
from jax.experimental import pallas as pl
from jax.experimental.pallas import tpu as pltpu
from jax.sharding import PartitionSpec as P

MESH = pl.DeviceIdType.MESH
STEPS = 32
LEV = 62
BY = 32
BX = 128
SLOTS = 4
CHUNKS = 4
CH = BY // CHUNKS
NX_CHIPS, NY_CHIPS, NZ_CHIPS, CORES = 4, 4, 4, 2
A_SIZE = NX_CHIPS * CORES
B_SIZE = NY_CHIPS * NZ_CHIPS
AROUND = ((-1, -1), (-1, 0), (-1, 1), (0, -1), (0, 1), (1, -1), (1, 0), (1, 1))
SIDES = tuple(d for d in AROUND if d[0] != 0)
UNIT = 16
UNITS = SLOTS * BY // UNIT
PIECES = 2

mix_rate = 0.25
drag_step = 0.5
force_scale = 0.25
pressure_gain = 0.5
surface_shift = 1.0 / 64.0
speed_floor = 0.01


def chebyshev_table(total_steps):
    highest = surface_shift + 8.0
    centre = 0.5 * (highest + surface_shift)
    radius = 0.5 * (highest - surface_shift)
    sigma_ratio = centre / radius
    ratio_prev = 1.0 / sigma_ratio
    table = []
    for _ in range(total_steps):
        ratio_next = 1.0 / (2.0 * sigma_ratio - ratio_prev)
        table.append((ratio_next * ratio_prev, 2.0 * ratio_next / radius))
        ratio_prev = ratio_next
    return (centre, table)


def lane_roll(values, shift):
    return pltpu.roll(values, shift % values.shape[-1], values.ndim - 1)


def mix_unit(unit, levels_ref, drag_ref, mixed_ref, velocity_ref, pull_ref, drag_out_ref):
    slot = lax.div(unit, BY // UNIT)
    rows = pl.ds(pl.multiple_of(lax.rem(unit, BY // UNIT) * UNIT, UNIT), UNIT)
    levels = levels_ref[slot, rows, :]
    zero = jnp.zeros((UNIT, BX), jnp.float32)

    def level(k, state, first_level=False):
        above0, flux0, above1, flux1, flow_b, column_b, rate = state
        last = k >= LEV - 1
        wet_next = levels > k + 1
        rate_next = jnp.where(wet_next, mix_rate, 0.0)
        bottom = levels == k
        out = [[], [], [], [], [], []]
        for c in range(2):
            if last:
                below = down = zero
                first = above0[c] - flux0[c]
            else:
                below = jnp.where(wet_next, mixed_ref[slot, c, k + 1, rows, :], 0.0)
                down = (below - above0[c]) * rate_next
                first = above0[c] + down - flux0[c]
            if first_level:
                down1, flow, col = zero, flow_b[c], column_b[c]
            else:
                down1 = zero if k == LEV else (first - above1[c]) * rate
                second = above1[c] + down1 - flux1[c]
                mixed_ref[slot, c, k - 1, rows, :] = second
                col = jnp.where(bottom, second, column_b[c])
                flow = jnp.where(bottom, velocity_ref[slot, c, k - 1, rows, :].astype(jnp.float32), flow_b[c])
            for pile, value in zip(out, (below, down, first, down1, flow, col)):
                pile.append(value)
        return (*(tuple(pile) for pile in out), rate_next)

    wet_top = levels > 0
    top = tuple(jnp.where(wet_top, mixed_ref[slot, c, 0, rows, :], 0.0) for c in range(2))
    both = (zero, zero)
    state = level(0, (top, both, both, both, both, both, zero), first_level=True)
    for k in range(1, LEV + 1):
        state = level(k, state)
    flow_b, column_b = state[4], state[5]
    speed = jnp.sqrt(flow_b[0] * flow_b[0] + flow_b[1] * flow_b[1] + speed_floor)
    along = flow_b[0] * column_b[0] + flow_b[1] * column_b[1]
    ratio = along / speed
    drag = drag_ref[slot, rows, :]
    drag_out_ref[slot, rows, :] = -drag_step * speed * along
    for c in range(2):
        pull_ref[slot, c, rows, :] = drag_step * (drag * (speed * column_b[c] + flow_b[c] * ratio))


def main_kernel(
    ids_ref,
    table_ref,
    count_ref,
    drag_ref,
    bathymetry_ref,
    mask_ref,
    adjoint_hbm,
    velocity_hbm,
    mixed_ref,
    press_ref,
    pull_ref,
    drag_out_ref,
    surface_ref,
    sens_ref,
    levels_ref,
    velocity_ref,
    idbuf,
    forward_vec,
    back_vec,
    forward_idx,
    back_idx,
    cand,
    spread,
    gathered,
    source_own,
    scaled_out,
    scaled_own,
    result_out,
    result_in,
    packed_scaled,
    packed_source,
    vert_scaled,
    vert_source,
    side_scaled,
    side_source,
    east_w,
    north_w,
    scaled_ext,
    direction,
    residual,
    height,
    west_w,
    south_w,
    diagonal,
    returned,
    edge_pairs,
    edges,
    slot_out,
    slot_in,
    edge_out,
    edge_in,
    slot_sum,
    load_sem,
    id_send,
    id_recv,
    a_send,
    a_recv,
    b_send,
    b_recv,
    h_send,
    h_recv,
    g_send,
    g_recv,
    rb_send,
    rb_recv,
    ra_send,
    ra_recv,
    place_send,
    place_recv,
    local_sem,
):
    gx = lax.axis_index("gx")
    gy = lax.axis_index("gy")
    my_x, my_zh = lax.div(gx, 2), lax.rem(gx, 2)
    my_y, my_zl, my_c = lax.div(gy, 4), lax.rem(lax.div(gy, 2), 2), lax.rem(gy, 2)
    my_z = my_zh * 2 + my_zl

    def a_peer(o, sign):
        step_x, step_c = o // 2, o % 2
        if sign < 0:
            step_x = (NX_CHIPS - step_x) % NX_CHIPS
        x = lax.rem(my_x + step_x, NX_CHIPS)
        c = lax.rem(my_c + step_c, CORES)
        return (x * 2 + my_zh, my_y * 4 + my_zl * 2 + c)

    def b_peer(p, sign):
        step_y, step_z = p // NZ_CHIPS, p % NZ_CHIPS
        if sign < 0:
            step_y = (NY_CHIPS - step_y) % NY_CHIPS
            step_z = (NZ_CHIPS - step_z) % NZ_CHIPS
        y = lax.rem(my_y + step_y, NY_CHIPS)
        z = lax.rem(my_z + step_z, NZ_CHIPS)
        return (my_x * 2 + lax.div(z, 2), y * 4 + lax.rem(z, 2) * 2 + my_c)

    def snake(y_grid, z):
        return z + lax.rem(y_grid, 2) * (NZ_CHIPS - 1 - 2 * z)

    def solver_of(lon, lat):
        y_grid = lax.div(lat, NZ_CHIPS)
        z = snake(y_grid, lax.rem(lat, NZ_CHIPS))
        y = lax.rem(y_grid + NY_CHIPS - 1, NY_CHIPS)
        return (lax.div(lon, 2) * 2 + lax.div(z, 2), y * 4 + lax.rem(z, 2) * 2 + lax.rem(lon, 2))

    lon = my_x * 2 + my_c
    my_y_grid = lax.rem(my_y + 1, NY_CHIPS)
    lat = my_y_grid * NZ_CHIPS + snake(my_y_grid, my_z)

    def near(n):
        dx, dy = AROUND[n]
        return solver_of(lax.rem(lon + dx + 8, 8), lax.rem(lat + dy + 16, 16))

    def copy(src, dst, send, recv, to):
        return pltpu.make_async_remote_copy(
            src_ref=src, dst_ref=dst, send_sem=send, recv_sem=recv, device_id=to, device_id_type=MESH
        )

    def arrived(whole, send, recv):
        copy(whole, whole, send, recv, (gx, gy)).wait()

    a_order = sorted(range(1, A_SIZE), key=lambda o: -min(o // 2, NX_CHIPS - o // 2))
    b_order = sorted(
        range(1, B_SIZE),
        key=lambda p: -min(p // NZ_CHIPS, NY_CHIPS - p // NZ_CHIPS) - min(p % NZ_CHIPS, NZ_CHIPS - p % NZ_CHIPS),
    )

    loads = []
    for q in range(CHUNKS):
        part = (slice(None), slice(None), slice(None), pl.ds(q * CH, CH))
        loads.append(pltpu.make_async_copy(adjoint_hbm.at[part], mixed_ref.at[part], load_sem.at[q]))
    loads.append(pltpu.make_async_copy(velocity_hbm, velocity_ref, load_sem.at[CHUNKS]))
    loads[0].start()
    loads[1].start()

    barrier = pltpu.get_barrier_semaphore()
    for o in range(1, A_SIZE):
        pl.semaphore_signal(barrier, inc=1, device_id=a_peer(o, 1), device_id_type=MESH)
    for p in range(1, B_SIZE):
        pl.semaphore_signal(barrier, inc=1, device_id=b_peer(p, 1), device_id_type=MESH)
    for n in range(8):
        pl.semaphore_signal(barrier, inc=1, device_id=near(n), device_id_type=MESH)
    pl.semaphore_signal(barrier, inc=1, device_id=solver_of(gx, gy), device_id_type=MESH)
    pl.semaphore_signal(barrier, inc=1, device_id=(lon, lat), device_id_type=MESH)

    lane8 = lax.broadcasted_iota(jnp.int32, (8, BX), 1)
    lane32 = lax.broadcasted_iota(jnp.int32, (BY, BX), 1)
    row8 = lax.broadcasted_iota(jnp.int32, (8, BX), 0)
    row32 = lax.broadcasted_iota(jnp.int32, (BY, BX), 0)

    id_row = jnp.full((8, BX), -1, jnp.int32)
    for s in range(SLOTS):
        id_row = jnp.where(lane8 == s, ids_ref[s], id_row)
        levels_ref[s] = count_ref[s] * jnp.where(ids_ref[s] < 256, 1, 0)
    idbuf[0] = id_row
    for q in range(CHUNKS):
        cand[q][0] = jnp.zeros((CH, BX), jnp.float32)
        returned[q][0] = jnp.zeros((CH, BX), jnp.float32)
    edges[0] = jnp.zeros((8, BX), jnp.float32)

    def pack(block, base):
        out = jnp.zeros((8, BX), jnp.float32)
        for q in range(4):
            part = lane_roll(block[8 * q : 8 * q + 8, :], 32 * q - base)
            out = jnp.where(lane8 // 32 == q, part, out)
        return out

    def unpack(packed, base):
        return jnp.concatenate([lane_roll(packed, base - 32 * q) for q in range(4)], axis=0)

    scaled = bathymetry_ref[...] * mask_ref[...].astype(jnp.float32)
    scaled_out[0] = scaled[:, :BX]
    scaled_out[1] = scaled[:, BX:]

    def force(q):
        rows = slice(q * CH, (q + 1) * CH)

        def one(s, carry):
            levels = levels_ref[s, rows, :]
            totals = [jnp.zeros((CH, BX), jnp.float32)] * 4
            for k in range(LEV):
                pair = mixed_ref[s, 0, k, rows, :] + mixed_ref[s, 1, k, rows, :]
                totals[k % 4] = totals[k % 4] + jnp.where(levels > k, pair, 0.0)
            cand[q][1 + s] = force_scale * ((totals[0] + totals[1]) + (totals[2] + totals[3]))
            return carry

        lax.fori_loop(0, SLOTS, one, 0)

    loads[0].wait()
    loads[2].start()
    force(0)
    pl.semaphore_wait(barrier, A_SIZE - 1 + B_SIZE - 1 + 8 + 2)

    for o in a_order:
        copy(idbuf.at[0], idbuf.at[o], id_send.at[0], id_recv.at[0], a_peer(o, 1)).start()

    place_copy = copy(scaled_out, scaled_own, place_send.at[0], place_recv.at[0], solver_of(gx, gy))
    place_copy.start()
    def send_a(q):
        for o in a_order:
            copy(
                cand[q].at[pl.ds(1, SLOTS)],
                cand[q].at[pl.ds(1 + SLOTS * o, SLOTS)],
                a_send.at[q],
                a_recv.at[q],
                a_peer(o, 1),
            ).start()

    send_a(0)

    def send_halo(own, packed, vert, side, send, recv):
        for n, (dx, dy) in enumerate(AROUND):
            if dx == 0:
                copy(own, vert.at[0 if dy < 0 else 1], send.at[0], recv.at[0], near(n)).start()
        for n, (dx, dy) in enumerate(AROUND):
            if dx != 0:
                copy(packed.at[0 if dx < 0 else 1], side.at[SIDES.index((dx, dy))], send.at[1], recv.at[1], near(n)).start()

    def halo_arrived(vert, side, send, recv):
        arrived(vert, send.at[0], recv.at[0])
        arrived(side, send.at[1], recv.at[1])

    def extended(own, vert, side):
        bands = []
        for dy in (-1, 0, 1):
            if dy == 0:
                left, right = own[0], own[1]
                inside = jnp.float32(1.0)
            else:
                k = 0 if dy > 0 else 1
                left, right = vert[k, 0], vert[k, 1]
                inside = jnp.where(lat + dy >= 0, 1.0, 0.0) * jnp.where(lat + dy < 16, 1.0, 0.0)
            west = unpack(side[SIDES.index((1, -dy))], 32) * jnp.where(lon > 0, 1.0, 0.0)
            east = unpack(side[SIDES.index((-1, -dy))], 64) * jnp.where(lon < 7, 1.0, 0.0)
            left, right = lane_roll(left, 64), lane_roll(right, 64)
            first = jnp.where(lane32 < 32, 0.0, jnp.where(lane32 < 64, west, left))
            middle = jnp.where(lane32 < 64, left, right)
            last = jnp.where(lane32 < 64, right, jnp.where(lane32 < 96, east, 0.0))
            bands.append(jnp.concatenate([first, middle, last], axis=1) * inside)
        return jnp.concatenate(bands, axis=0)

    def units(first, last):
        def one(unit, carry):
            mix_unit(unit, levels_ref, drag_ref, mixed_ref, velocity_ref, pull_ref, drag_out_ref)
            return carry

        lax.fori_loop(first, last, one, 0)

    for q in range(1, CHUNKS):
        loads[q].wait()
        if q + 2 <= CHUNKS:
            loads[q + 2].start()
        force(q)
        send_a(q)

    place_copy.wait()
    packed_scaled[0] = pack(scaled_own[0], 0)
    packed_scaled[1] = pack(scaled_own[1], 96)
    send_halo(scaled_own, packed_scaled, vert_scaled, side_scaled, h_send, h_recv)

    loads[CHUNKS].wait()
    units(0, 2)
    arrived(idbuf.at[pl.ds(1, A_SIZE - 1)], id_send.at[0], id_recv.at[0])
    spot = lax.broadcasted_iota(jnp.int32, (2 * B_SIZE, BX), 0)
    spot_lane = lax.broadcasted_iota(jnp.int32, (2 * B_SIZE, BX), 1)
    spot_p = spot // 2
    spot_y = (my_y + spot_p // NZ_CHIPS + 1) % NY_CHIPS
    spot_z = (my_z + spot_p % NZ_CHIPS) % NZ_CHIPS
    owner = lon * 16 + spot_y * NZ_CHIPS + spot_z + (spot_y % 2) * (NZ_CHIPS - 1 - 2 * spot_z)
    target = owner * 2 + spot % 2
    forward = jnp.zeros((2 * B_SIZE, BX), jnp.int32)
    for o in range(A_SIZE):
        ids = jnp.broadcast_to(idbuf[o, 0:1, :], (2 * B_SIZE, BX))
        hit = ids == target
        forward = forward + jnp.where(hit, spot_lane + (1 + SLOTS * o), 0)
        back = jnp.sum(jnp.where(hit, spot + 1, 0), axis=0, keepdims=True)
        back_vec[o : o + 1, :] = back
    forward_vec[...] = jnp.broadcast_to(jnp.sum(forward, axis=1, keepdims=True), forward.shape)
    to_scalar = [
        pltpu.make_async_copy(forward_vec, forward_idx, local_sem.at[0]),
        pltpu.make_async_copy(back_vec, back_idx, local_sem.at[1]),
    ]
    for c in to_scalar:
        c.start()
    for c in to_scalar:
        c.wait()

    def picked(r):
        return jnp.clip(forward_idx[r, 0], 0, SLOTS * A_SIZE)

    def back_of(o, s):
        return jnp.clip(back_idx[o, s], 0, 2 * B_SIZE)

    for q in range(CHUNKS):
        arrived(cand[q].at[pl.ds(1 + SLOTS, SLOTS * (A_SIZE - 1))], a_send.at[q], a_recv.at[q])
        for p in b_order + [0]:
            for h in range(2):
                spread[q, p, h] = cand[q][picked(2 * p + h)]
            if p > 0:
                copy(spread.at[q, p], gathered.at[q, p], b_send.at[q], b_recv.at[q], b_peer(p, 1)).start()

    units(2, 6)
    halo_arrived(vert_scaled, side_scaled, h_send, h_recv)
    scaled_ext[...] = extended(scaled_own, vert_scaled, side_scaled)
    all_scaled = scaled_ext[...]
    tall = all_scaled.shape[0]
    east_w[...] = jnp.sqrt(all_scaled * lane_roll(all_scaled, -1))
    north_w[...] = jnp.sqrt(all_scaled * pltpu.roll(all_scaled, tall - 1, 0))
    west_w[...] = lane_roll(east_w[...], 1)
    south_w[...] = pltpu.roll(north_w[...], 1, 0)
    diagonal[...] = surface_shift + ((east_w[...] + west_w[...]) + (north_w[...] + south_w[...]))

    for q in range(CHUNKS):
        arrived(gathered.at[q, pl.ds(1, B_SIZE - 1)], b_send.at[q], b_recv.at[q])
        rows = slice(q * CH, (q + 1) * CH)
        for h in range(2):
            total = spread[q, 0, h]
            for p in range(1, B_SIZE):
                total = total + gathered[q, p, h]
            source_own[h, rows, :] = jnp.where(scaled_own[h, rows, :] > 0.0, total, 0.0)

    packed_source[0] = pack(source_own[0], 0)
    packed_source[1] = pack(source_own[1], 96)
    send_halo(source_own, packed_source, vert_source, side_source, g_send, g_recv)
    halo_arrived(vert_source, side_source, g_send, g_recv)
    start = extended(source_own, vert_source, side_source)
    centre, _ = chebyshev_table(STEPS)
    residual[...] = start
    direction[...] = start / centre
    core = slice(BY - 8, 2 * BY + 8)
    height[...] = jnp.zeros(height.shape, jnp.float32)

    def group(step, count, phase):
        band = slice(8 * phase, tall - 8 * phase)
        rows = tall - 16 * phase
        inner = slice(BY - 8 - 8 * phase, BY - 8 - 8 * phase + BY + 16)
        now, left, total = direction[band, :], residual[band, :], height[...]
        for i in range(count):
            total = total + now[inner, :]
            image = diagonal[band, :] * now
            image = image - (east_w[band, :] * lane_roll(now, -1) + west_w[band, :] * lane_roll(now, 1))
            image = image - (north_w[band, :] * pltpu.roll(now, rows - 1, 0) + south_w[band, :] * pltpu.roll(now, 1, 0))
            left = left - image
            now = table_ref[2 * (step + i)] * now + table_ref[2 * (step + i) + 1] * left
        direction[band, :], residual[band, :], height[...] = now, left, total

    for phase in range(3):
        group(8 * phase, 8, phase)
    group(24, 7, 3)
    height[...] = height[...] + direction[core, :]

    def own_blocks(values):
        a, b, c = (lane_roll(values[:, k * BX : (k + 1) * BX], 64) for k in range(3))
        low = lax.broadcasted_iota(jnp.int32, a.shape, 1) < 64
        return jnp.where(low, a, b), jnp.where(low, b, c)

    mid = height[8 : BY + 8, :]
    own_heights = own_blocks(mid)
    next_rows = own_blocks(height[BY + 8 : BY + 16, :])
    pair = jnp.zeros((8, BX), jnp.float32)
    for h in range(2):
        tile = mid[:, (h + 1) * BX : (h + 2) * BX]
        column = jnp.sum(jnp.where(lane32 == 64, tile, 0.0), axis=1, keepdims=True)
        flat = jnp.sum(jnp.where(row32 == lane32, column, 0.0), axis=0, keepdims=True)
        next_row = next_rows[h] if h == 0 else pltpu.roll(next_rows[h], 2 * h, 0)
        pair = jnp.where(row8 == 2 * h, next_row, jnp.where(row8 == 2 * h + 1, flat, pair))
        for q in range(CHUNKS):
            returned[q][1 + h] = own_heights[h][q * CH : (q + 1) * CH, :]
    edge_pairs[0] = pair

    for p in b_order:
        copy(edge_pairs.at[0], edge_pairs.at[p], rb_send.at[CHUNKS], rb_recv.at[CHUNKS], b_peer(p, -1)).start()
    for q in range(CHUNKS):
        for p in b_order:
            copy(
                returned[q].at[pl.ds(1, 2)],
                returned[q].at[pl.ds(1 + 2 * p, 2)],
                rb_send.at[q],
                rb_recv.at[q],
                b_peer(p, -1),
            ).start()

    east_step = lane_roll(mid, -1) - mid
    north_step = height[9 : BY + 9, :] - mid
    south_step = mid - height[7 : BY + 7, :]
    east_energy = east_w[BY : 2 * BY, :] * east_step * east_step
    total = (
        east_energy
        + lane_roll(east_energy, 1)
        + north_w[BY : 2 * BY, :] * north_step * north_step
        + north_w[BY - 1 : 2 * BY - 1, :] * south_step * south_step
    )
    sens = 0.25 * total / jnp.maximum(scaled_ext[BY : 2 * BY, :], 0.25)
    for h, (sens_part, height_part) in enumerate(zip(own_blocks(sens), own_heights)):
        result_out[0, :, h * BX : (h + 1) * BX] = height_part
        result_out[1, :, h * BX : (h + 1) * BX] = sens_part

    units(6, 8)
    arrived(edge_pairs.at[pl.ds(1, B_SIZE - 1)], rb_send.at[CHUNKS], rb_recv.at[CHUNKS])
    for p in range(B_SIZE):
        both = edge_pairs[p]
        edges[1 + 2 * p] = jnp.where(row8 < 2, both, 0.0)
        edges[2 + 2 * p] = jnp.where(row8 < 2, pltpu.roll(both, 6, 0), 0.0)
    for o in a_order + [0]:
        tile = edges[back_of(o, 0)]
        for s in range(1, SLOTS):
            tile = tile + pltpu.roll(edges[back_of(o, s)], 2 * s, 0)
        edge_out[o] = tile
        if o > 0:
            copy(edge_out.at[o], edge_in.at[o], ra_send.at[CHUNKS], ra_recv.at[CHUNKS], a_peer(o, -1)).start()
    for q in range(CHUNKS):
        arrived(returned[q].at[pl.ds(3, 2 * (B_SIZE - 1))], rb_send.at[q], rb_recv.at[q])
        for o in a_order + [0]:
            for s in range(SLOTS):
                slot_out[q, o, s] = returned[q][back_of(o, s)]
            if o > 0:
                copy(slot_out.at[q, o], slot_in.at[q, o], ra_send.at[q], ra_recv.at[q], a_peer(o, -1)).start()
    result_copy = copy(result_out, result_in, place_send.at[1], place_recv.at[1], (lon, lat))
    result_copy.start()
    arrived(edge_in.at[pl.ds(1, A_SIZE - 1)], ra_send.at[CHUNKS], ra_recv.at[CHUNKS])
    edge = edge_out[0]
    for o in range(1, A_SIZE):
        edge = edge + edge_in[o]
    for s in range(SLOTS):
        slot_sum[s, BY : BY + 8, :] = edge if s == 0 else pltpu.roll(edge, 8 - 2 * s, 0)
    for q in range(CHUNKS):
        arrived(slot_in.at[q, pl.ds(1, A_SIZE - 1)], ra_send.at[q], ra_recv.at[q])
        for s in range(SLOTS):
            total = slot_out[q, 0, s]
            for o in range(1, A_SIZE):
                total = total + slot_in[q, o, s]
            slot_sum[s, q * CH : (q + 1) * CH, :] = total
    result_copy.wait()
    surface_ref[...] = result_in[0]
    sens_ref[...] = result_in[1]
    for s in range(SLOTS):
        here = slot_sum[s, 0:BY, :]
        flat = jnp.broadcast_to(slot_sum[s, BY + 1 : BY + 2, :], (BY, BX))
        column = jnp.sum(jnp.where(row32 == lane32, flat, 0.0), axis=1, keepdims=True)
        beside = jnp.where(lane32 == BX - 1, column, lane_roll(here, -1))
        press_ref[s, 0] = pressure_gain * (beside - here)
        press_ref[s, 1] = pressure_gain * (slot_sum[s, 1 : BY + 1, :] - here)


def main_call(block_ids, level_count, drag_coef, bathymetry, land_mask, adjoint_vel, velocity):
    _, table = chebyshev_table(STEPS)
    flat_table = jnp.array([v for pair in table for v in pair], jnp.float32)
    f32, i32 = jnp.float32, jnp.int32
    wide = (3 * BY, 3 * BX)
    dma = pltpu.SemaphoreType.DMA
    vmem = pl.BlockSpec(memory_space=pltpu.VMEM)
    smem = pl.BlockSpec(memory_space=pltpu.SMEM)
    hbm = pl.BlockSpec(memory_space=pltpu.HBM)
    return pl.pallas_call(
        main_kernel,
        out_shape=(
            pltpu.VMEM((SLOTS, 2, LEV, BY, BX), f32),
            pltpu.VMEM((SLOTS, 2, BY, BX), f32),
            pltpu.VMEM((SLOTS, 2, BY, BX), f32),
            pltpu.VMEM((SLOTS, BY, BX), f32),
            pltpu.VMEM((BY, 2 * BX), f32),
            pltpu.VMEM((BY, 2 * BX), f32),
        ),
        in_specs=[smem, smem, vmem, vmem, vmem, vmem, hbm, hbm],
        out_specs=(vmem,) * 6,
        scratch_shapes=[
            pltpu.VMEM((SLOTS, BY, BX), i32),
            pltpu.VMEM((SLOTS, 2, LEV, BY, BX), jnp.bfloat16),
            pltpu.VMEM((A_SIZE, 8, BX), i32),
            pltpu.VMEM((2 * B_SIZE, BX), i32),
            pltpu.VMEM((A_SIZE, BX), i32),
            pltpu.SMEM((2 * B_SIZE, BX), i32),
            pltpu.SMEM((A_SIZE, BX), i32),
            [pltpu.VMEM((1 + SLOTS * A_SIZE, CH, BX), f32) for _ in range(CHUNKS)],
            pltpu.VMEM((CHUNKS, B_SIZE, 2, CH, BX), f32),
            pltpu.VMEM((CHUNKS, B_SIZE, 2, CH, BX), f32),
            pltpu.VMEM((2, BY, BX), f32),
            pltpu.VMEM((2, BY, BX), f32),
            pltpu.VMEM((2, BY, BX), f32),
            pltpu.VMEM((2, BY, 2 * BX), f32),
            pltpu.VMEM((2, BY, 2 * BX), f32),
            pltpu.VMEM((2, 8, BX), f32),
            pltpu.VMEM((2, 8, BX), f32),
            pltpu.VMEM((2, 2, BY, BX), f32),
            pltpu.VMEM((2, 2, BY, BX), f32),
            pltpu.VMEM((len(SIDES), 8, BX), f32),
            pltpu.VMEM((len(SIDES), 8, BX), f32),
            pltpu.VMEM(wide, f32),
            pltpu.VMEM(wide, f32),
            pltpu.VMEM(wide, f32),
            pltpu.VMEM(wide, f32),
            pltpu.VMEM(wide, f32),
            pltpu.VMEM((BY + 16, 3 * BX), f32),
            pltpu.VMEM(wide, f32),
            pltpu.VMEM(wide, f32),
            pltpu.VMEM(wide, f32),
            [pltpu.VMEM((1 + 2 * B_SIZE, CH, BX), f32) for _ in range(CHUNKS)],
            pltpu.VMEM((B_SIZE, 8, BX), f32),
            pltpu.VMEM((1 + 2 * B_SIZE, 8, BX), f32),
            pltpu.VMEM((CHUNKS, A_SIZE, SLOTS, CH, BX), f32),
            pltpu.VMEM((CHUNKS, A_SIZE, SLOTS, CH, BX), f32),
            pltpu.VMEM((A_SIZE, 8, BX), f32),
            pltpu.VMEM((A_SIZE, 8, BX), f32),
            pltpu.VMEM((SLOTS, BY + 8, BX), f32),
            dma((CHUNKS + 1,)),
            dma((1,)),
            dma((1,)),
            dma((CHUNKS,)),
            dma((CHUNKS,)),
            dma((CHUNKS,)),
            dma((CHUNKS,)),
            dma((2,)),
            dma((2,)),
            dma((2,)),
            dma((2,)),
            dma((CHUNKS + 1,)),
            dma((CHUNKS + 1,)),
            dma((CHUNKS + 1,)),
            dma((CHUNKS + 1,)),
            dma((2,)),
            dma((2,)),
            dma((2,)),
        ],
        compiler_params=pltpu.CompilerParams(
            collective_id=0, has_side_effects=True, vmem_limit_bytes=50 * 2**20
        ),
        name="columns_and_surface",
    )(block_ids, flat_table, level_count, drag_coef, bathymetry, land_mask, adjoint_vel, velocity)


def final_kernel(
    count_ref, mixed_ref, press_ref, pull_ref, drag_ref, surface_ref, sens_ref,
    out_hbm, drag_out_ref, surface_out_ref, sens_out_ref, stage, sems, small_sems,
):
    small = ((drag_ref, drag_out_ref), (surface_ref, surface_out_ref), (sens_ref, sens_out_ref))
    puts = [pltpu.make_async_copy(src, dst, small_sems.at[i]) for i, (src, dst) in enumerate(small)]
    for c in puts:
        c.start()
    for slot in range(SLOTS):
        levels = count_ref[slot]
        for c in range(2):
            press = press_ref[slot, c]
            bed = press + pull_ref[slot, c]
            for piece in range(PIECES):
                for k in range(piece * LEV // PIECES, (piece + 1) * LEV // PIECES):
                    less = jnp.where(levels == k + 1, bed, jnp.where(levels > k, press, 0.0))
                    stage[slot, c, k] = mixed_ref[slot, c, k] - less
                part = (slot, c, pl.ds(piece * LEV // PIECES, LEV // PIECES))
                puts.append(pltpu.make_async_copy(stage.at[part], out_hbm.at[part], sems.at[len(puts) - len(small)]))
                puts[-1].start()
    for c in puts:
        c.wait()


def final_call(level_count, mixed, press, pull, drag_grad, surface, sens):
    f32 = jnp.float32
    vmem = pl.BlockSpec(memory_space=pltpu.VMEM)
    deep = (SLOTS, 2, LEV, BY, BX)
    return pl.pallas_call(
        final_kernel,
        out_shape=(
            jax.ShapeDtypeStruct(deep, f32),
            jax.ShapeDtypeStruct(drag_grad.shape, f32),
            jax.ShapeDtypeStruct(surface.shape, f32),
            jax.ShapeDtypeStruct(sens.shape, f32),
        ),
        in_specs=[vmem] * 7,
        out_specs=(pl.BlockSpec(memory_space=pltpu.HBM),) * 4,
        scratch_shapes=[pltpu.VMEM(deep, f32), pltpu.SemaphoreType.DMA((SLOTS * 2 * PIECES,)), pltpu.SemaphoreType.DMA((3,))],
        compiler_params=pltpu.CompilerParams(vmem_limit_bytes=24 * 2**20),
        name="pressure_correction",
    )(level_count, mixed, press, pull, drag_grad, surface, sens)


def per_device(adjoint_vel, velocity, drag_coef, level_count, block_ids, bathymetry, land_mask):
    mixed, press, pull, drag_grad, surface, sens = main_call(
        block_ids, level_count, drag_coef, bathymetry, land_mask, adjoint_vel, velocity
    )
    return final_call(level_count, mixed, press, pull, drag_grad, surface, sens)


def solution(mesh):
    slots = P(("gx", "gy"), None, None, None, None)
    flat = P(("gx", "gy"), None, None)
    return jax.shard_map(
        per_device,
        mesh=mesh,
        in_specs=(slots, slots, flat, flat, P(("gx", "gy")), P("gy", "gx"), P("gy", "gx")),
        out_specs=(slots, flat, P("gy", "gx"), P("gy", "gx")),
        check_vma=False,
    )
```

```python
import jax
import jax.numpy as jnp
from jax import lax
from jax.experimental import pallas as pl
from jax.experimental.pallas import tpu as pltpu
from jax.sharding import PartitionSpec as P

MESH = pl.DeviceIdType.MESH
STEPS = 32
LEV = 62
BY = 32
BX = 128
SLOTS = 4
CHUNKS = 4
CH = BY // CHUNKS
NX_CHIPS, NY_CHIPS, NZ_CHIPS, CORES = 4, 4, 4, 2
A_SIZE = NX_CHIPS * CORES
B_SIZE = NY_CHIPS * NZ_CHIPS
AROUND = ((-1, -1), (-1, 0), (-1, 1), (0, -1), (0, 1), (1, -1), (1, 0), (1, 1))
SIDES = tuple(d for d in AROUND if d[0] != 0)
UNIT = 16
UNITS = SLOTS * BY // UNIT
PIECES = 2

mix_rate = 0.25
drag_step = 0.5
force_scale = 0.25
pressure_gain = 0.5
surface_shift = 1.0 / 64.0
speed_floor = 0.01


def chebyshev_table(total_steps):
    highest = surface_shift + 8.0
    centre = 0.5 * (highest + surface_shift)
    radius = 0.5 * (highest - surface_shift)
    sigma_ratio = centre / radius
    ratio_prev = 1.0 / sigma_ratio
    table = []
    for _ in range(total_steps):
        ratio_next = 1.0 / (2.0 * sigma_ratio - ratio_prev)
        table.append((ratio_next * ratio_prev, 2.0 * ratio_next / radius))
        ratio_prev = ratio_next
    return (centre, table)


def lane_roll(values, shift):
    return pltpu.roll(values, shift % values.shape[-1], values.ndim - 1)


def mix_unit(unit, levels_ref, drag_ref, mixed_ref, velocity_ref, pull_ref, drag_out_ref):
    slot = lax.div(unit, BY // UNIT)
    rows = pl.ds(pl.multiple_of(lax.rem(unit, BY // UNIT) * UNIT, UNIT), UNIT)
    levels = levels_ref[slot, rows, :]
    zero = jnp.zeros((UNIT, BX), jnp.float32)

    def level(k, state, first_level=False):
        above0, flux0, above1, flux1, flow_b, column_b, rate = state
        last = k >= LEV - 1
        wet_next = levels > k + 1
        rate_next = jnp.where(wet_next, mix_rate, 0.0)
        bottom = levels == k
        out = [[], [], [], [], [], []]
        for c in range(2):
            if last:
                below = down = zero
                first = above0[c] - flux0[c]
            else:
                below = jnp.where(wet_next, mixed_ref[slot, c, k + 1, rows, :], 0.0)
                down = (below - above0[c]) * rate_next
                first = above0[c] + down - flux0[c]
            if first_level:
                down1, flow, col = zero, flow_b[c], column_b[c]
            else:
                down1 = zero if k == LEV else (first - above1[c]) * rate
                second = above1[c] + down1 - flux1[c]
                mixed_ref[slot, c, k - 1, rows, :] = second
                col = jnp.where(bottom, second, column_b[c])
                flow = jnp.where(bottom, velocity_ref[slot, c, k - 1, rows, :].astype(jnp.float32), flow_b[c])
            for pile, value in zip(out, (below, down, first, down1, flow, col)):
                pile.append(value)
        return (*(tuple(pile) for pile in out), rate_next)

    wet_top = levels > 0
    top = tuple(jnp.where(wet_top, mixed_ref[slot, c, 0, rows, :], 0.0) for c in range(2))
    both = (zero, zero)
    state = level(0, (top, both, both, both, both, both, zero), first_level=True)
    for k in range(1, LEV + 1):
        state = level(k, state)
    flow_b, column_b = state[4], state[5]
    speed = jnp.sqrt(flow_b[0] * flow_b[0] + flow_b[1] * flow_b[1] + speed_floor)
    along = flow_b[0] * column_b[0] + flow_b[1] * column_b[1]
    ratio = along / speed
    drag = drag_ref[slot, rows, :]
    drag_out_ref[slot, rows, :] = -drag_step * speed * along
    for c in range(2):
        pull_ref[slot, c, rows, :] = drag_step * (drag * (speed * column_b[c] + flow_b[c] * ratio))


def main_kernel(
    ids_hbm,
    count_hbm,
    drag_hbm,
    bathymetry_hbm,
    mask_hbm,
    adjoint_hbm,
    velocity_hbm,
    mixed_ref,
    press_ref,
    pull_ref,
    drag_out_ref,
    surface_ref,
    sens_ref,
    levels_ref,
    velocity_ref,
    ids_ref,
    count_ref,
    drag_ref,
    bathymetry_ref,
    mask_ref,
    idbuf,
    forward_vec,
    back_vec,
    forward_idx,
    back_idx,
    cand,
    spread,
    gathered,
    source_own,
    scaled_out,
    scaled_own,
    result_out,
    result_in,
    packed_scaled,
    packed_source,
    vert_scaled,
    vert_source,
    side_scaled,
    side_source,
    east_w,
    north_w,
    scaled_ext,
    direction,
    residual,
    height,
    diagonal,
    returned,
    edge_pairs,
    edges,
    slot_out,
    slot_in,
    edge_out,
    edge_in,
    slot_sum,
    load_sem,
    id_send,
    id_recv,
    a_send,
    a_recv,
    b_send,
    b_recv,
    h_send,
    h_recv,
    g_send,
    g_recv,
    rb_send,
    rb_recv,
    ra_send,
    ra_recv,
    place_send,
    place_recv,
    local_sem,
    small_sem,
):
    gx = lax.axis_index("gx")
    gy = lax.axis_index("gy")
    my_x, my_zh = lax.div(gx, 2), lax.rem(gx, 2)
    my_y, my_zl, my_c = lax.div(gy, 4), lax.rem(lax.div(gy, 2), 2), lax.rem(gy, 2)
    my_z = my_zh * 2 + my_zl

    def a_peer(o, sign):
        step_x, step_c = o // 2, o % 2
        if sign < 0:
            step_x = (NX_CHIPS - step_x) % NX_CHIPS
        x = lax.rem(my_x + step_x, NX_CHIPS)
        c = lax.rem(my_c + step_c, CORES)
        return (x * 2 + my_zh, my_y * 4 + my_zl * 2 + c)

    def b_peer(p, sign):
        step_y, step_z = p // NZ_CHIPS, p % NZ_CHIPS
        if sign < 0:
            step_y = (NY_CHIPS - step_y) % NY_CHIPS
            step_z = (NZ_CHIPS - step_z) % NZ_CHIPS
        y = lax.rem(my_y + step_y, NY_CHIPS)
        z = lax.rem(my_z + step_z, NZ_CHIPS)
        return (my_x * 2 + lax.div(z, 2), y * 4 + lax.rem(z, 2) * 2 + my_c)

    def snake(y_grid, z):
        return z + lax.rem(y_grid, 2) * (NZ_CHIPS - 1 - 2 * z)

    def solver_of(lon, lat):
        y_grid = lax.div(lat, NZ_CHIPS)
        z = snake(y_grid, lax.rem(lat, NZ_CHIPS))
        y = lax.rem(y_grid + NY_CHIPS - 1, NY_CHIPS)
        return (lax.div(lon, 2) * 2 + lax.div(z, 2), y * 4 + lax.rem(z, 2) * 2 + lax.rem(lon, 2))

    lon = my_x * 2 + my_c
    my_y_grid = lax.rem(my_y + 1, NY_CHIPS)
    lat = my_y_grid * NZ_CHIPS + snake(my_y_grid, my_z)

    def near(n):
        dx, dy = AROUND[n]
        return solver_of(lax.rem(lon + dx + 8, 8), lax.rem(lat + dy + 16, 16))

    def copy(src, dst, send, recv, to):
        return pltpu.make_async_remote_copy(
            src_ref=src, dst_ref=dst, send_sem=send, recv_sem=recv, device_id=to, device_id_type=MESH
        )

    def arrived(whole, send, recv):
        copy(whole, whole, send, recv, (gx, gy)).wait()

    a_order = sorted(range(1, A_SIZE), key=lambda o: -min(o // 2, NX_CHIPS - o // 2))
    b_order = sorted(
        range(1, B_SIZE),
        key=lambda p: -min(p // NZ_CHIPS, NY_CHIPS - p // NZ_CHIPS) - min(p % NZ_CHIPS, NZ_CHIPS - p % NZ_CHIPS),
    )

    loads = []
    for q in range(CHUNKS):
        part = (slice(None), slice(None), slice(None), pl.ds(q * CH, CH))
        loads.append(pltpu.make_async_copy(adjoint_hbm.at[part], mixed_ref.at[part], load_sem.at[q]))
    loads.append(pltpu.make_async_copy(velocity_hbm, velocity_ref, load_sem.at[CHUNKS]))
    pairs = (
        (ids_hbm, ids_ref),
        (count_hbm, count_ref),
        (bathymetry_hbm, bathymetry_ref),
        (mask_hbm, mask_ref),
        (drag_hbm, drag_ref),
    )
    small = [pltpu.make_async_copy(src, dst, small_sem.at[i]) for i, (src, dst) in enumerate(pairs)]
    small[0].start()
    small[1].start()
    loads[0].start()
    for c in small[2:]:
        c.start()
    loads[1].start()

    barrier = pltpu.get_barrier_semaphore()
    for p in b_order:
        pl.semaphore_signal(barrier, inc=1, device_id=b_peer(p, 1), device_id_type=MESH)
    for o in a_order:
        pl.semaphore_signal(barrier, inc=1, device_id=a_peer(o, 1), device_id_type=MESH)
    for n in range(8):
        pl.semaphore_signal(barrier, inc=1, device_id=near(n), device_id_type=MESH)
    pl.semaphore_signal(barrier, inc=1, device_id=solver_of(gx, gy), device_id_type=MESH)
    pl.semaphore_signal(barrier, inc=1, device_id=(lon, lat), device_id_type=MESH)

    lane8 = lax.broadcasted_iota(jnp.int32, (8, BX), 1)
    lane32 = lax.broadcasted_iota(jnp.int32, (BY, BX), 1)
    row8 = lax.broadcasted_iota(jnp.int32, (8, BX), 0)
    row32 = lax.broadcasted_iota(jnp.int32, (BY, BX), 0)

    small[0].wait()
    small[1].wait()
    id_row = jnp.full((8, BX), -1, jnp.int32)
    for s in range(SLOTS):
        id_row = jnp.where(lane8 == s, ids_ref[s], id_row)
        levels_ref[s] = count_ref[s] * jnp.where(ids_ref[s] < 256, 1, 0)
    idbuf[0] = id_row
    for q in range(CHUNKS):
        cand[q][0] = jnp.zeros((CH, BX), jnp.float32)
        returned[q][0] = jnp.zeros((CH, BX), jnp.float32)
    edges[0] = jnp.zeros((8, BX), jnp.float32)

    def pack(block, base):
        out = jnp.zeros((8, BX), jnp.float32)
        for q in range(4):
            part = lane_roll(block[8 * q : 8 * q + 8, :], 32 * q - base)
            out = jnp.where(lane8 // 32 == q, part, out)
        return out

    def unpack(packed, base):
        return jnp.concatenate([lane_roll(packed, base - 32 * q) for q in range(4)], axis=0)

    small[2].wait()
    small[3].wait()
    scaled = bathymetry_ref[...] * mask_ref[...].astype(jnp.float32)
    scaled_out[0] = scaled[:, :BX]
    scaled_out[1] = scaled[:, BX:]

    def force(q):
        rows = slice(q * CH, (q + 1) * CH)

        def one(s, carry):
            levels = levels_ref[s, rows, :]
            totals = [jnp.zeros((CH, BX), jnp.float32)] * 4
            for k in range(LEV):
                pair = mixed_ref[s, 0, k, rows, :] + mixed_ref[s, 1, k, rows, :]
                totals[k % 4] = totals[k % 4] + jnp.where(levels > k, pair, 0.0)
            cand[q][1 + s] = force_scale * ((totals[0] + totals[1]) + (totals[2] + totals[3]))
            return carry

        lax.fori_loop(0, SLOTS, one, 0)

    loads[0].wait()
    loads[2].start()
    force(0)
    pl.semaphore_wait(barrier, A_SIZE - 1 + B_SIZE - 1 + 8 + 2)

    for o in a_order:
        copy(idbuf.at[0], idbuf.at[o], id_send.at[0], id_recv.at[0], a_peer(o, 1)).start()

    place_copy = copy(scaled_out, scaled_own, place_send.at[0], place_recv.at[0], solver_of(gx, gy))
    place_copy.start()
    def send_a(q):
        for o in a_order:
            copy(
                cand[q].at[pl.ds(1, SLOTS)],
                cand[q].at[pl.ds(1 + SLOTS * o, SLOTS)],
                a_send.at[q],
                a_recv.at[q],
                a_peer(o, 1),
            ).start()

    send_a(0)

    def send_halo(own, packed, vert, side, send, recv):
        for n, (dx, dy) in enumerate(AROUND):
            if dx == 0:
                copy(own, vert.at[0 if dy < 0 else 1], send.at[0], recv.at[0], near(n)).start()
        for n, (dx, dy) in enumerate(AROUND):
            if dx != 0:
                copy(packed.at[0 if dx < 0 else 1], side.at[SIDES.index((dx, dy))], send.at[1], recv.at[1], near(n)).start()

    def halo_arrived(vert, side, send, recv):
        arrived(vert, send.at[0], recv.at[0])
        arrived(side, send.at[1], recv.at[1])

    def extended(own, vert, side):
        bands = []
        for dy in (-1, 0, 1):
            if dy == 0:
                left, right = own[0], own[1]
                inside = jnp.float32(1.0)
            else:
                k = 0 if dy > 0 else 1
                left, right = vert[k, 0], vert[k, 1]
                inside = jnp.where(lat + dy >= 0, 1.0, 0.0) * jnp.where(lat + dy < 16, 1.0, 0.0)
            west = unpack(side[SIDES.index((1, -dy))], 32) * jnp.where(lon > 0, 1.0, 0.0)
            east = unpack(side[SIDES.index((-1, -dy))], 64) * jnp.where(lon < 7, 1.0, 0.0)
            left, right = lane_roll(left, 64), lane_roll(right, 64)
            first = jnp.where(lane32 < 32, 0.0, jnp.where(lane32 < 64, west, left))
            middle = jnp.where(lane32 < 64, left, right)
            last = jnp.where(lane32 < 64, right, jnp.where(lane32 < 96, east, 0.0))
            bands.append(jnp.concatenate([first, middle, last], axis=1) * inside)
        return jnp.concatenate(bands, axis=0)

    def units(first, last):
        def one(unit, carry):
            mix_unit(unit, levels_ref, drag_ref, mixed_ref, velocity_ref, pull_ref, drag_out_ref)
            return carry

        lax.fori_loop(first, last, one, 0)

    for q in range(1, CHUNKS):
        loads[q].wait()
        if q + 2 <= CHUNKS:
            loads[q + 2].start()
        force(q)
        send_a(q)

    arrived(idbuf.at[pl.ds(1, A_SIZE - 1)], id_send.at[0], id_recv.at[0])
    spot = lax.broadcasted_iota(jnp.int32, (2 * B_SIZE, BX), 0)
    spot_lane = lax.broadcasted_iota(jnp.int32, (2 * B_SIZE, BX), 1)
    spot_p = spot // 2
    spot_y = (my_y + spot_p // NZ_CHIPS + 1) % NY_CHIPS
    spot_z = (my_z + spot_p % NZ_CHIPS) % NZ_CHIPS
    owner = lon * 16 + spot_y * NZ_CHIPS + spot_z + (spot_y % 2) * (NZ_CHIPS - 1 - 2 * spot_z)
    target = owner * 2 + spot % 2
    forward = jnp.zeros((2 * B_SIZE, BX), jnp.int32)
    for o in range(A_SIZE):
        ids = jnp.broadcast_to(idbuf[o, 0:1, :], (2 * B_SIZE, BX))
        hit = ids == target
        forward = forward + jnp.where(hit, spot_lane + (1 + SLOTS * o), 0)
        back = jnp.sum(jnp.where(hit, spot + 1, 0), axis=0, keepdims=True)
        back_vec[o : o + 1, :] = back
    forward_vec[...] = jnp.broadcast_to(jnp.sum(forward, axis=1, keepdims=True), forward.shape)
    to_scalar = [
        pltpu.make_async_copy(forward_vec, forward_idx, local_sem.at[0]),
        pltpu.make_async_copy(back_vec, back_idx, local_sem.at[1]),
    ]
    for c in to_scalar:
        c.start()
    for c in to_scalar:
        c.wait()

    def picked(r):
        return jnp.clip(forward_idx[r, 0], 0, SLOTS * A_SIZE)

    def back_of(o, s):
        return jnp.clip(back_idx[o, s], 0, 2 * B_SIZE)

    place_copy.wait()
    packed_scaled[0] = pack(scaled_own[0], 0)
    packed_scaled[1] = pack(scaled_own[1], 96)
    send_halo(scaled_own, packed_scaled, vert_scaled, side_scaled, h_send, h_recv)

    for q in range(CHUNKS):
        arrived(cand[q].at[pl.ds(1 + SLOTS, SLOTS * (A_SIZE - 1))], a_send.at[q], a_recv.at[q])
        for p in b_order + [0]:
            for h in range(2):
                spread[q, p, h] = cand[q][picked(2 * p + h)]
            if p > 0:
                copy(spread.at[q, p], gathered.at[q, p], b_send.at[q], b_recv.at[q], b_peer(p, 1)).start()

    small[4].wait()
    loads[CHUNKS].wait()
    units(0, 6)
    halo_arrived(vert_scaled, side_scaled, h_send, h_recv)
    scaled_ext[...] = extended(scaled_own, vert_scaled, side_scaled)
    all_scaled = scaled_ext[...]
    tall = all_scaled.shape[0]
    east_w[...] = jnp.sqrt(all_scaled * lane_roll(all_scaled, -1))
    north_w[...] = jnp.sqrt(all_scaled * pltpu.roll(all_scaled, tall - 1, 0))
    east, north = east_w[...], north_w[...]
    diagonal[...] = surface_shift + ((east + lane_roll(east, 1)) + (north + pltpu.roll(north, 1, 0)))

    for q in range(CHUNKS):
        arrived(gathered.at[q, pl.ds(1, B_SIZE - 1)], b_send.at[q], b_recv.at[q])
        rows = slice(q * CH, (q + 1) * CH)
        for h in range(2):
            total = spread[q, 0, h]
            for p in range(1, B_SIZE):
                total = total + gathered[q, p, h]
            source_own[h, rows, :] = jnp.where(scaled_own[h, rows, :] > 0.0, total, 0.0)

    packed_source[0] = pack(source_own[0], 0)
    packed_source[1] = pack(source_own[1], 96)
    send_halo(source_own, packed_source, vert_source, side_source, g_send, g_recv)
    halo_arrived(vert_source, side_source, g_send, g_recv)
    start = extended(source_own, vert_source, side_source)
    centre, table = chebyshev_table(STEPS)
    residual[...] = start
    direction[...] = start / centre
    core = slice(BY - 8, 2 * BY + 8)
    height[...] = jnp.zeros(height.shape, jnp.float32)

    def group(step, count, phase):
        band = slice(8 * phase, tall - 8 * phase)
        rows = tall - 16 * phase
        inner = slice(BY - 8 - 8 * phase, BY - 8 - 8 * phase + BY + 16)
        now, left, total = direction[band, :], residual[band, :], height[...]
        for i in range(count):
            total = total + now[inner, :]
            east, north = east_w[band, :], north_w[band, :]
            image = diagonal[band, :] * now
            image = image - (east * lane_roll(now, -1) + lane_roll(east * now, 1))
            image = image - (north * pltpu.roll(now, rows - 1, 0) + pltpu.roll(north * now, 1, 0))
            left = left - image
            carry, push = table[step + i]
            now = carry * now + push * left
        direction[band, :], residual[band, :], height[...] = now, left, total

    for phase in range(3):
        group(8 * phase, 8, phase)
    group(24, 7, 3)
    height[...] = height[...] + direction[core, :]

    def own_blocks(values):
        a, b, c = (lane_roll(values[:, k * BX : (k + 1) * BX], 64) for k in range(3))
        low = lax.broadcasted_iota(jnp.int32, a.shape, 1) < 64
        return jnp.where(low, a, b), jnp.where(low, b, c)

    mid = height[8 : BY + 8, :]
    own_heights = own_blocks(mid)
    next_rows = own_blocks(height[BY + 8 : BY + 16, :])
    pair = jnp.zeros((8, BX), jnp.float32)
    for h in range(2):
        tile = mid[:, (h + 1) * BX : (h + 2) * BX]
        column = jnp.sum(jnp.where(lane32 == 64, tile, 0.0), axis=1, keepdims=True)
        flat = jnp.sum(jnp.where(row32 == lane32, column, 0.0), axis=0, keepdims=True)
        next_row = next_rows[h] if h == 0 else pltpu.roll(next_rows[h], 2 * h, 0)
        pair = jnp.where(row8 == 2 * h, next_row, jnp.where(row8 == 2 * h + 1, flat, pair))
        for q in range(CHUNKS):
            returned[q][1 + h] = own_heights[h][q * CH : (q + 1) * CH, :]
    edge_pairs[0] = pair

    for p in b_order:
        copy(edge_pairs.at[0], edge_pairs.at[p], rb_send.at[CHUNKS], rb_recv.at[CHUNKS], b_peer(p, -1)).start()
    for q in range(CHUNKS):
        for p in b_order:
            copy(
                returned[q].at[pl.ds(1, 2)],
                returned[q].at[pl.ds(1 + 2 * p, 2)],
                rb_send.at[q],
                rb_recv.at[q],
                b_peer(p, -1),
            ).start()

    east_step = lane_roll(mid, -1) - mid
    north_step = height[9 : BY + 9, :] - mid
    south_step = mid - height[7 : BY + 7, :]
    east_energy = east_w[BY : 2 * BY, :] * east_step * east_step
    total = (
        east_energy
        + lane_roll(east_energy, 1)
        + north_w[BY : 2 * BY, :] * north_step * north_step
        + north_w[BY - 1 : 2 * BY - 1, :] * south_step * south_step
    )
    sens = 0.25 * total / jnp.maximum(scaled_ext[BY : 2 * BY, :], 0.25)
    for h, (sens_part, height_part) in enumerate(zip(own_blocks(sens), own_heights)):
        result_out[0, :, h * BX : (h + 1) * BX] = height_part
        result_out[1, :, h * BX : (h + 1) * BX] = sens_part

    units(6, 8)
    arrived(edge_pairs.at[pl.ds(1, B_SIZE - 1)], rb_send.at[CHUNKS], rb_recv.at[CHUNKS])
    for p in range(B_SIZE):
        both = edge_pairs[p]
        edges[1 + 2 * p] = jnp.where(row8 < 2, both, 0.0)
        edges[2 + 2 * p] = jnp.where(row8 < 2, pltpu.roll(both, 6, 0), 0.0)
    for o in a_order + [0]:
        tile = edges[back_of(o, 0)]
        for s in range(1, SLOTS):
            tile = tile + pltpu.roll(edges[back_of(o, s)], 2 * s, 0)
        edge_out[o] = tile
        if o > 0:
            copy(edge_out.at[o], edge_in.at[o], ra_send.at[CHUNKS], ra_recv.at[CHUNKS], a_peer(o, -1)).start()
    for q in range(CHUNKS):
        arrived(returned[q].at[pl.ds(3, 2 * (B_SIZE - 1))], rb_send.at[q], rb_recv.at[q])
        for o in a_order + [0]:
            for s in range(SLOTS):
                slot_out[q, o, s] = returned[q][back_of(o, s)]
            if o > 0:
                copy(slot_out.at[q, o], slot_in.at[q, o], ra_send.at[q], ra_recv.at[q], a_peer(o, -1)).start()
    result_copy = copy(result_out, result_in, place_send.at[1], place_recv.at[1], (lon, lat))
    result_copy.start()
    arrived(edge_in.at[pl.ds(1, A_SIZE - 1)], ra_send.at[CHUNKS], ra_recv.at[CHUNKS])
    edge = edge_out[0]
    for o in range(1, A_SIZE):
        edge = edge + edge_in[o]
    for s in range(SLOTS):
        slot_sum[s, BY : BY + 8, :] = edge if s == 0 else pltpu.roll(edge, 8 - 2 * s, 0)
    for q in range(CHUNKS):
        arrived(slot_in.at[q, pl.ds(1, A_SIZE - 1)], ra_send.at[q], ra_recv.at[q])
        for s in range(SLOTS):
            total = slot_out[q, 0, s]
            for o in range(1, A_SIZE):
                total = total + slot_in[q, o, s]
            slot_sum[s, q * CH : (q + 1) * CH, :] = total
    result_copy.wait()
    surface_ref[...] = result_in[0]
    sens_ref[...] = result_in[1]
    for s in range(SLOTS):
        here = slot_sum[s, 0:BY, :]
        flat = jnp.broadcast_to(slot_sum[s, BY + 1 : BY + 2, :], (BY, BX))
        column = jnp.sum(jnp.where(row32 == lane32, flat, 0.0), axis=1, keepdims=True)
        beside = jnp.where(lane32 == BX - 1, column, lane_roll(here, -1))
        press_ref[s, 0] = pressure_gain * (beside - here)
        press_ref[s, 1] = pressure_gain * (slot_sum[s, 1 : BY + 1, :] - here)


def main_call(block_ids, level_count, drag_coef, bathymetry, land_mask, adjoint_vel, velocity):
    f32, i32 = jnp.float32, jnp.int32
    wide = (3 * BY, 3 * BX)
    dma = pltpu.SemaphoreType.DMA
    vmem = pl.BlockSpec(memory_space=pltpu.VMEM)
    hbm = pl.BlockSpec(memory_space=pltpu.HBM)
    return pl.pallas_call(
        main_kernel,
        out_shape=(
            pltpu.VMEM((SLOTS, 2, LEV, BY, BX), f32),
            pltpu.VMEM((SLOTS, 2, BY, BX), f32),
            pltpu.VMEM((SLOTS, 2, BY, BX), f32),
            pltpu.VMEM((SLOTS, BY, BX), f32),
            pltpu.VMEM((BY, 2 * BX), f32),
            pltpu.VMEM((BY, 2 * BX), f32),
        ),
        in_specs=[hbm] * 7,
        out_specs=(vmem,) * 6,
        scratch_shapes=[
            pltpu.VMEM((SLOTS, BY, BX), i32),
            pltpu.VMEM((SLOTS, 2, LEV, BY, BX), jnp.bfloat16),
            pltpu.SMEM((SLOTS,), i32),
            pltpu.VMEM((SLOTS, BY, BX), i32),
            pltpu.VMEM((SLOTS, BY, BX), f32),
            pltpu.VMEM((BY, 2 * BX), f32),
            pltpu.VMEM((BY, 2 * BX), i32),
            pltpu.VMEM((A_SIZE, 8, BX), i32),
            pltpu.VMEM((2 * B_SIZE, BX), i32),
            pltpu.VMEM((A_SIZE, BX), i32),
            pltpu.SMEM((2 * B_SIZE, BX), i32),
            pltpu.SMEM((A_SIZE, BX), i32),
            [pltpu.VMEM((1 + SLOTS * A_SIZE, CH, BX), f32) for _ in range(CHUNKS)],
            pltpu.VMEM((CHUNKS, B_SIZE, 2, CH, BX), f32),
            pltpu.VMEM((CHUNKS, B_SIZE, 2, CH, BX), f32),
            pltpu.VMEM((2, BY, BX), f32),
            pltpu.VMEM((2, BY, BX), f32),
            pltpu.VMEM((2, BY, BX), f32),
            pltpu.VMEM((2, BY, 2 * BX), f32),
            pltpu.VMEM((2, BY, 2 * BX), f32),
            pltpu.VMEM((2, 8, BX), f32),
            pltpu.VMEM((2, 8, BX), f32),
            pltpu.VMEM((2, 2, BY, BX), f32),
            pltpu.VMEM((2, 2, BY, BX), f32),
            pltpu.VMEM((len(SIDES), 8, BX), f32),
            pltpu.VMEM((len(SIDES), 8, BX), f32),
            pltpu.VMEM(wide, f32),
            pltpu.VMEM(wide, f32),
            pltpu.VMEM(wide, f32),
            pltpu.VMEM(wide, f32),
            pltpu.VMEM(wide, f32),
            pltpu.VMEM((BY + 16, 3 * BX), f32),
            pltpu.VMEM(wide, f32),
            [pltpu.VMEM((1 + 2 * B_SIZE, CH, BX), f32) for _ in range(CHUNKS)],
            pltpu.VMEM((B_SIZE, 8, BX), f32),
            pltpu.VMEM((1 + 2 * B_SIZE, 8, BX), f32),
            pltpu.VMEM((CHUNKS, A_SIZE, SLOTS, CH, BX), f32),
            pltpu.VMEM((CHUNKS, A_SIZE, SLOTS, CH, BX), f32),
            pltpu.VMEM((A_SIZE, 8, BX), f32),
            pltpu.VMEM((A_SIZE, 8, BX), f32),
            pltpu.VMEM((SLOTS, BY + 8, BX), f32),
            dma((CHUNKS + 1,)),
            dma((1,)),
            dma((1,)),
            dma((CHUNKS,)),
            dma((CHUNKS,)),
            dma((CHUNKS,)),
            dma((CHUNKS,)),
            dma((2,)),
            dma((2,)),
            dma((2,)),
            dma((2,)),
            dma((CHUNKS + 1,)),
            dma((CHUNKS + 1,)),
            dma((CHUNKS + 1,)),
            dma((CHUNKS + 1,)),
            dma((2,)),
            dma((2,)),
            dma((2,)),
            dma((5,)),
        ],
        compiler_params=pltpu.CompilerParams(
            collective_id=0, has_side_effects=True, vmem_limit_bytes=50 * 2**20
        ),
        name="columns_and_surface",
    )(block_ids, level_count, drag_coef, bathymetry, land_mask, adjoint_vel, velocity)


def final_kernel(
    count_ref, mixed_ref, press_ref, pull_ref, drag_ref, surface_ref, sens_ref,
    out_hbm, drag_out_ref, surface_out_ref, sens_out_ref, stage, sems, small_sems,
):
    small = ((drag_ref, drag_out_ref), (surface_ref, surface_out_ref), (sens_ref, sens_out_ref))
    puts = [pltpu.make_async_copy(src, dst, small_sems.at[i]) for i, (src, dst) in enumerate(small)]
    for c in puts:
        c.start()
    for slot in range(SLOTS):
        levels = count_ref[slot]
        for c in range(2):
            press = press_ref[slot, c]
            bed = press + pull_ref[slot, c]
            for piece in range(PIECES):
                for k in range(piece * LEV // PIECES, (piece + 1) * LEV // PIECES):
                    less = jnp.where(levels == k + 1, bed, jnp.where(levels > k, press, 0.0))
                    stage[slot, c, k] = mixed_ref[slot, c, k] - less
                part = (slot, c, pl.ds(piece * LEV // PIECES, LEV // PIECES))
                puts.append(pltpu.make_async_copy(stage.at[part], out_hbm.at[part], sems.at[len(puts) - len(small)]))
                puts[-1].start()
    for c in puts:
        c.wait()


def final_call(level_count, mixed, press, pull, drag_grad, surface, sens):
    f32 = jnp.float32
    vmem = pl.BlockSpec(memory_space=pltpu.VMEM)
    deep = (SLOTS, 2, LEV, BY, BX)
    return pl.pallas_call(
        final_kernel,
        out_shape=(
            jax.ShapeDtypeStruct(deep, f32),
            jax.ShapeDtypeStruct(drag_grad.shape, f32),
            jax.ShapeDtypeStruct(surface.shape, f32),
            jax.ShapeDtypeStruct(sens.shape, f32),
        ),
        in_specs=[vmem] * 7,
        out_specs=(pl.BlockSpec(memory_space=pltpu.HBM),) * 4,
        scratch_shapes=[pltpu.VMEM(deep, f32), pltpu.SemaphoreType.DMA((SLOTS * 2 * PIECES,)), pltpu.SemaphoreType.DMA((3,))],
        compiler_params=pltpu.CompilerParams(vmem_limit_bytes=24 * 2**20),
        name="pressure_correction",
    )(level_count, mixed, press, pull, drag_grad, surface, sens)


def per_device(adjoint_vel, velocity, drag_coef, level_count, block_ids, bathymetry, land_mask):
    mixed, press, pull, drag_grad, surface, sens = main_call(
        block_ids, level_count, drag_coef, bathymetry, land_mask, adjoint_vel, velocity
    )
    return final_call(level_count, mixed, press, pull, drag_grad, surface, sens)


def solution(mesh):
    slots = P(("gx", "gy"), None, None, None, None)
    flat = P(("gx", "gy"), None, None)
    return jax.shard_map(
        per_device,
        mesh=mesh,
        in_specs=(slots, slots, flat, flat, P(("gx", "gy")), P("gy", "gx"), P("gy", "gx")),
        out_specs=(slots, flat, P("gy", "gx"), P("gy", "gx")),
        check_vma=False,
    )
```

```python
import jax
import jax.numpy as jnp
from jax import lax
from jax.experimental import pallas as pl
from jax.experimental.pallas import tpu as pltpu
from jax.sharding import PartitionSpec as P

MESH = pl.DeviceIdType.MESH
STEPS = 32
LEV = 62
BY = 32
BX = 128
SLOTS = 4
CHUNKS = 4
CH = BY // CHUNKS
NX_CHIPS, NY_CHIPS, NZ_CHIPS, CORES = 4, 4, 4, 2
A_SIZE = NX_CHIPS * CORES
B_SIZE = NY_CHIPS * NZ_CHIPS
AROUND = ((-1, -1), (-1, 0), (-1, 1), (0, -1), (0, 1), (1, -1), (1, 0), (1, 1))
SIDES = tuple(d for d in AROUND if d[0] != 0)
UNIT = 16
UNITS = SLOTS * BY // UNIT
PIECES = 2

mix_rate = 0.25
drag_step = 0.5
force_scale = 0.25
pressure_gain = 0.5
surface_shift = 1.0 / 64.0
speed_floor = 0.01


def chebyshev_table(total_steps):
    highest = surface_shift + 8.0
    centre = 0.5 * (highest + surface_shift)
    radius = 0.5 * (highest - surface_shift)
    sigma_ratio = centre / radius
    ratio_prev = 1.0 / sigma_ratio
    table = []
    for _ in range(total_steps):
        ratio_next = 1.0 / (2.0 * sigma_ratio - ratio_prev)
        table.append((ratio_next * ratio_prev, 2.0 * ratio_next / radius))
        ratio_prev = ratio_next
    return (centre, table)


def lane_roll(values, shift):
    return pltpu.roll(values, shift % values.shape[-1], values.ndim - 1)


def mix_unit(unit, levels_ref, drag_ref, mixed_ref, velocity_ref, pull_ref, drag_out_ref):
    slot = lax.div(unit, BY // UNIT)
    rows = pl.ds(pl.multiple_of(lax.rem(unit, BY // UNIT) * UNIT, UNIT), UNIT)
    levels = levels_ref[slot, rows, :]
    zero = jnp.zeros((UNIT, BX), jnp.float32)

    def level(k, state, first_level=False):
        above0, flux0, above1, flux1, flow_b, column_b, rate = state
        last = k >= LEV - 1
        wet_next = levels > k + 1
        rate_next = jnp.where(wet_next, mix_rate, 0.0)
        bottom = levels == k
        out = [[], [], [], [], [], []]
        for c in range(2):
            if last:
                below = down = zero
                first = above0[c] - flux0[c]
            else:
                below = jnp.where(wet_next, mixed_ref[slot, c, k + 1, rows, :], 0.0)
                down = (below - above0[c]) * rate_next
                first = above0[c] + down - flux0[c]
            if first_level:
                down1, flow, col = zero, flow_b[c], column_b[c]
            else:
                down1 = zero if k == LEV else (first - above1[c]) * rate
                second = above1[c] + down1 - flux1[c]
                mixed_ref[slot, c, k - 1, rows, :] = second
                col = jnp.where(bottom, second, column_b[c])
                flow = jnp.where(bottom, velocity_ref[slot, c, k - 1, rows, :].astype(jnp.float32), flow_b[c])
            for pile, value in zip(out, (below, down, first, down1, flow, col)):
                pile.append(value)
        return (*(tuple(pile) for pile in out), rate_next)

    wet_top = levels > 0
    top = tuple(jnp.where(wet_top, mixed_ref[slot, c, 0, rows, :], 0.0) for c in range(2))
    both = (zero, zero)
    state = level(0, (top, both, both, both, both, both, zero), first_level=True)
    for k in range(1, LEV + 1):
        state = level(k, state)
    flow_b, column_b = state[4], state[5]
    speed = jnp.sqrt(flow_b[0] * flow_b[0] + flow_b[1] * flow_b[1] + speed_floor)
    along = flow_b[0] * column_b[0] + flow_b[1] * column_b[1]
    ratio = along / speed
    drag = drag_ref[slot, rows, :]
    drag_out_ref[slot, rows, :] = -drag_step * speed * along
    for c in range(2):
        pull_ref[slot, c, rows, :] = drag_step * (drag * (speed * column_b[c] + flow_b[c] * ratio))


def main_kernel(
    ids_hbm,
    count_hbm,
    drag_hbm,
    bathymetry_hbm,
    mask_hbm,
    adjoint_hbm,
    velocity_hbm,
    mixed_ref,
    press_ref,
    pull_ref,
    drag_out_ref,
    surface_ref,
    sens_ref,
    levels_ref,
    velocity_ref,
    ids_ref,
    count_ref,
    drag_ref,
    bathymetry_ref,
    mask_ref,
    idbuf,
    forward_vec,
    back_vec,
    forward_idx,
    back_idx,
    cand,
    spread,
    gathered,
    source_own,
    scaled_out,
    scaled_own,
    result_out,
    result_in,
    packed_scaled,
    packed_source,
    vert_scaled,
    vert_source,
    side_scaled,
    side_source,
    east_w,
    north_w,
    scaled_ext,
    direction,
    residual,
    height,
    diagonal,
    returned,
    edge_pairs,
    edges,
    slot_out,
    slot_in,
    edge_out,
    edge_in,
    slot_sum,
    load_sem,
    id_send,
    id_recv,
    a_send,
    a_recv,
    b_send,
    b_recv,
    h_send,
    h_recv,
    g_send,
    g_recv,
    rb_send,
    rb_recv,
    ra_send,
    ra_recv,
    place_send,
    place_recv,
    local_sem,
    small_sem,
):
    gx = lax.axis_index("gx")
    gy = lax.axis_index("gy")
    my_x, my_zh = lax.div(gx, 2), lax.rem(gx, 2)
    my_y, my_zl, my_c = lax.div(gy, 4), lax.rem(lax.div(gy, 2), 2), lax.rem(gy, 2)
    my_z = my_zh * 2 + my_zl

    def a_peer(o, sign):
        step_x, step_c = o // 2, o % 2
        if sign < 0:
            step_x = (NX_CHIPS - step_x) % NX_CHIPS
        x = lax.rem(my_x + step_x, NX_CHIPS)
        c = lax.rem(my_c + step_c, CORES)
        return (x * 2 + my_zh, my_y * 4 + my_zl * 2 + c)

    def b_peer(p, sign):
        step_y, step_z = p // NZ_CHIPS, p % NZ_CHIPS
        if sign < 0:
            step_y = (NY_CHIPS - step_y) % NY_CHIPS
            step_z = (NZ_CHIPS - step_z) % NZ_CHIPS
        y = lax.rem(my_y + step_y, NY_CHIPS)
        z = lax.rem(my_z + step_z, NZ_CHIPS)
        return (my_x * 2 + lax.div(z, 2), y * 4 + lax.rem(z, 2) * 2 + my_c)

    def snake(y_grid, z):
        return z + lax.rem(y_grid, 2) * (NZ_CHIPS - 1 - 2 * z)

    def solver_of(lon, lat):
        y_grid = lax.div(lat, NZ_CHIPS)
        z = snake(y_grid, lax.rem(lat, NZ_CHIPS))
        y = lax.rem(y_grid + NY_CHIPS - 1, NY_CHIPS)
        return (lax.div(lon, 2) * 2 + lax.div(z, 2), y * 4 + lax.rem(z, 2) * 2 + lax.rem(lon, 2))

    lon = my_x * 2 + my_c
    my_y_grid = lax.rem(my_y + 1, NY_CHIPS)
    lat = my_y_grid * NZ_CHIPS + snake(my_y_grid, my_z)

    def near(n):
        dx, dy = AROUND[n]
        return solver_of(lax.rem(lon + dx + 8, 8), lax.rem(lat + dy + 16, 16))

    def copy(src, dst, send, recv, to):
        return pltpu.make_async_remote_copy(
            src_ref=src, dst_ref=dst, send_sem=send, recv_sem=recv, device_id=to, device_id_type=MESH
        )

    def arrived(whole, send, recv):
        copy(whole, whole, send, recv, (gx, gy)).wait()

    a_order = sorted(range(1, A_SIZE), key=lambda o: -min(o // 2, NX_CHIPS - o // 2))
    b_order = sorted(
        range(1, B_SIZE),
        key=lambda p: -min(p // NZ_CHIPS, NY_CHIPS - p // NZ_CHIPS) - min(p % NZ_CHIPS, NZ_CHIPS - p % NZ_CHIPS),
    )

    loads = []
    for q in range(CHUNKS):
        part = (slice(None), slice(None), slice(None), pl.ds(q * CH, CH))
        loads.append(pltpu.make_async_copy(adjoint_hbm.at[part], mixed_ref.at[part], load_sem.at[q]))
    loads.append(pltpu.make_async_copy(velocity_hbm, velocity_ref, load_sem.at[CHUNKS]))
    pairs = (
        (ids_hbm, ids_ref),
        (count_hbm, count_ref),
        (bathymetry_hbm, bathymetry_ref),
        (mask_hbm, mask_ref),
        (drag_hbm, drag_ref),
    )
    small = [pltpu.make_async_copy(src, dst, small_sem.at[i]) for i, (src, dst) in enumerate(pairs)]
    small[0].start()
    small[1].start()
    loads[0].start()

    barrier = pltpu.get_barrier_semaphore()
    for p in b_order:
        pl.semaphore_signal(barrier, inc=1, device_id=b_peer(p, 1), device_id_type=MESH)
    for o in a_order:
        pl.semaphore_signal(barrier, inc=1, device_id=a_peer(o, 1), device_id_type=MESH)
    for n in range(8):
        pl.semaphore_signal(barrier, inc=1, device_id=near(n), device_id_type=MESH)
    pl.semaphore_signal(barrier, inc=1, device_id=solver_of(gx, gy), device_id_type=MESH)
    pl.semaphore_signal(barrier, inc=1, device_id=(lon, lat), device_id_type=MESH)

    for c in small[2:]:
        c.start()
    loads[1].start()

    lane8 = lax.broadcasted_iota(jnp.int32, (8, BX), 1)
    lane32 = lax.broadcasted_iota(jnp.int32, (BY, BX), 1)
    row8 = lax.broadcasted_iota(jnp.int32, (8, BX), 0)
    row32 = lax.broadcasted_iota(jnp.int32, (BY, BX), 0)

    small[0].wait()
    small[1].wait()
    id_row = jnp.full((8, BX), -1, jnp.int32)
    for s in range(SLOTS):
        id_row = jnp.where(lane8 == s, ids_ref[s], id_row)
        levels_ref[s] = count_ref[s] * jnp.where(ids_ref[s] < 256, 1, 0)
    idbuf[0] = id_row
    for q in range(CHUNKS):
        cand[q][0] = jnp.zeros((CH, BX), jnp.float32)
        returned[q][0] = jnp.zeros((CH, BX), jnp.float32)
    edges[0] = jnp.zeros((8, BX), jnp.float32)

    def pack(block, base):
        out = jnp.zeros((8, BX), jnp.float32)
        for q in range(4):
            part = lane_roll(block[8 * q : 8 * q + 8, :], 32 * q - base)
            out = jnp.where(lane8 // 32 == q, part, out)
        return out

    def unpack(packed, base):
        return jnp.concatenate([lane_roll(packed, base - 32 * q) for q in range(4)], axis=0)

    small[2].wait()
    small[3].wait()
    scaled = bathymetry_ref[...] * mask_ref[...].astype(jnp.float32)
    scaled_out[0] = scaled[:, :BX]
    scaled_out[1] = scaled[:, BX:]

    def force(q):
        rows = slice(q * CH, (q + 1) * CH)

        def one(s, carry):
            levels = levels_ref[s, rows, :]
            totals = [jnp.zeros((CH, BX), jnp.float32)] * 4
            for k in range(LEV):
                pair = mixed_ref[s, 0, k, rows, :] + mixed_ref[s, 1, k, rows, :]
                totals[k % 4] = totals[k % 4] + jnp.where(levels > k, pair, 0.0)
            cand[q][1 + s] = force_scale * ((totals[0] + totals[1]) + (totals[2] + totals[3]))
            return carry

        lax.fori_loop(0, SLOTS, one, 0)

    loads[0].wait()
    loads[2].start()
    force(0)
    pl.semaphore_wait(barrier, A_SIZE - 1 + B_SIZE - 1 + 8 + 2)

    for o in a_order:
        copy(idbuf.at[0], idbuf.at[o], id_send.at[0], id_recv.at[0], a_peer(o, 1)).start()

    place_copy = copy(scaled_out, scaled_own, place_send.at[0], place_recv.at[0], solver_of(gx, gy))
    place_copy.start()
    def send_a(q):
        for o in a_order:
            copy(
                cand[q].at[pl.ds(1, SLOTS)],
                cand[q].at[pl.ds(1 + SLOTS * o, SLOTS)],
                a_send.at[q],
                a_recv.at[q],
                a_peer(o, 1),
            ).start()

    send_a(0)

    def send_halo(own, packed, vert, side, send, recv):
        for n, (dx, dy) in enumerate(AROUND):
            if dx != 0:
                copy(packed.at[0 if dx < 0 else 1], side.at[SIDES.index((dx, dy))], send.at[1], recv.at[1], near(n)).start()
        for n, (dx, dy) in enumerate(AROUND):
            if dx == 0:
                copy(own, vert.at[0 if dy < 0 else 1], send.at[0], recv.at[0], near(n)).start()

    def halo_arrived(vert, side, send, recv):
        arrived(vert, send.at[0], recv.at[0])
        arrived(side, send.at[1], recv.at[1])

    def extended(own, vert, side):
        bands = []
        for dy in (-1, 0, 1):
            if dy == 0:
                left, right = own[0], own[1]
                inside = jnp.float32(1.0)
            else:
                k = 0 if dy > 0 else 1
                left, right = vert[k, 0], vert[k, 1]
                inside = jnp.where(lat + dy >= 0, 1.0, 0.0) * jnp.where(lat + dy < 16, 1.0, 0.0)
            west = unpack(side[SIDES.index((1, -dy))], 32) * jnp.where(lon > 0, 1.0, 0.0)
            east = unpack(side[SIDES.index((-1, -dy))], 64) * jnp.where(lon < 7, 1.0, 0.0)
            left, right = lane_roll(left, 64), lane_roll(right, 64)
            first = jnp.where(lane32 < 32, 0.0, jnp.where(lane32 < 64, west, left))
            middle = jnp.where(lane32 < 64, left, right)
            last = jnp.where(lane32 < 64, right, jnp.where(lane32 < 96, east, 0.0))
            bands.append(jnp.concatenate([first, middle, last], axis=1) * inside)
        return jnp.concatenate(bands, axis=0)

    def units(first, last):
        def one(unit, carry):
            mix_unit(unit, levels_ref, drag_ref, mixed_ref, velocity_ref, pull_ref, drag_out_ref)
            return carry

        lax.fori_loop(first, last, one, 0)

    for q in range(1, CHUNKS):
        loads[q].wait()
        if q + 2 <= CHUNKS:
            loads[q + 2].start()
        force(q)
        send_a(q)

    arrived(idbuf.at[pl.ds(1, A_SIZE - 1)], id_send.at[0], id_recv.at[0])
    spot = lax.broadcasted_iota(jnp.int32, (2 * B_SIZE, BX), 0)
    spot_lane = lax.broadcasted_iota(jnp.int32, (2 * B_SIZE, BX), 1)
    spot_p = spot // 2
    spot_y = (my_y + spot_p // NZ_CHIPS + 1) % NY_CHIPS
    spot_z = (my_z + spot_p % NZ_CHIPS) % NZ_CHIPS
    owner = lon * 16 + spot_y * NZ_CHIPS + spot_z + (spot_y % 2) * (NZ_CHIPS - 1 - 2 * spot_z)
    target = owner * 2 + spot % 2
    forward = jnp.zeros((2 * B_SIZE, BX), jnp.int32)
    for o in range(A_SIZE):
        ids = jnp.broadcast_to(idbuf[o, 0:1, :], (2 * B_SIZE, BX))
        hit = ids == target
        forward = forward + jnp.where(hit, spot_lane + (1 + SLOTS * o), 0)
        back = jnp.sum(jnp.where(hit, spot + 1, 0), axis=0, keepdims=True)
        back_vec[o : o + 1, :] = back
    forward_vec[...] = jnp.broadcast_to(jnp.sum(forward, axis=1, keepdims=True), forward.shape)
    to_scalar = [
        pltpu.make_async_copy(forward_vec, forward_idx, local_sem.at[0]),
        pltpu.make_async_copy(back_vec, back_idx, local_sem.at[1]),
    ]
    for c in to_scalar:
        c.start()
    for c in to_scalar:
        c.wait()

    def picked(r):
        return jnp.clip(forward_idx[r, 0], 0, SLOTS * A_SIZE)

    def back_of(o, s):
        return jnp.clip(back_idx[o, s], 0, 2 * B_SIZE)

    place_copy.wait()
    packed_scaled[0] = pack(scaled_own[0], 0)
    packed_scaled[1] = pack(scaled_own[1], 96)
    send_halo(scaled_own, packed_scaled, vert_scaled, side_scaled, h_send, h_recv)

    for q in range(CHUNKS):
        arrived(cand[q].at[pl.ds(1 + SLOTS, SLOTS * (A_SIZE - 1))], a_send.at[q], a_recv.at[q])
        for p in b_order + [0]:
            for h in range(2):
                spread[q, p, h] = cand[q][picked(2 * p + h)]
            if p > 0:
                copy(spread.at[q, p], gathered.at[q, p], b_send.at[q], b_recv.at[q], b_peer(p, 1)).start()

    small[4].wait()
    loads[CHUNKS].wait()
    units(0, 6)
    halo_arrived(vert_scaled, side_scaled, h_send, h_recv)
    scaled_ext[...] = extended(scaled_own, vert_scaled, side_scaled)
    all_scaled = scaled_ext[...]
    tall = all_scaled.shape[0]
    east_w[...] = jnp.sqrt(all_scaled * lane_roll(all_scaled, -1))
    north_w[...] = jnp.sqrt(all_scaled * pltpu.roll(all_scaled, tall - 1, 0))
    east, north = east_w[...], north_w[...]
    diagonal[...] = surface_shift + ((east + lane_roll(east, 1)) + (north + pltpu.roll(north, 1, 0)))

    for q in range(CHUNKS):
        arrived(gathered.at[q, pl.ds(1, B_SIZE - 1)], b_send.at[q], b_recv.at[q])
        rows = slice(q * CH, (q + 1) * CH)
        for h in range(2):
            total = spread[q, 0, h]
            for p in range(1, B_SIZE):
                total = total + gathered[q, p, h]
            source_own[h, rows, :] = jnp.where(scaled_own[h, rows, :] > 0.0, total, 0.0)

    packed_source[0] = pack(source_own[0], 0)
    packed_source[1] = pack(source_own[1], 96)
    send_halo(source_own, packed_source, vert_source, side_source, g_send, g_recv)
    halo_arrived(vert_source, side_source, g_send, g_recv)
    start = extended(source_own, vert_source, side_source)
    centre, table = chebyshev_table(STEPS)
    residual[...] = start
    direction[...] = start / centre
    core = slice(BY - 8, 2 * BY + 8)
    height[...] = jnp.zeros(height.shape, jnp.float32)

    def group(step, count, phase):
        band = slice(8 * phase, tall - 8 * phase)
        rows = tall - 16 * phase
        inner = slice(BY - 8 - 8 * phase, BY - 8 - 8 * phase + BY + 16)
        now, left, total = direction[band, :], residual[band, :], height[...]
        for i in range(count):
            total = total + now[inner, :]
            east, north = east_w[band, :], north_w[band, :]
            image = diagonal[band, :] * now
            image = image - (east * lane_roll(now, -1) + lane_roll(east * now, 1))
            image = image - (north * pltpu.roll(now, rows - 1, 0) + pltpu.roll(north * now, 1, 0))
            left = left - image
            carry, push = table[step + i]
            now = carry * now + push * left
        direction[band, :], residual[band, :], height[...] = now, left, total

    for phase in range(3):
        group(8 * phase, 8, phase)
    group(24, 7, 3)
    height[...] = height[...] + direction[core, :]

    def own_blocks(values):
        a, b, c = (lane_roll(values[:, k * BX : (k + 1) * BX], 64) for k in range(3))
        low = lax.broadcasted_iota(jnp.int32, a.shape, 1) < 64
        return jnp.where(low, a, b), jnp.where(low, b, c)

    mid = height[8 : BY + 8, :]
    own_heights = own_blocks(mid)
    next_rows = own_blocks(height[BY + 8 : BY + 16, :])
    pair = jnp.zeros((8, BX), jnp.float32)
    for h in range(2):
        tile = mid[:, (h + 1) * BX : (h + 2) * BX]
        column = jnp.sum(jnp.where(lane32 == 64, tile, 0.0), axis=1, keepdims=True)
        flat = jnp.sum(jnp.where(row32 == lane32, column, 0.0), axis=0, keepdims=True)
        next_row = next_rows[h] if h == 0 else pltpu.roll(next_rows[h], 2 * h, 0)
        pair = jnp.where(row8 == 2 * h, next_row, jnp.where(row8 == 2 * h + 1, flat, pair))
        for q in range(CHUNKS):
            returned[q][1 + h] = own_heights[h][q * CH : (q + 1) * CH, :]
    edge_pairs[0] = pair[0:4, :]

    for p in b_order:
        copy(edge_pairs.at[0], edge_pairs.at[p], rb_send.at[CHUNKS], rb_recv.at[CHUNKS], b_peer(p, -1)).start()
    for q in range(CHUNKS):
        for p in b_order:
            copy(
                returned[q].at[pl.ds(1, 2)],
                returned[q].at[pl.ds(1 + 2 * p, 2)],
                rb_send.at[q],
                rb_recv.at[q],
                b_peer(p, -1),
            ).start()

    east_step = lane_roll(mid, -1) - mid
    north_step = height[9 : BY + 9, :] - mid
    south_step = mid - height[7 : BY + 7, :]
    east_energy = east_w[BY : 2 * BY, :] * east_step * east_step
    total = (
        east_energy
        + lane_roll(east_energy, 1)
        + north_w[BY : 2 * BY, :] * north_step * north_step
        + north_w[BY - 1 : 2 * BY - 1, :] * south_step * south_step
    )
    sens = 0.25 * total / jnp.maximum(scaled_ext[BY : 2 * BY, :], 0.25)
    for h, (sens_part, height_part) in enumerate(zip(own_blocks(sens), own_heights)):
        result_out[0, :, h * BX : (h + 1) * BX] = height_part
        result_out[1, :, h * BX : (h + 1) * BX] = sens_part

    units(6, 8)
    arrived(edge_pairs.at[pl.ds(1, B_SIZE - 1)], rb_send.at[CHUNKS], rb_recv.at[CHUNKS])
    for p in range(B_SIZE):
        both = jnp.concatenate([edge_pairs[p], jnp.zeros((4, BX), jnp.float32)], axis=0)
        edges[1 + 2 * p] = jnp.where(row8 < 2, both, 0.0)
        edges[2 + 2 * p] = jnp.where(row8 < 2, pltpu.roll(both, 6, 0), 0.0)
    for o in a_order + [0]:
        tile = edges[back_of(o, 0)]
        for s in range(1, SLOTS):
            tile = tile + pltpu.roll(edges[back_of(o, s)], 2 * s, 0)
        edge_out[o] = tile
        if o > 0:
            copy(edge_out.at[o], edge_in.at[o], ra_send.at[CHUNKS], ra_recv.at[CHUNKS], a_peer(o, -1)).start()
    for q in range(CHUNKS):
        arrived(returned[q].at[pl.ds(3, 2 * (B_SIZE - 1))], rb_send.at[q], rb_recv.at[q])
        for o in a_order + [0]:
            for s in range(SLOTS):
                slot_out[q, o, s] = returned[q][back_of(o, s)]
            if o > 0:
                copy(slot_out.at[q, o], slot_in.at[q, o], ra_send.at[q], ra_recv.at[q], a_peer(o, -1)).start()
    result_copy = copy(result_out, result_in, place_send.at[1], place_recv.at[1], (lon, lat))
    result_copy.start()
    arrived(edge_in.at[pl.ds(1, A_SIZE - 1)], ra_send.at[CHUNKS], ra_recv.at[CHUNKS])
    edge = edge_out[0]
    for o in range(1, A_SIZE):
        edge = edge + edge_in[o]
    for s in range(SLOTS):
        slot_sum[s, BY : BY + 8, :] = edge if s == 0 else pltpu.roll(edge, 8 - 2 * s, 0)
    for q in range(CHUNKS):
        arrived(slot_in.at[q, pl.ds(1, A_SIZE - 1)], ra_send.at[q], ra_recv.at[q])
        for s in range(SLOTS):
            total = slot_out[q, 0, s]
            for o in range(1, A_SIZE):
                total = total + slot_in[q, o, s]
            slot_sum[s, q * CH : (q + 1) * CH, :] = total
    result_copy.wait()
    surface_ref[...] = result_in[0]
    sens_ref[...] = result_in[1]
    for s in range(SLOTS):
        here = slot_sum[s, 0:BY, :]
        flat = jnp.broadcast_to(slot_sum[s, BY + 1 : BY + 2, :], (BY, BX))
        column = jnp.sum(jnp.where(row32 == lane32, flat, 0.0), axis=1, keepdims=True)
        beside = jnp.where(lane32 == BX - 1, column, lane_roll(here, -1))
        press_ref[s, 0] = pressure_gain * (beside - here)
        press_ref[s, 1] = pressure_gain * (slot_sum[s, 1 : BY + 1, :] - here)


def main_call(block_ids, level_count, drag_coef, bathymetry, land_mask, adjoint_vel, velocity):
    f32, i32 = jnp.float32, jnp.int32
    wide = (3 * BY, 3 * BX)
    dma = pltpu.SemaphoreType.DMA
    vmem = pl.BlockSpec(memory_space=pltpu.VMEM)
    hbm = pl.BlockSpec(memory_space=pltpu.HBM)
    return pl.pallas_call(
        main_kernel,
        out_shape=(
            pltpu.VMEM((SLOTS, 2, LEV, BY, BX), f32),
            pltpu.VMEM((SLOTS, 2, BY, BX), f32),
            pltpu.VMEM((SLOTS, 2, BY, BX), f32),
            pltpu.VMEM((SLOTS, BY, BX), f32),
            pltpu.VMEM((BY, 2 * BX), f32),
            pltpu.VMEM((BY, 2 * BX), f32),
        ),
        in_specs=[hbm] * 7,
        out_specs=(vmem,) * 6,
        scratch_shapes=[
            pltpu.VMEM((SLOTS, BY, BX), i32),
            pltpu.VMEM((SLOTS, 2, LEV, BY, BX), jnp.bfloat16),
            pltpu.SMEM((SLOTS,), i32),
            pltpu.VMEM((SLOTS, BY, BX), i32),
            pltpu.VMEM((SLOTS, BY, BX), f32),
            pltpu.VMEM((BY, 2 * BX), f32),
            pltpu.VMEM((BY, 2 * BX), i32),
            pltpu.VMEM((A_SIZE, 8, BX), i32),
            pltpu.VMEM((2 * B_SIZE, BX), i32),
            pltpu.VMEM((A_SIZE, BX), i32),
            pltpu.SMEM((2 * B_SIZE, BX), i32),
            pltpu.SMEM((A_SIZE, BX), i32),
            [pltpu.VMEM((1 + SLOTS * A_SIZE, CH, BX), f32) for _ in range(CHUNKS)],
            pltpu.VMEM((CHUNKS, B_SIZE, 2, CH, BX), f32),
            pltpu.VMEM((CHUNKS, B_SIZE, 2, CH, BX), f32),
            pltpu.VMEM((2, BY, BX), f32),
            pltpu.VMEM((2, BY, BX), f32),
            pltpu.VMEM((2, BY, BX), f32),
            pltpu.VMEM((2, BY, 2 * BX), f32),
            pltpu.VMEM((2, BY, 2 * BX), f32),
            pltpu.VMEM((2, 8, BX), f32),
            pltpu.VMEM((2, 8, BX), f32),
            pltpu.VMEM((2, 2, BY, BX), f32),
            pltpu.VMEM((2, 2, BY, BX), f32),
            pltpu.VMEM((len(SIDES), 8, BX), f32),
            pltpu.VMEM((len(SIDES), 8, BX), f32),
            pltpu.VMEM(wide, f32),
            pltpu.VMEM(wide, f32),
            pltpu.VMEM(wide, f32),
            pltpu.VMEM(wide, f32),
            pltpu.VMEM(wide, f32),
            pltpu.VMEM((BY + 16, 3 * BX), f32),
            pltpu.VMEM(wide, f32),
            [pltpu.VMEM((1 + 2 * B_SIZE, CH, BX), f32) for _ in range(CHUNKS)],
            pltpu.VMEM((B_SIZE, 4, BX), f32),
            pltpu.VMEM((1 + 2 * B_SIZE, 8, BX), f32),
            pltpu.VMEM((CHUNKS, A_SIZE, SLOTS, CH, BX), f32),
            pltpu.VMEM((CHUNKS, A_SIZE, SLOTS, CH, BX), f32),
            pltpu.VMEM((A_SIZE, 8, BX), f32),
            pltpu.VMEM((A_SIZE, 8, BX), f32),
            pltpu.VMEM((SLOTS, BY + 8, BX), f32),
            dma((CHUNKS + 1,)),
            dma((1,)),
            dma((1,)),
            dma((CHUNKS,)),
            dma((CHUNKS,)),
            dma((CHUNKS,)),
            dma((CHUNKS,)),
            dma((2,)),
            dma((2,)),
            dma((2,)),
            dma((2,)),
            dma((CHUNKS + 1,)),
            dma((CHUNKS + 1,)),
            dma((CHUNKS + 1,)),
            dma((CHUNKS + 1,)),
            dma((2,)),
            dma((2,)),
            dma((2,)),
            dma((5,)),
        ],
        compiler_params=pltpu.CompilerParams(
            collective_id=0, has_side_effects=True, vmem_limit_bytes=50 * 2**20
        ),
        name="columns_and_surface",
    )(block_ids, level_count, drag_coef, bathymetry, land_mask, adjoint_vel, velocity)


def final_kernel(
    count_ref, mixed_ref, press_ref, pull_ref, drag_ref, surface_ref, sens_ref,
    out_hbm, drag_out_ref, surface_out_ref, sens_out_ref, stage, sems, small_sems,
):
    small = ((drag_ref, drag_out_ref), (surface_ref, surface_out_ref), (sens_ref, sens_out_ref))
    extra = [pltpu.make_async_copy(src, dst, small_sems.at[i]) for i, (src, dst) in enumerate(small)]
    for c in extra:
        c.start()
    for slot in range(SLOTS):
        levels = count_ref[slot]
        for c in range(2):
            press = press_ref[slot, c]
            bed = press + pull_ref[slot, c]
            for piece in range(PIECES):
                for k in range(piece * LEV // PIECES, (piece + 1) * LEV // PIECES):
                    less = jnp.where(levels == k + 1, bed, jnp.where(levels > k, press, 0.0))
                    stage[slot, c, k] = mixed_ref[slot, c, k] - less
                part = (slot, c, pl.ds(piece * LEV // PIECES, LEV // PIECES))
                pltpu.make_async_copy(stage.at[part], out_hbm.at[part], sems.at[0]).start()
    for c in extra:
        c.wait()
    pltpu.make_async_copy(stage, out_hbm, sems.at[0]).wait()


def final_call(level_count, mixed, press, pull, drag_grad, surface, sens):
    f32 = jnp.float32
    vmem = pl.BlockSpec(memory_space=pltpu.VMEM)
    deep = (SLOTS, 2, LEV, BY, BX)
    return pl.pallas_call(
        final_kernel,
        out_shape=(
            jax.ShapeDtypeStruct(deep, f32),
            jax.ShapeDtypeStruct(drag_grad.shape, f32),
            jax.ShapeDtypeStruct(surface.shape, f32),
            jax.ShapeDtypeStruct(sens.shape, f32),
        ),
        in_specs=[vmem] * 7,
        out_specs=(pl.BlockSpec(memory_space=pltpu.HBM),) * 4,
        scratch_shapes=[pltpu.VMEM(deep, f32), pltpu.SemaphoreType.DMA((1,)), pltpu.SemaphoreType.DMA((3,))],
        compiler_params=pltpu.CompilerParams(vmem_limit_bytes=24 * 2**20),
        name="pressure_correction",
    )(level_count, mixed, press, pull, drag_grad, surface, sens)


def per_device(adjoint_vel, velocity, drag_coef, level_count, block_ids, bathymetry, land_mask):
    mixed, press, pull, drag_grad, surface, sens = main_call(
        block_ids, level_count, drag_coef, bathymetry, land_mask, adjoint_vel, velocity
    )
    return final_call(level_count, mixed, press, pull, drag_grad, surface, sens)


def solution(mesh):
    slots = P(("gx", "gy"), None, None, None, None)
    flat = P(("gx", "gy"), None, None)
    return jax.shard_map(
        per_device,
        mesh=mesh,
        in_specs=(slots, slots, flat, flat, P(("gx", "gy")), P("gy", "gx"), P("gy", "gx")),
        out_specs=(slots, flat, P("gy", "gx"), P("gy", "gx")),
        check_vma=False,
    )
```

```python
import jax
import jax.numpy as jnp
from jax import lax
from jax.experimental import pallas as pl
from jax.experimental.pallas import tpu as pltpu
from jax.sharding import PartitionSpec as P

MESH = pl.DeviceIdType.MESH
STEPS = 32
LEV = 62
BY = 32
BX = 128
SLOTS = 4
CHUNKS = 4
CH = BY // CHUNKS
NX_CHIPS, NY_CHIPS, NZ_CHIPS, CORES = 4, 4, 4, 2
A_SIZE = NX_CHIPS * CORES
B_SIZE = NY_CHIPS * NZ_CHIPS
AROUND = ((-1, -1), (-1, 0), (-1, 1), (0, -1), (0, 1), (1, -1), (1, 0), (1, 1))
SIDES = tuple(d for d in AROUND if d[0] != 0)
UNIT = 16
UNITS = SLOTS * BY // UNIT
PIECES = 2

mix_rate = 0.25
drag_step = 0.5
force_scale = 0.25
pressure_gain = 0.5
surface_shift = 1.0 / 64.0
speed_floor = 0.01


def chebyshev_table(total_steps):
    highest = surface_shift + 8.0
    centre = 0.5 * (highest + surface_shift)
    radius = 0.5 * (highest - surface_shift)
    sigma_ratio = centre / radius
    ratio_prev = 1.0 / sigma_ratio
    table = []
    for _ in range(total_steps):
        ratio_next = 1.0 / (2.0 * sigma_ratio - ratio_prev)
        table.append((ratio_next * ratio_prev, 2.0 * ratio_next / radius))
        ratio_prev = ratio_next
    return (centre, table)


def lane_roll(values, shift):
    return pltpu.roll(values, shift % values.shape[-1], values.ndim - 1)


def mix_unit(unit, levels_ref, drag_ref, mixed_ref, velocity_ref, pull_ref, drag_out_ref):
    slot = lax.div(unit, BY // UNIT)
    rows = pl.ds(pl.multiple_of(lax.rem(unit, BY // UNIT) * UNIT, UNIT), UNIT)
    levels = levels_ref[slot, rows, :]
    zero = jnp.zeros((UNIT, BX), jnp.float32)

    def level(k, state, first_level=False):
        above0, flux0, above1, flux1, flow_b, column_b, rate = state
        last = k >= LEV - 1
        wet_next = levels > k + 1
        rate_next = jnp.where(wet_next, mix_rate, 0.0)
        bottom = levels == k
        out = [[], [], [], [], [], []]
        for c in range(2):
            if last:
                below = down = zero
                first = above0[c] - flux0[c]
            else:
                below = jnp.where(wet_next, mixed_ref[slot, c, k + 1, rows, :], 0.0)
                down = (below - above0[c]) * rate_next
                first = above0[c] + down - flux0[c]
            if first_level:
                down1, flow, col = zero, flow_b[c], column_b[c]
            else:
                down1 = zero if k == LEV else (first - above1[c]) * rate
                second = above1[c] + down1 - flux1[c]
                mixed_ref[slot, c, k - 1, rows, :] = second
                col = jnp.where(bottom, second, column_b[c])
                flow = jnp.where(bottom, velocity_ref[slot, c, k - 1, rows, :].astype(jnp.float32), flow_b[c])
            for pile, value in zip(out, (below, down, first, down1, flow, col)):
                pile.append(value)
        return (*(tuple(pile) for pile in out), rate_next)

    wet_top = levels > 0
    top = tuple(jnp.where(wet_top, mixed_ref[slot, c, 0, rows, :], 0.0) for c in range(2))
    both = (zero, zero)
    state = level(0, (top, both, both, both, both, both, zero), first_level=True)
    for k in range(1, LEV + 1):
        state = level(k, state)
    flow_b, column_b = state[4], state[5]
    speed = jnp.sqrt(flow_b[0] * flow_b[0] + flow_b[1] * flow_b[1] + speed_floor)
    along = flow_b[0] * column_b[0] + flow_b[1] * column_b[1]
    ratio = along / speed
    drag = drag_ref[slot, rows, :]
    drag_out_ref[slot, rows, :] = -drag_step * speed * along
    for c in range(2):
        pull_ref[slot, c, rows, :] = drag_step * (drag * (speed * column_b[c] + flow_b[c] * ratio))


def main_kernel(
    ids_hbm,
    count_hbm,
    drag_hbm,
    bathymetry_hbm,
    mask_hbm,
    adjoint_hbm,
    velocity_hbm,
    mixed_ref,
    press_ref,
    pull_ref,
    drag_out_ref,
    surface_ref,
    sens_ref,
    levels_ref,
    velocity_ref,
    ids_ref,
    count_ref,
    drag_ref,
    bathymetry_ref,
    mask_ref,
    idbuf,
    forward_vec,
    back_vec,
    forward_idx,
    back_idx,
    cand,
    spread,
    gathered,
    source_own,
    scaled_out,
    scaled_own,
    result_out,
    result_in,
    packed_scaled,
    packed_source,
    vert_scaled,
    vert_source,
    side_scaled,
    side_source,
    east_w,
    north_w,
    scaled_ext,
    direction,
    residual,
    height,
    diagonal,
    returned,
    edge_pairs,
    edges,
    slot_out,
    slot_in,
    edge_out,
    edge_in,
    slot_sum,
    load_sem,
    id_send,
    id_recv,
    a_send,
    a_recv,
    b_send,
    b_recv,
    h_send,
    h_recv,
    g_send,
    g_recv,
    rb_send,
    rb_recv,
    ra_send,
    ra_recv,
    place_send,
    place_recv,
    local_sem,
    small_sem,
):
    gx = lax.axis_index("gx")
    gy = lax.axis_index("gy")
    my_x, my_zh = lax.div(gx, 2), lax.rem(gx, 2)
    my_y, my_zl, my_c = lax.div(gy, 4), lax.rem(lax.div(gy, 2), 2), lax.rem(gy, 2)
    my_z = my_zh * 2 + my_zl

    def a_peer(o, sign):
        step_x, step_c = o // 2, o % 2
        if sign < 0:
            step_x = (NX_CHIPS - step_x) % NX_CHIPS
        x = lax.rem(my_x + step_x, NX_CHIPS)
        c = lax.rem(my_c + step_c, CORES)
        return (x * 2 + my_zh, my_y * 4 + my_zl * 2 + c)

    def b_peer(p, sign):
        step_y, step_z = p // NZ_CHIPS, p % NZ_CHIPS
        if sign < 0:
            step_y = (NY_CHIPS - step_y) % NY_CHIPS
            step_z = (NZ_CHIPS - step_z) % NZ_CHIPS
        y = lax.rem(my_y + step_y, NY_CHIPS)
        z = lax.rem(my_z + step_z, NZ_CHIPS)
        return (my_x * 2 + lax.div(z, 2), y * 4 + lax.rem(z, 2) * 2 + my_c)

    def snake(y_grid, z):
        return z + lax.rem(y_grid, 2) * (NZ_CHIPS - 1 - 2 * z)

    def solver_of(lon, lat):
        y_grid = lax.div(lat, NZ_CHIPS)
        z = snake(y_grid, lax.rem(lat, NZ_CHIPS))
        y = lax.rem(y_grid + NY_CHIPS - 1, NY_CHIPS)
        return (lax.div(lon, 2) * 2 + lax.div(z, 2), y * 4 + lax.rem(z, 2) * 2 + lax.rem(lon, 2))

    lon = my_x * 2 + my_c
    my_y_grid = lax.rem(my_y + 1, NY_CHIPS)
    lat = my_y_grid * NZ_CHIPS + snake(my_y_grid, my_z)

    def near(n):
        dx, dy = AROUND[n]
        return solver_of(lax.rem(lon + dx + 8, 8), lax.rem(lat + dy + 16, 16))

    def copy(src, dst, send, recv, to):
        return pltpu.make_async_remote_copy(
            src_ref=src, dst_ref=dst, send_sem=send, recv_sem=recv, device_id=to, device_id_type=MESH
        )

    def arrived(whole, send, recv):
        copy(whole, whole, send, recv, (gx, gy)).wait()

    a_order = sorted(range(1, A_SIZE), key=lambda o: -min(o // 2, NX_CHIPS - o // 2))
    b_order = sorted(
        range(1, B_SIZE),
        key=lambda p: -min(p // NZ_CHIPS, NY_CHIPS - p // NZ_CHIPS) - min(p % NZ_CHIPS, NZ_CHIPS - p % NZ_CHIPS),
    )

    loads = []
    for q in range(CHUNKS):
        part = (slice(None), slice(None), slice(None), pl.ds(q * CH, CH))
        loads.append(pltpu.make_async_copy(adjoint_hbm.at[part], mixed_ref.at[part], load_sem.at[q]))
    loads.append(pltpu.make_async_copy(velocity_hbm, velocity_ref, load_sem.at[CHUNKS]))
    pairs = (
        (ids_hbm, ids_ref),
        (count_hbm, count_ref),
        (bathymetry_hbm, bathymetry_ref),
        (mask_hbm, mask_ref),
        (drag_hbm, drag_ref),
    )
    small = [pltpu.make_async_copy(src, dst, small_sem.at[i]) for i, (src, dst) in enumerate(pairs)]
    small[0].start()
    small[1].start()
    loads[0].start()

    barrier = pltpu.get_barrier_semaphore()
    for p in b_order:
        pl.semaphore_signal(barrier, inc=1, device_id=b_peer(p, 1), device_id_type=MESH)
    for o in a_order:
        pl.semaphore_signal(barrier, inc=1, device_id=a_peer(o, 1), device_id_type=MESH)
    for n in range(8):
        pl.semaphore_signal(barrier, inc=1, device_id=near(n), device_id_type=MESH)
    pl.semaphore_signal(barrier, inc=1, device_id=solver_of(gx, gy), device_id_type=MESH)
    pl.semaphore_signal(barrier, inc=1, device_id=(lon, lat), device_id_type=MESH)

    for c in small[2:]:
        c.start()
    loads[1].start()

    lane8 = lax.broadcasted_iota(jnp.int32, (8, BX), 1)
    lane32 = lax.broadcasted_iota(jnp.int32, (BY, BX), 1)
    row8 = lax.broadcasted_iota(jnp.int32, (8, BX), 0)
    row32 = lax.broadcasted_iota(jnp.int32, (BY, BX), 0)

    small[0].wait()
    small[1].wait()
    lane1 = lax.broadcasted_iota(jnp.int32, (1, BX), 1)
    id_row = jnp.full((1, BX), -1, jnp.int32)
    for s in range(SLOTS):
        id_row = jnp.where(lane1 == s, ids_ref[s], id_row)
        levels_ref[s] = count_ref[s] * jnp.where(ids_ref[s] < 256, 1, 0)
    idbuf[0] = id_row
    for q in range(CHUNKS):
        cand[q][0] = jnp.zeros((CH, BX), jnp.float32)
        returned[q][0] = jnp.zeros((CH, BX), jnp.float32)
    edges[0] = jnp.zeros((8, BX), jnp.float32)

    def pack(block, base):
        out = jnp.zeros((8, BX), jnp.float32)
        for q in range(4):
            part = lane_roll(block[8 * q : 8 * q + 8, :], 32 * q - base)
            out = jnp.where(lane8 // 32 == q, part, out)
        return out

    def unpack(packed, base):
        return jnp.concatenate([lane_roll(packed, base - 32 * q) for q in range(4)], axis=0)

    small[2].wait()
    small[3].wait()
    scaled = bathymetry_ref[...] * mask_ref[...].astype(jnp.float32)
    scaled_out[0] = scaled[:, :BX]
    scaled_out[1] = scaled[:, BX:]

    def force(q):
        rows = slice(q * CH, (q + 1) * CH)

        def one(s, carry):
            levels = levels_ref[s, rows, :]
            totals = [jnp.zeros((CH, BX), jnp.float32)] * 4
            for k in range(LEV):
                pair = mixed_ref[s, 0, k, rows, :] + mixed_ref[s, 1, k, rows, :]
                totals[k % 4] = totals[k % 4] + jnp.where(levels > k, pair, 0.0)
            cand[q][1 + s] = force_scale * ((totals[0] + totals[1]) + (totals[2] + totals[3]))
            return carry

        lax.fori_loop(0, SLOTS, one, 0)

    loads[0].wait()
    loads[2].start()
    force(0)
    pl.semaphore_wait(barrier, A_SIZE - 1 + B_SIZE - 1 + 8 + 2)

    for o in a_order:
        copy(idbuf.at[0], idbuf.at[o], id_send.at[0], id_recv.at[0], a_peer(o, 1)).start()

    place_copy = copy(scaled_out, scaled_own, place_send.at[0], place_recv.at[0], solver_of(gx, gy))
    place_copy.start()
    def send_a(q):
        for o in a_order:
            copy(
                cand[q].at[pl.ds(1, SLOTS)],
                cand[q].at[pl.ds(1 + SLOTS * o, SLOTS)],
                a_send.at[q],
                a_recv.at[q],
                a_peer(o, 1),
            ).start()

    send_a(0)

    def send_halo(own, packed, vert, side, send, recv):
        for n, (dx, dy) in enumerate(AROUND):
            if dx != 0:
                copy(packed.at[0 if dx < 0 else 1], side.at[SIDES.index((dx, dy))], send.at[1], recv.at[1], near(n)).start()
        for n, (dx, dy) in enumerate(AROUND):
            if dx == 0:
                copy(own, vert.at[0 if dy < 0 else 1], send.at[0], recv.at[0], near(n)).start()

    def halo_arrived(vert, side, send, recv):
        arrived(vert, send.at[0], recv.at[0])
        arrived(side, send.at[1], recv.at[1])

    def extended(own, vert, side):
        bands = []
        for dy in (-1, 0, 1):
            if dy == 0:
                left, right = own[0], own[1]
                inside = jnp.float32(1.0)
            else:
                k = 0 if dy > 0 else 1
                left, right = vert[k, 0], vert[k, 1]
                inside = jnp.where(lat + dy >= 0, 1.0, 0.0) * jnp.where(lat + dy < 16, 1.0, 0.0)
            west = unpack(side[SIDES.index((1, -dy))], 32) * jnp.where(lon > 0, 1.0, 0.0)
            east = unpack(side[SIDES.index((-1, -dy))], 64) * jnp.where(lon < 7, 1.0, 0.0)
            left, right = lane_roll(left, 64), lane_roll(right, 64)
            first = jnp.where(lane32 < 32, 0.0, jnp.where(lane32 < 64, west, left))
            middle = jnp.where(lane32 < 64, left, right)
            last = jnp.where(lane32 < 64, right, jnp.where(lane32 < 96, east, 0.0))
            bands.append(jnp.concatenate([first, middle, last], axis=1) * inside)
        return jnp.concatenate(bands, axis=0)

    def units(first, last):
        def one(unit, carry):
            mix_unit(unit, levels_ref, drag_ref, mixed_ref, velocity_ref, pull_ref, drag_out_ref)
            return carry

        lax.fori_loop(first, last, one, 0)

    for q in range(1, CHUNKS):
        loads[q].wait()
        if q + 2 <= CHUNKS:
            loads[q + 2].start()
        force(q)
        send_a(q)

    arrived(idbuf.at[pl.ds(1, A_SIZE - 1)], id_send.at[0], id_recv.at[0])
    spot = lax.broadcasted_iota(jnp.int32, (2 * B_SIZE, BX), 0)
    spot_lane = lax.broadcasted_iota(jnp.int32, (2 * B_SIZE, BX), 1)
    spot_p = spot // 2
    spot_y = (my_y + spot_p // NZ_CHIPS + 1) % NY_CHIPS
    spot_z = (my_z + spot_p % NZ_CHIPS) % NZ_CHIPS
    owner = lon * 16 + spot_y * NZ_CHIPS + spot_z + (spot_y % 2) * (NZ_CHIPS - 1 - 2 * spot_z)
    target = owner * 2 + spot % 2
    forward = jnp.zeros((2 * B_SIZE, BX), jnp.int32)
    for o in range(A_SIZE):
        ids = jnp.broadcast_to(idbuf[o, 0:1, :], (2 * B_SIZE, BX))
        hit = ids == target
        forward = forward + jnp.where(hit, spot_lane + (1 + SLOTS * o), 0)
        back = jnp.sum(jnp.where(hit, spot + 1, 0), axis=0, keepdims=True)
        back_vec[o : o + 1, :] = back
    forward_vec[...] = jnp.broadcast_to(jnp.sum(forward, axis=1, keepdims=True), forward.shape)
    to_scalar = [
        pltpu.make_async_copy(forward_vec, forward_idx, local_sem.at[0]),
        pltpu.make_async_copy(back_vec, back_idx, local_sem.at[1]),
    ]
    for c in to_scalar:
        c.start()
    for c in to_scalar:
        c.wait()

    def picked(r):
        return jnp.clip(forward_idx[r, 0], 0, SLOTS * A_SIZE)

    def back_of(o, s):
        return jnp.clip(back_idx[o, s], 0, 2 * B_SIZE)

    place_copy.wait()
    packed_scaled[0] = pack(scaled_own[0], 0)
    packed_scaled[1] = pack(scaled_own[1], 96)
    send_halo(scaled_own, packed_scaled, vert_scaled, side_scaled, h_send, h_recv)

    for q in range(CHUNKS):
        arrived(cand[q].at[pl.ds(1 + SLOTS, SLOTS * (A_SIZE - 1))], a_send.at[q], a_recv.at[q])
        for p in b_order + [0]:
            for h in range(2):
                spread[q, p, h] = cand[q][picked(2 * p + h)]
            if p > 0:
                copy(spread.at[q, p], gathered.at[q, p], b_send.at[q], b_recv.at[q], b_peer(p, 1)).start()

    small[4].wait()
    loads[CHUNKS].wait()
    units(0, 6)
    halo_arrived(vert_scaled, side_scaled, h_send, h_recv)
    scaled_ext[...] = extended(scaled_own, vert_scaled, side_scaled)
    all_scaled = scaled_ext[...]
    tall = all_scaled.shape[0]
    east_w[...] = jnp.sqrt(all_scaled * lane_roll(all_scaled, -1))
    north_w[...] = jnp.sqrt(all_scaled * pltpu.roll(all_scaled, tall - 1, 0))
    east, north = east_w[...], north_w[...]
    diagonal[...] = surface_shift + ((east + lane_roll(east, 1)) + (north + pltpu.roll(north, 1, 0)))

    for q in range(CHUNKS):
        arrived(gathered.at[q, pl.ds(1, B_SIZE - 1)], b_send.at[q], b_recv.at[q])
        rows = slice(q * CH, (q + 1) * CH)
        for h in range(2):
            total = spread[q, 0, h]
            for p in range(1, B_SIZE):
                total = total + gathered[q, p, h]
            source_own[h, rows, :] = jnp.where(scaled_own[h, rows, :] > 0.0, total, 0.0)

    packed_source[0] = pack(source_own[0], 0)
    packed_source[1] = pack(source_own[1], 96)
    send_halo(source_own, packed_source, vert_source, side_source, g_send, g_recv)
    halo_arrived(vert_source, side_source, g_send, g_recv)
    start = extended(source_own, vert_source, side_source)
    centre, table = chebyshev_table(STEPS)
    residual[...] = start
    direction[...] = start / centre
    core = slice(BY - 8, 2 * BY + 8)
    height[...] = jnp.zeros(height.shape, jnp.float32)

    def group(step, count, phase):
        band = slice(8 * phase, tall - 8 * phase)
        rows = tall - 16 * phase
        inner = slice(BY - 8 - 8 * phase, BY - 8 - 8 * phase + BY + 16)
        now, left, total = direction[band, :], residual[band, :], height[...]
        for i in range(count):
            total = total + now[inner, :]
            east, north = east_w[band, :], north_w[band, :]
            image = diagonal[band, :] * now
            image = image - (east * lane_roll(now, -1) + lane_roll(east * now, 1))
            image = image - (north * pltpu.roll(now, rows - 1, 0) + pltpu.roll(north * now, 1, 0))
            left = left - image
            carry, push = table[step + i]
            now = carry * now + push * left
        direction[band, :], residual[band, :], height[...] = now, left, total

    for phase in range(3):
        group(8 * phase, 8, phase)
    group(24, 7, 3)
    height[...] = height[...] + direction[core, :]

    def own_blocks(values):
        a, b, c = (lane_roll(values[:, k * BX : (k + 1) * BX], 64) for k in range(3))
        low = lax.broadcasted_iota(jnp.int32, a.shape, 1) < 64
        return jnp.where(low, a, b), jnp.where(low, b, c)

    mid = height[8 : BY + 8, :]
    own_heights = own_blocks(mid)
    next_rows = own_blocks(height[BY + 8 : BY + 16, :])
    pair = jnp.zeros((8, BX), jnp.float32)
    for h in range(2):
        tile = mid[:, (h + 1) * BX : (h + 2) * BX]
        column = jnp.sum(jnp.where(lane32 == 64, tile, 0.0), axis=1, keepdims=True)
        flat = jnp.sum(jnp.where(row32 == lane32, column, 0.0), axis=0, keepdims=True)
        next_row = next_rows[h] if h == 0 else pltpu.roll(next_rows[h], 2 * h, 0)
        pair = jnp.where(row8 == 2 * h, next_row, jnp.where(row8 == 2 * h + 1, flat, pair))
        for q in range(CHUNKS):
            returned[q][1 + h] = own_heights[h][q * CH : (q + 1) * CH, :]
    edge_pairs[0] = pair[0:4, :]

    for p in b_order:
        copy(edge_pairs.at[0], edge_pairs.at[p], rb_send.at[CHUNKS], rb_recv.at[CHUNKS], b_peer(p, -1)).start()
    for q in range(CHUNKS):
        for p in b_order:
            copy(
                returned[q].at[pl.ds(1, 2)],
                returned[q].at[pl.ds(1 + 2 * p, 2)],
                rb_send.at[q],
                rb_recv.at[q],
                b_peer(p, -1),
            ).start()

    east_step = lane_roll(mid, -1) - mid
    north_step = height[9 : BY + 9, :] - mid
    south_step = mid - height[7 : BY + 7, :]
    east_energy = east_w[BY : 2 * BY, :] * east_step * east_step
    total = (
        east_energy
        + lane_roll(east_energy, 1)
        + north_w[BY : 2 * BY, :] * north_step * north_step
        + north_w[BY - 1 : 2 * BY - 1, :] * south_step * south_step
    )
    sens = 0.25 * total / jnp.maximum(scaled_ext[BY : 2 * BY, :], 0.25)
    for h, (sens_part, height_part) in enumerate(zip(own_blocks(sens), own_heights)):
        result_out[0, :, h * BX : (h + 1) * BX] = height_part
        result_out[1, :, h * BX : (h + 1) * BX] = sens_part

    units(6, 8)
    arrived(edge_pairs.at[pl.ds(1, B_SIZE - 1)], rb_send.at[CHUNKS], rb_recv.at[CHUNKS])
    for p in range(B_SIZE):
        both = jnp.concatenate([edge_pairs[p], jnp.zeros((4, BX), jnp.float32)], axis=0)
        edges[1 + 2 * p] = jnp.where(row8 < 2, both, 0.0)
        edges[2 + 2 * p] = jnp.where(row8 < 2, pltpu.roll(both, 6, 0), 0.0)
    for o in a_order + [0]:
        tile = edges[back_of(o, 0)]
        for s in range(1, SLOTS):
            tile = tile + pltpu.roll(edges[back_of(o, s)], 2 * s, 0)
        edge_out[o] = tile
        if o > 0:
            copy(edge_out.at[o], edge_in.at[o], ra_send.at[CHUNKS], ra_recv.at[CHUNKS], a_peer(o, -1)).start()
    for q in range(CHUNKS):
        arrived(returned[q].at[pl.ds(3, 2 * (B_SIZE - 1))], rb_send.at[q], rb_recv.at[q])
        for o in a_order + [0]:
            for s in range(SLOTS):
                slot_out[q, o, s] = returned[q][back_of(o, s)]
            if o > 0:
                copy(slot_out.at[q, o], slot_in.at[q, o], ra_send.at[q], ra_recv.at[q], a_peer(o, -1)).start()
    result_copy = copy(result_out, result_in, place_send.at[1], place_recv.at[1], (lon, lat))
    result_copy.start()
    arrived(edge_in.at[pl.ds(1, A_SIZE - 1)], ra_send.at[CHUNKS], ra_recv.at[CHUNKS])
    edge = edge_out[0]
    for o in range(1, A_SIZE):
        edge = edge + edge_in[o]
    for s in range(SLOTS):
        slot_sum[s, BY : BY + 8, :] = edge if s == 0 else pltpu.roll(edge, 8 - 2 * s, 0)
    for q in range(CHUNKS):
        arrived(slot_in.at[q, pl.ds(1, A_SIZE - 1)], ra_send.at[q], ra_recv.at[q])
        for s in range(SLOTS):
            total = slot_out[q, 0, s]
            for o in range(1, A_SIZE):
                total = total + slot_in[q, o, s]
            slot_sum[s, q * CH : (q + 1) * CH, :] = total
    result_copy.wait()
    surface_ref[...] = result_in[0]
    sens_ref[...] = result_in[1]
    for s in range(SLOTS):
        here = slot_sum[s, 0:BY, :]
        flat = jnp.broadcast_to(slot_sum[s, BY + 1 : BY + 2, :], (BY, BX))
        column = jnp.sum(jnp.where(row32 == lane32, flat, 0.0), axis=1, keepdims=True)
        beside = jnp.where(lane32 == BX - 1, column, lane_roll(here, -1))
        press_ref[s, 0] = pressure_gain * (beside - here)
        press_ref[s, 1] = pressure_gain * (slot_sum[s, 1 : BY + 1, :] - here)


def main_call(block_ids, level_count, drag_coef, bathymetry, land_mask, adjoint_vel, velocity):
    f32, i32 = jnp.float32, jnp.int32
    wide = (3 * BY, 3 * BX)
    dma = pltpu.SemaphoreType.DMA
    vmem = pl.BlockSpec(memory_space=pltpu.VMEM)
    hbm = pl.BlockSpec(memory_space=pltpu.HBM)
    return pl.pallas_call(
        main_kernel,
        out_shape=(
            pltpu.VMEM((SLOTS, 2, LEV, BY, BX), f32),
            pltpu.VMEM((SLOTS, 2, BY, BX), f32),
            pltpu.VMEM((SLOTS, 2, BY, BX), f32),
            pltpu.VMEM((SLOTS, BY, BX), f32),
            pltpu.VMEM((BY, 2 * BX), f32),
            pltpu.VMEM((BY, 2 * BX), f32),
        ),
        in_specs=[hbm] * 7,
        out_specs=(vmem,) * 6,
        scratch_shapes=[
            pltpu.VMEM((SLOTS, BY, BX), i32),
            pltpu.VMEM((SLOTS, 2, LEV, BY, BX), jnp.bfloat16),
            pltpu.SMEM((SLOTS,), i32),
            pltpu.VMEM((SLOTS, BY, BX), i32),
            pltpu.VMEM((SLOTS, BY, BX), f32),
            pltpu.VMEM((BY, 2 * BX), f32),
            pltpu.VMEM((BY, 2 * BX), i32),
            pltpu.VMEM((A_SIZE, 1, BX), i32),
            pltpu.VMEM((2 * B_SIZE, BX), i32),
            pltpu.VMEM((A_SIZE, BX), i32),
            pltpu.SMEM((2 * B_SIZE, BX), i32),
            pltpu.SMEM((A_SIZE, BX), i32),
            [pltpu.VMEM((1 + SLOTS * A_SIZE, CH, BX), f32) for _ in range(CHUNKS)],
            pltpu.VMEM((CHUNKS, B_SIZE, 2, CH, BX), f32),
            pltpu.VMEM((CHUNKS, B_SIZE, 2, CH, BX), f32),
            pltpu.VMEM((2, BY, BX), f32),
            pltpu.VMEM((2, BY, BX), f32),
            pltpu.VMEM((2, BY, BX), f32),
            pltpu.VMEM((2, BY, 2 * BX), f32),
            pltpu.VMEM((2, BY, 2 * BX), f32),
            pltpu.VMEM((2, 8, BX), f32),
            pltpu.VMEM((2, 8, BX), f32),
            pltpu.VMEM((2, 2, BY, BX), f32),
            pltpu.VMEM((2, 2, BY, BX), f32),
            pltpu.VMEM((len(SIDES), 8, BX), f32),
            pltpu.VMEM((len(SIDES), 8, BX), f32),
            pltpu.VMEM(wide, f32),
            pltpu.VMEM(wide, f32),
            pltpu.VMEM(wide, f32),
            pltpu.VMEM(wide, f32),
            pltpu.VMEM(wide, f32),
            pltpu.VMEM((BY + 16, 3 * BX), f32),
            pltpu.VMEM(wide, f32),
            [pltpu.VMEM((1 + 2 * B_SIZE, CH, BX), f32) for _ in range(CHUNKS)],
            pltpu.VMEM((B_SIZE, 4, BX), f32),
            pltpu.VMEM((1 + 2 * B_SIZE, 8, BX), f32),
            pltpu.VMEM((CHUNKS, A_SIZE, SLOTS, CH, BX), f32),
            pltpu.VMEM((CHUNKS, A_SIZE, SLOTS, CH, BX), f32),
            pltpu.VMEM((A_SIZE, 8, BX), f32),
            pltpu.VMEM((A_SIZE, 8, BX), f32),
            pltpu.VMEM((SLOTS, BY + 8, BX), f32),
            dma((CHUNKS + 1,)),
            dma((1,)),
            dma((1,)),
            dma((CHUNKS,)),
            dma((CHUNKS,)),
            dma((CHUNKS,)),
            dma((CHUNKS,)),
            dma((2,)),
            dma((2,)),
            dma((2,)),
            dma((2,)),
            dma((CHUNKS + 1,)),
            dma((CHUNKS + 1,)),
            dma((CHUNKS + 1,)),
            dma((CHUNKS + 1,)),
            dma((2,)),
            dma((2,)),
            dma((2,)),
            dma((5,)),
        ],
        compiler_params=pltpu.CompilerParams(
            collective_id=0, has_side_effects=True, vmem_limit_bytes=50 * 2**20
        ),
        name="columns_and_surface",
    )(block_ids, level_count, drag_coef, bathymetry, land_mask, adjoint_vel, velocity)


def final_kernel(
    count_ref, mixed_ref, press_ref, pull_ref, drag_ref, surface_ref, sens_ref,
    out_hbm, drag_out_ref, surface_out_ref, sens_out_ref, stage, sems, small_sems,
):
    small = ((drag_ref, drag_out_ref), (surface_ref, surface_out_ref), (sens_ref, sens_out_ref))
    extra = [pltpu.make_async_copy(src, dst, small_sems.at[i]) for i, (src, dst) in enumerate(small)]
    for c in extra:
        c.start()
    for slot in range(SLOTS):
        levels = count_ref[slot]
        for c in range(2):
            press = press_ref[slot, c]
            bed = press + pull_ref[slot, c]
            for piece in range(PIECES):
                for k in range(piece * LEV // PIECES, (piece + 1) * LEV // PIECES):
                    less = jnp.where(levels == k + 1, bed, jnp.where(levels > k, press, 0.0))
                    stage[slot, c, k] = mixed_ref[slot, c, k] - less
                part = (slot, c, pl.ds(piece * LEV // PIECES, LEV // PIECES))
                pltpu.make_async_copy(stage.at[part], out_hbm.at[part], sems.at[0]).start()
    for c in extra:
        c.wait()
    pltpu.make_async_copy(stage, out_hbm, sems.at[0]).wait()


def final_call(level_count, mixed, press, pull, drag_grad, surface, sens):
    f32 = jnp.float32
    vmem = pl.BlockSpec(memory_space=pltpu.VMEM)
    deep = (SLOTS, 2, LEV, BY, BX)
    return pl.pallas_call(
        final_kernel,
        out_shape=(
            jax.ShapeDtypeStruct(deep, f32),
            jax.ShapeDtypeStruct(drag_grad.shape, f32),
            jax.ShapeDtypeStruct(surface.shape, f32),
            jax.ShapeDtypeStruct(sens.shape, f32),
        ),
        in_specs=[vmem] * 7,
        out_specs=(pl.BlockSpec(memory_space=pltpu.HBM),) * 4,
        scratch_shapes=[pltpu.VMEM(deep, f32), pltpu.SemaphoreType.DMA((1,)), pltpu.SemaphoreType.DMA((3,))],
        compiler_params=pltpu.CompilerParams(vmem_limit_bytes=24 * 2**20),
        name="pressure_correction",
    )(level_count, mixed, press, pull, drag_grad, surface, sens)


def per_device(adjoint_vel, velocity, drag_coef, level_count, block_ids, bathymetry, land_mask):
    mixed, press, pull, drag_grad, surface, sens = main_call(
        block_ids, level_count, drag_coef, bathymetry, land_mask, adjoint_vel, velocity
    )
    return final_call(level_count, mixed, press, pull, drag_grad, surface, sens)


def solution(mesh):
    slots = P(("gx", "gy"), None, None, None, None)
    flat = P(("gx", "gy"), None, None)
    return jax.shard_map(
        per_device,
        mesh=mesh,
        in_specs=(slots, slots, flat, flat, P(("gx", "gy")), P("gy", "gx"), P("gy", "gx")),
        out_specs=(slots, flat, P("gy", "gx"), P("gy", "gx")),
        check_vma=False,
    )
```
